32 devices in a mesh: rep: 8 (over y, x, core), fsdp: 4 (over z).
Axes of the slice: x: 2, y: 2, z: 4, core: 2. Of those that a mesh axis runs over, the one named last changes fastest.
Arguments:
- tokens: bfloat16 [32768, 768], P(('rep', 'fsdp')), may hold values from -11 to 11
- segments: int32 [32768], P(('rep', 'fsdp')), may hold values from -1 to 1, as said below
- random_blocks: int32 [32, 16, 3], P(('rep', 'fsdp')), may hold values from 0 to 15, as said below
- out_grad: bfloat16 [32768, 768], P(('rep', 'fsdp')), may hold values from -6 to 6
- w_query: bfloat16 [768, 768], P('fsdp'), may hold values from -0.21875 to 0.21875
- w_key: bfloat16 [768, 768], P('fsdp'), may hold values from -0.21875 to 0.21875
- w_value: bfloat16 [768, 768], P('fsdp'), may hold values from -0.21875 to 0.21875
- w_out: bfloat16 [768, 768], P('fsdp'), may hold values from -0.875 to 0.875
- w_up: bfloat16 [768, 3072], P('fsdp'), may hold values from -0.21875 to 0.21875
- w_down: bfloat16 [3072, 768], P('fsdp'), may hold values from -0.109375 to 0.109375
- vectors: bfloat16 [8, 768], P(None, 'fsdp'), may hold values from -1.5 to 1.5
- up_bias: bfloat16 [3072], P('fsdp'), may hold values from -1 to 1
Outputs:
- layer_out: bfloat16 [32768, 768], P(('rep', 'fsdp'))
- tokens_grad: bfloat16 [32768, 768], P(('rep', 'fsdp'))
- w_query_grad: float32 [768, 768], P('fsdp')
- w_key_grad: float32 [768, 768], P('fsdp')
- w_value_grad: float32 [768, 768], P('fsdp')
- w_out_grad: float32 [768, 768], P('fsdp')
- w_up_grad: float32 [768, 3072], P('fsdp')
- w_down_grad: float32 [3072, 768], P('fsdp')
- vectors_grad: float32 [8, 768], P(None, 'fsdp')
- up_bias_grad: float32 [3072], P('fsdp')
- rms_values: float32 [3], replicated
The draws below stay inside these ranges and needn't reach their ends.
Inputs may be any that keep to these rules, and one draw needn't show every extreme that they name: `segments`: in each sequence the tokens that are not padding come first with segment numbers that never fall and take every value 0 to 1; the rest are -1, and every sequence has some. `random_blocks`: for query block b >= 2 of a sequence, three distinct block numbers, none of them 0, 1, b - 1, b or b + 1; the rows of blocks 0 and 1 are not read.
All inputs are finite; a program needn't handle non-finite values.
Results may differ from the reference program's by a relative error of at most 0.017.
Values may be sent and summed in bfloat16 or wider, within the bound.
A program may use at most 320 MiB of HBM per device.

```python
import math
import jax
import jax.numpy as jnp
from jax import lax

D = 768
H = 12
DH = 64
FF = 3072
BLK = 64
RAND = 3
SEQ_LEN = 1024
NB = 16
SEQS = 32
TOKENS = 32768


def draw_tokens(key, part):
    values = jnp.clip(jax.random.normal(key, (TOKENS, D), jnp.float32), -6.0, 6.0)
    ranks = jnp.arange(TOKENS, dtype=jnp.float32) / max(TOKENS - 1, 1)
    scales = jnp.exp(0.5 * math.log(3.0) * ranks)
    return (values * scales[:, None]).astype(jnp.bfloat16)


def draw_segments(key, part):
    last_seq = max(SEQS - 1, 1)

    def one_sequence(seq_key, seq_index):
        pad_key, cut_key = jax.random.split(seq_key)
        base_pad = SEQ_LEN * 5 * (SEQS - 1 - seq_index) // (8 * last_seq)
        padding = base_pad + jax.random.randint(pad_key, (), SEQ_LEN // 64, SEQ_LEN // 32 + 1)
        filled = SEQ_LEN - padding
        depth = jax.random.randint(cut_key, (), 1, 6)
        first_len = jnp.maximum(jnp.right_shift(filled, depth), 1)
        places = jnp.arange(SEQ_LEN, dtype=jnp.int32)
        numbers = (places >= first_len).astype(jnp.int32)
        return jnp.where(places < filled, numbers, -1).astype(jnp.int32)
    seq_keys = jax.random.split(key, SEQS)
    seq_ids = jnp.arange(SEQS, dtype=jnp.int32)
    return jax.vmap(one_sequence)(seq_keys, seq_ids).reshape(TOKENS).astype(jnp.int32)


def draw_random_blocks(key, part):

    def one_row(row_key, current):
        places = jnp.arange(NB, dtype=jnp.int32)
        ranking = jax.random.randint(row_key, (NB,), 0, 1 << 20) * NB + places
        banned = (places <= 1) | (places >= current - 1) & (places <= current + 1)
        ranking = jnp.where(banned, (1 << 30) + places, ranking)
        return jnp.argsort(ranking, stable=True)[:RAND].astype(jnp.int32)
    row_keys = jax.random.split(key, SEQS * NB)
    currents = jnp.tile(jnp.arange(NB, dtype=jnp.int32), SEQS)
    return jax.vmap(one_row)(row_keys, currents).reshape(SEQS, NB, RAND).astype(jnp.int32)


def draw_vectors(key, part):
    first_key, second_key = jax.random.split(key)
    row_ids = jnp.arange(8)[:, None]
    gain_rows = (row_ids == 3) | (row_ids == 6)
    shifts = 0.2 * jnp.clip(jax.random.normal(first_key, (8, D), jnp.float32), -5.0, 5.0)
    gains = jax.random.uniform(second_key, (8, D), jnp.float32, 0.6, 1.4)
    return jnp.where(gain_rows, gains, shifts).astype(jnp.bfloat16)


def steps_of(key, shape, cuts, smallest, largest):
    def one(axis_at, shards_of):
        heights = jax.random.uniform(jax.random.fold_in(jax.random.fold_in(key, 6), axis_at), (shards_of,), jnp.float32, smallest / len(cuts), largest / len(cuts))
        return jnp.repeat(jnp.exp(heights), shape[axis_at] // shards_of).reshape((-1,) + (1,) * (len(shape) - axis_at - 1))

    level = one(*cuts[0])
    for cut in cuts[1:]:
        level = level * one(*cut)
    return level


def bell_draw(rng, extent, width, limit, shards=(), kind=jnp.bfloat16):
    loudness = steps_of(rng, extent, shards, -0.22, 0.18) if shards else 1.0
    result = jax.random.normal(rng, extent, jnp.float32) * width * loudness
    return jnp.minimum(jnp.maximum(result, -limit), limit).astype(kind)


def setup_inputs(seed: int = 0) -> dict:
    key_of = jax.random.split(jax.random.key(seed), 13)
    return {
        "tokens": draw_tokens(jax.random.fold_in(key_of[12], 71), 0),
        "segments": draw_segments(jax.random.fold_in(key_of[12], 71), 0),
        "random_blocks": draw_random_blocks(jax.random.fold_in(key_of[12], 71), 0),
        "out_grad": bell_draw(key_of[3], (TOKENS, D), 1.0, 6.0, ((0, 32),)),
        "w_query": bell_draw(key_of[4], (D, D), D ** -0.5, 0.21875, ((0, 4),)),
        "w_key": bell_draw(key_of[5], (D, D), D ** -0.5, 0.21875, ((0, 4),)),
        "w_value": bell_draw(key_of[6], (D, D), D ** -0.5, 0.21875, ((0, 4),)),
        "w_out": bell_draw(key_of[7], (D, D), (D // 16) ** -0.5, 0.875, ((0, 4),)),
        "w_up": bell_draw(key_of[8], (D, FF), D ** -0.5, 0.21875, ((0, 4),)),
        "w_down": bell_draw(key_of[9], (FF, D), FF ** -0.5, 0.109375, ((0, 4),)),
        "vectors": draw_vectors(jax.random.fold_in(key_of[12], 71), 0),
        "up_bias": bell_draw(key_of[11], (FF,), 0.2, 1.0, ((0, 4),)),
    }


@jax.custom_vjp
def low(v):
    return lax.optimization_barrier(v.astype(jnp.bfloat16)).astype(jnp.float32)

@jax.custom_vjp
def low_back(v):
    return v

def low_keep(v):
    return (low(v), None)

def low_pass(kept, grad):
    return (grad,)

def back_keep(v):
    return (v, None)

def back_low(kept, grad):
    return (low(grad),)
low.defvjp(low_keep, low_pass)
low_back.defvjp(back_keep, back_low)
highest = lax.Precision.HIGHEST
masked_score = -1e+30
layer_eps = 1e-05

def normalize(values, gain, shift):
    centered = values - lax.optimization_barrier(jnp.mean(values, axis=-1, keepdims=True))
    variance = lax.optimization_barrier(jnp.mean(centered * centered, axis=-1, keepdims=True))
    return centered * lax.rsqrt(variance + layer_eps) * gain + shift

def slot_tables(random_row):
    later = jnp.arange(2, NB, dtype=jnp.int32)
    zeros_col = jnp.zeros_like(later)
    slot_table = jnp.stack([zeros_col, zeros_col + 1, later - 1, later, jnp.minimum(later + 1, NB - 1), random_row[2:, 0], random_row[2:, 1], random_row[2:, 2]], axis=1)
    always = later >= 0
    slot_ok = jnp.stack([always, always, later >= 3, always, later <= NB - 2, always, always, always], axis=1)
    return (slot_table, slot_ok)

def visibility(seg_row, slot_table, slot_ok):
    seg_blocks = seg_row.reshape(NB, BLK)
    seg_picked = jnp.take(seg_blocks, slot_table, axis=0)
    local_seen = slot_ok[:, None, :, None] & (seg_blocks[2:][:, :, None, None] == seg_picked[:, None, :, :])
    local_seen = local_seen.reshape(NB - 2, 1, BLK, 8 * BLK)
    global_seen = (seg_row[:2 * BLK][:, None] == seg_row[None, :])[None]
    return (local_seen, global_seen)

def attend(queries, key_rows, value_rows, seg_row, random_row):
    slot_table, slot_ok = slot_tables(random_row)
    local_seen, global_seen = visibility(seg_row, slot_table, slot_ok)
    q_heads = queries.reshape(NB, BLK, H, DH)
    k_heads = key_rows.reshape(NB, BLK, H, DH)
    v_heads = value_rows.reshape(NB, BLK, H, DH)
    k_picked = jnp.take(k_heads, slot_table, axis=0)
    v_picked = jnp.take(v_heads, slot_table, axis=0)
    scores = jnp.einsum('nqhd,nsjhd->nhqsj', q_heads[2:], k_picked, precision=highest) * 0.125
    scores = low_back(scores).reshape(NB - 2, H, BLK, 8 * BLK)
    probs = low(jax.nn.softmax(jnp.where(local_seen, scores, masked_score), axis=-1))
    local_out = jnp.einsum('nhqsj,nsjhd->nqhd', probs.reshape(NB - 2, H, BLK, 8, BLK), v_picked, precision=highest)
    q_glob = queries[:2 * BLK].reshape(2 * BLK, H, DH)
    k_all = key_rows.reshape(SEQ_LEN, H, DH)
    v_all = value_rows.reshape(SEQ_LEN, H, DH)
    g_scores = low_back(jnp.einsum('qhd,khd->hqk', q_glob, k_all, precision=highest) * 0.125)
    g_probs = low(jax.nn.softmax(jnp.where(global_seen, g_scores, masked_score), axis=-1))
    global_out = jnp.einsum('hqk,khd->qhd', g_probs, v_all, precision=highest)
    return jnp.concatenate([global_out.reshape(2 * BLK, D), local_out.reshape((NB - 2) * BLK, D)], axis=0)

def attend_group(group):
    return attend(group[0], group[1], group[2], group[3], group[4])

def forward(inputs, w_query, w_key, w_value, w_out, w_up, w_down, vectors, up_bias, segments, random_blocks):
    queries = low(low_back(jnp.dot(inputs, w_query, precision=highest) + vectors[0]))
    key_rows = low(low_back(jnp.dot(inputs, w_key, precision=highest)))
    value_rows = low(low_back(jnp.dot(inputs, w_value, precision=highest) + vectors[1]))
    attended = lax.map(jax.checkpoint(attend_group), (queries.reshape(-1, SEQ_LEN, D), key_rows.reshape(-1, SEQ_LEN, D), value_rows.reshape(-1, SEQ_LEN, D), segments.reshape(-1, SEQ_LEN), random_blocks))
    mixed = low(low_back(attended.reshape(-1, D)))
    attn_out = low_back(jnp.dot(mixed, w_out, precision=highest) + vectors[2])
    first_sum = inputs + attn_out
    normed_one = normalize(first_sum, vectors[3], vectors[4])
    up_proj = low_back(jnp.dot(low(normed_one), w_up, precision=highest) + up_bias)
    activated = low(jax.nn.gelu(up_proj, approximate=False))
    mlp_out = low_back(jnp.dot(activated, w_down, precision=highest) + vectors[5])
    second_sum = normed_one + mlp_out
    layer_out = normalize(second_sum, vectors[6], vectors[7])
    return (layer_out, (first_sum, attn_out, mlp_out))

def reference(tokens, segments, random_blocks, out_grad, w_query, w_key, w_value, w_out, w_up, w_down, vectors, up_bias):

    def wrapped(inputs, query_f, key_f, value_f, out_f, up_f, down_f, vectors_f, upbias_f):
        return forward(inputs, query_f, key_f, value_f, out_f, up_f, down_f, vectors_f, upbias_f, segments, random_blocks)
    layer_out, pullback, extras = jax.vjp(wrapped, tokens.astype(jnp.float32), w_query.astype(jnp.float32), w_key.astype(jnp.float32), w_value.astype(jnp.float32), w_out.astype(jnp.float32), w_up.astype(jnp.float32), w_down.astype(jnp.float32), vectors.astype(jnp.float32), up_bias.astype(jnp.float32), has_aux=True)
    gradients = pullback(out_grad.astype(jnp.float32))
    valid = (segments >= 0).astype(jnp.float32)[:, None]
    counted = jnp.sum(valid)
    squares = jnp.stack([jnp.sum(valid * extras[0] * extras[0]), jnp.sum(valid * extras[1] * extras[1]), jnp.sum(valid * extras[2] * extras[2])])
    rms_values = jnp.sqrt(squares / (counted * D))
    return (layer_out.astype(jnp.bfloat16), gradients[0].astype(jnp.bfloat16), gradients[1], gradients[2], gradients[3], gradients[4], gradients[5], gradients[6], gradients[7], gradients[8], rms_values)
```

```python
import jax
import jax.numpy as jnp
from jax import lax
from jax.experimental import pallas as pl
from jax.experimental.pallas import tpu as pltpu
from jax.sharding import PartitionSpec as P

D = 768
H = 12
DH = 64
BLK = 64
SEQ_LEN = 1024
NB = 16


masked_score = -1e30
layer_eps = 1e-05


def normalize(values, gain, shift):
    centered = values - jnp.mean(values, axis=-1, keepdims=True)
    variance = jnp.mean(centered * centered, axis=-1, keepdims=True)
    return centered * lax.rsqrt(variance + layer_eps) * gain + shift


def gelu_exact(values):
    return jax.nn.gelu(values, approximate=False)


def dot_tn(left, right):
    return lax.dot_general(
        left, right, (((0,), (0,)), ((), ())), preferred_element_type=jnp.float32
    )


def dot_nt(left, right):
    return lax.dot_general(
        left, right, (((1,), (1,)), ((), ())), preferred_element_type=jnp.float32
    )


def col_sums(values):
    return jnp.sum(values.astype(jnp.float32), axis=0)


LOG2E=1.4426950408889634
BIG=1e30

def dot_nn(a,b): return lax.dot_general(a,b,(((1,),(0,)),((),())),preferred_element_type=jnp.float32)

def mask_features(seg_row, random_row):
    blocks = jnp.arange(NB, dtype=jnp.int32)
    near = jnp.abs(blocks[:, None] - blocks[None, :]) <= 1
    first = (blocks[:, None] < 2) | (blocks[None, :] < 2)
    picked = jnp.any(random_row[:, :, None] == blocks[None, None, :], axis=1)
    seen = first | near | picked
    q_block = jnp.where(seen, 0.0, -BIG)
    q_block = jnp.repeat(q_block, BLK, axis=0)
    k_block = jnp.repeat(jnp.eye(NB, dtype=jnp.float32), BLK, axis=0)
    numbers = jnp.arange(-1, 2, dtype=jnp.int32)
    same = seg_row[:, None] == numbers[None, :]
    q_seg = jnp.where(same, 0.0, -BIG)
    k_seg = same.astype(jnp.float32)
    rest = SEQ_LEN, 128 - NB - 3
    ones = jnp.ones((SEQ_LEN, 3), jnp.float32)
    q_feat = jnp.concatenate([q_block, q_seg, jnp.zeros(rest, jnp.float32)], axis=1)
    k_feat = jnp.concatenate([k_block, k_seg, ones, jnp.zeros((SEQ_LEN, 128 - NB - 6), jnp.float32)], axis=1)
    return q_feat.astype(jnp.bfloat16), k_feat.astype(jnp.bfloat16)

TQ=256
def fwd_kernel(q_ref,k_ref,v_ref,qf_ref,kf_ref,o_ref,aux_ref,qc,kc,vm):
    lane = lax.broadcasted_iota(jnp.int32,(SEQ_LEN,128),1)
    kc[:,:128]=k_ref[...]
    kc[:,128:]=kf_ref[...]
    q=q_ref[...]*jnp.bfloat16(0.125)
    v=v_ref[...]
    zero=jnp.zeros_like(q)
    for h in range(2):
        sel = (lane<64) if h==0 else (lane>=64)
        qc[h,:,:128]=jnp.where(sel,q,zero)
        qc[h,:,128:]=qf_ref[...]
        vm[h]=jnp.where(sel,v,zero)
    for t in range(SEQ_LEN//TQ):
        rows=pl.ds(t*TQ,TQ)
        total=None
        for h in range(2):
            s=dot_nt(qc[h,rows,:],kc[...])
            m=jnp.max(s,axis=1,keepdims=True)
            p=jnp.exp2((s-m)*LOG2E)
            l=jnp.sum(p,axis=1,keepdims=True)
            o=dot_nn(p.astype(jnp.bfloat16),vm[h])*(1.0/l)
            total=o if total is None else total+o
            lse=-(m+jnp.log(l))
            hi=lse.astype(jnp.bfloat16).astype(jnp.float32)
            r=lse-hi
            mid=r.astype(jnp.bfloat16).astype(jnp.float32)
            lo=r-mid
            ln=lax.broadcasted_iota(jnp.int32,(TQ,128),1)
            a=jnp.where(ln==19,hi,jnp.where(ln==20,mid,jnp.where(ln==21,lo,qf_ref[rows,:].astype(jnp.float32))))
            aux_ref[h,rows,:]=a.astype(jnp.bfloat16)
        o_ref[rows,:]=total.astype(jnp.bfloat16)

def attention_forward(q,k,v,qf,kf):
    pair=pl.BlockSpec((SEQ_LEN,128),lambda i:(0,i))
    whole=pl.BlockSpec((SEQ_LEN,128),lambda i:(0,0))
    return pl.pallas_call(fwd_kernel,grid=(H//2,),
        in_specs=[pair,pair,pair,whole,whole],
        out_specs=[pair,pl.BlockSpec((2,SEQ_LEN,128),lambda i:(i,0,0))],
        out_shape=[jax.ShapeDtypeStruct((SEQ_LEN,D),jnp.bfloat16),jax.ShapeDtypeStruct((H,SEQ_LEN,128),jnp.bfloat16)],
        scratch_shapes=[pltpu.VMEM((2,SEQ_LEN,256),jnp.bfloat16),pltpu.VMEM((SEQ_LEN,256),jnp.bfloat16),pltpu.VMEM((2,SEQ_LEN,128),jnp.bfloat16)],
        compiler_params=pltpu.CompilerParams(vmem_limit_bytes=48<<20),
        name="attention_forward")(q,k,v,qf,kf)

TK=256
def bwd_kernel(q_ref,k_ref,v_ref,do_ref,o_ref,aux_ref,kf_ref,dq_ref,dk_ref,dv_ref,qc,dc,kc,vc,km,dqa):
    lane = lax.broadcasted_iota(jnp.int32,(SEQ_LEN,128),1)
    kc[:,:128]=k_ref[...]
    kc[:,128:]=kf_ref[...]
    vc[:,:128]=v_ref[...]
    vc[:,128:]=kf_ref[...]
    q=q_ref[...]*jnp.bfloat16(0.125)
    k=k_ref[...]*jnp.bfloat16(0.125)
    do=do_ref[...]
    prod=do.astype(jnp.float32)*o_ref[...].astype(jnp.float32)
    zero=jnp.zeros_like(q)
    for h in range(2):
        sel = (lane<64) if h==0 else (lane>=64)
        qc[h,:,:128]=jnp.where(sel,q,zero)
        qc[h,:,128:]=aux_ref[h]
        km[h]=jnp.where(sel,k,zero)
        dc[h,:,:128]=jnp.where(sel,do,zero)
        delta=-jnp.sum(jnp.where(sel,prod,0.0),axis=1,keepdims=True)
        hi=delta.astype(jnp.bfloat16).astype(jnp.float32)
        lo=delta-hi
        dc[h,:,128:]=jnp.where(lane==19,hi,jnp.where(lane==20,lo,0.0)).astype(jnp.bfloat16)
    for t in range(SEQ_LEN//TK):
        rows=pl.ds(t*TK,TK)
        dv=None;dk=None;dq=None
        for h in range(2):
            s=dot_nt(kc[rows,:],qc[h])
            p=jnp.exp2(s*LOG2E)
            dp=dot_nt(vc[rows,:],dc[h])
            ds=(p*dp).astype(jnp.bfloat16)
            pb=p.astype(jnp.bfloat16)
            dvh=dot_nn(pb,dc[h,:,:128])
            dkh=dot_nn(ds,qc[h,:,:128])
            dqh=dot_tn(ds,km[h,rows,:])
            dv=dvh if dv is None else dv+dvh
            dk=dkh if dk is None else dk+dkh
            dq=dqh if dq is None else dq+dqh
        dk_ref[rows,:]=dk.astype(jnp.bfloat16)
        dv_ref[rows,:]=dv.astype(jnp.bfloat16)
        if t==0: dqa[...]=dq
        else: dqa[...]+=dq
    dq_ref[...]=dqa[...].astype(jnp.bfloat16)

def attention_backward(q,k,v,do,o,aux,kf):
    pair=pl.BlockSpec((SEQ_LEN,128),lambda i:(0,i))
    whole=pl.BlockSpec((SEQ_LEN,128),lambda i:(0,0))
    sd=jax.ShapeDtypeStruct((SEQ_LEN,D),jnp.bfloat16)
    B=jnp.bfloat16
    return pl.pallas_call(bwd_kernel,grid=(H//2,),
        in_specs=[pair]*5+[pl.BlockSpec((2,SEQ_LEN,128),lambda i:(i,0,0)),whole],
        out_specs=[pair]*3,out_shape=[sd]*3,
        scratch_shapes=[pltpu.VMEM((2,SEQ_LEN,256),B),pltpu.VMEM((2,SEQ_LEN,256),B),pltpu.VMEM((SEQ_LEN,256),B),pltpu.VMEM((SEQ_LEN,256),B),pltpu.VMEM((2,SEQ_LEN,128),B),pltpu.VMEM((SEQ_LEN,128),jnp.float32)],
        compiler_params=pltpu.CompilerParams(vmem_limit_bytes=48<<20),
        name="attention_backward")(q,k,v,do,o,aux,kf)


def per_device(
    tokens,
    segments,
    random_blocks,
    out_grad,
    w_query,
    w_key,
    w_value,
    w_out,
    w_up,
    w_down,
    vectors,
    up_bias,
):
    gathered = (
        lax.all_gather(w_query, "fsdp", axis=0, tiled=True),
        lax.all_gather(w_key, "fsdp", axis=0, tiled=True),
        lax.all_gather(w_value, "fsdp", axis=0, tiled=True),
        lax.all_gather(w_out, "fsdp", axis=0, tiled=True),
        lax.all_gather(w_up, "fsdp", axis=0, tiled=True),
        lax.all_gather(w_down, "fsdp", axis=0, tiled=True),
        lax.all_gather(vectors, "fsdp", axis=1, tiled=True),
        lax.all_gather(up_bias, "fsdp", axis=0, tiled=True),
    )
    full_query, full_key, full_value, full_out, full_up, full_down, full_vectors, full_upbias = (
        gathered
    )
    vec_float = full_vectors.astype(jnp.float32)
    inputs = tokens.astype(jnp.float32)
    q_low = (jnp.dot(tokens, full_query, preferred_element_type=jnp.float32) + vec_float[0]).astype(
        jnp.bfloat16
    )
    k_low = jnp.dot(tokens, full_key, preferred_element_type=jnp.float32).astype(jnp.bfloat16)
    v_low = (jnp.dot(tokens, full_value, preferred_element_type=jnp.float32) + vec_float[1]).astype(
        jnp.bfloat16
    )
    q_feat, k_feat = mask_features(segments, random_blocks[0])
    mixed_low, aux = attention_forward(q_low, k_low, v_low, q_feat, k_feat)
    attn_out = jnp.dot(mixed_low, full_out, preferred_element_type=jnp.float32) + vec_float[2]
    first_sum = inputs + attn_out
    normed_one, pull_one = jax.vjp(normalize, first_sum, vec_float[3], vec_float[4])
    normed_low = normed_one.astype(jnp.bfloat16)
    up_proj = jnp.dot(normed_low, full_up, preferred_element_type=jnp.float32) + full_upbias.astype(
        jnp.float32
    )
    activated, pull_gelu = jax.vjp(gelu_exact, up_proj)
    activated_low = activated.astype(jnp.bfloat16)
    mlp_out = jnp.dot(activated_low, full_down, preferred_element_type=jnp.float32) + vec_float[5]
    second_sum = normed_one + mlp_out
    layer_out, pull_two = jax.vjp(normalize, second_sum, vec_float[6], vec_float[7])
    valid = (segments >= 0).astype(jnp.float32)[:, None]
    squares = jnp.stack(
        [
            jnp.sum(valid * first_sum * first_sum),
            jnp.sum(valid * attn_out * attn_out),
            jnp.sum(valid * mlp_out * mlp_out),
        ]
    )
    squares, counted = lax.psum((squares, jnp.sum(valid)), ("rep", "fsdp"))
    rms_values = jnp.sqrt(squares / (counted * D))
    regathered = (
        lax.all_gather(w_query, "fsdp", axis=0, tiled=True),
        lax.all_gather(w_key, "fsdp", axis=0, tiled=True),
        lax.all_gather(w_value, "fsdp", axis=0, tiled=True),
        lax.all_gather(w_out, "fsdp", axis=0, tiled=True),
        lax.all_gather(w_up, "fsdp", axis=0, tiled=True),
        lax.all_gather(w_down, "fsdp", axis=0, tiled=True),
    )
    back_query, back_key, back_value, back_out, back_up, back_down = regathered
    d_second, d_gain_two, d_shift_two = pull_two(out_grad.astype(jnp.float32))
    d_mlp = d_second.astype(jnp.bfloat16)
    d_up = pull_gelu(dot_nt(d_mlp, back_down))[0].astype(jnp.bfloat16)
    d_normed = d_second + dot_nt(d_up, back_up)
    d_first, d_gain_one, d_shift_one = pull_one(d_normed)
    d_attn = d_first.astype(jnp.bfloat16)
    d_mixed = dot_nt(d_attn, back_out).astype(jnp.bfloat16)
    dq_low, dk_low, dv_low = attention_backward(
        q_low, k_low, v_low, d_mixed, mixed_low, aux, k_feat
    )
    tokens_grad = (
        d_first + dot_nt(dq_low, back_query) + dot_nt(dk_low, back_key) + dot_nt(dv_low, back_value)
    )
    grad_query = dot_tn(tokens, dq_low)
    grad_key = dot_tn(tokens, dk_low)
    grad_value = dot_tn(tokens, dv_low)
    grad_out = dot_tn(mixed_low, d_attn)
    grad_up = dot_tn(normed_low, d_up)
    grad_down = dot_tn(activated_low, d_mlp)
    grad_vectors = jnp.stack(
        [
            col_sums(dq_low),
            col_sums(dv_low),
            col_sums(d_attn),
            d_gain_one,
            d_shift_one,
            col_sums(d_mlp),
            d_gain_two,
            d_shift_two,
        ]
    )
    grad_upbias = col_sums(d_up)
    shard_sums = (
        lax.psum_scatter(
            grad_query.astype(jnp.bfloat16), "fsdp", scatter_dimension=0, tiled=True
        ).astype(jnp.float32),
        lax.psum_scatter(
            grad_key.astype(jnp.bfloat16), "fsdp", scatter_dimension=0, tiled=True
        ).astype(jnp.float32),
        lax.psum_scatter(
            grad_value.astype(jnp.bfloat16), "fsdp", scatter_dimension=0, tiled=True
        ).astype(jnp.float32),
        lax.psum_scatter(
            grad_out.astype(jnp.bfloat16), "fsdp", scatter_dimension=0, tiled=True
        ).astype(jnp.float32),
        lax.psum_scatter(
            grad_up.astype(jnp.bfloat16), "fsdp", scatter_dimension=0, tiled=True
        ).astype(jnp.float32),
        lax.psum_scatter(
            grad_down.astype(jnp.bfloat16), "fsdp", scatter_dimension=0, tiled=True
        ).astype(jnp.float32),
        lax.psum_scatter(
            grad_vectors.astype(jnp.bfloat16), "fsdp", scatter_dimension=1, tiled=True
        ).astype(jnp.float32),
        lax.psum_scatter(
            grad_upbias.astype(jnp.bfloat16), "fsdp", scatter_dimension=0, tiled=True
        ).astype(jnp.float32),
    )
    results = lax.psum(
        (
            shard_sums[0],
            shard_sums[1],
            shard_sums[2],
            shard_sums[3],
            shard_sums[4],
            shard_sums[5],
            shard_sums[6],
            shard_sums[7],
        ),
        "rep",
    )
    return (
        layer_out.astype(jnp.bfloat16),
        tokens_grad.astype(jnp.bfloat16),
        results[0],
        results[1],
        results[2],
        results[3],
        results[4],
        results[5],
        results[6],
        results[7],
        rms_values,
    )


def solution(mesh):
    in_specs = (
        P(("rep", "fsdp"), None),
        P(("rep", "fsdp")),
        P(("rep", "fsdp"), None, None),
        P(("rep", "fsdp"), None),
        P("fsdp", None),
        P("fsdp", None),
        P("fsdp", None),
        P("fsdp", None),
        P("fsdp", None),
        P("fsdp", None),
        P(None, "fsdp"),
        P("fsdp"),
    )
    out_specs = (
        P(("rep", "fsdp"), None),
        P(("rep", "fsdp"), None),
        P("fsdp", None),
        P("fsdp", None),
        P("fsdp", None),
        P("fsdp", None),
        P("fsdp", None),
        P("fsdp", None),
        P(None, "fsdp"),
        P("fsdp"),
        P(),
    )
    return jax.shard_map(
        per_device, mesh=mesh, in_specs=in_specs, out_specs=out_specs, check_vma=False
    )
```

```python
import jax
import jax.numpy as jnp
from jax import lax
from jax.experimental import pallas as pl
from jax.experimental.pallas import tpu as pltpu
from jax.sharding import PartitionSpec as P

D = 768
H = 12
DH = 64
BLK = 64
SEQ_LEN = 1024
NB = 16


masked_score = -1e30
layer_eps = 1e-05


def normalize(values, gain, shift):
    centered = values - jnp.mean(values, axis=-1, keepdims=True)
    variance = jnp.mean(centered * centered, axis=-1, keepdims=True)
    return centered * lax.rsqrt(variance + layer_eps) * gain + shift


def gelu_exact(values):
    return jax.nn.gelu(values, approximate=False)


def dot_tn(left, right):
    return lax.dot_general(
        left, right, (((0,), (0,)), ((), ())), preferred_element_type=jnp.float32
    )


def dot_nt(left, right):
    return lax.dot_general(
        left, right, (((1,), (1,)), ((), ())), preferred_element_type=jnp.float32
    )


def col_sums(values):
    return jnp.sum(values.astype(jnp.float32), axis=0)


LOG2E=1.4426950408889634
BIG=1e30

def dot_nn(a,b): return lax.dot_general(a,b,(((1,),(0,)),((),())),preferred_element_type=jnp.float32)

def mask_features(seg_row, random_row):
    blocks = jnp.arange(NB, dtype=jnp.int32)
    near = jnp.abs(blocks[:, None] - blocks[None, :]) <= 1
    first = (blocks[:, None] < 2) | (blocks[None, :] < 2)
    picked = jnp.any(random_row[:, :, None] == blocks[None, None, :], axis=1)
    seen = first | near | picked
    q_block = jnp.where(seen, 0.0, -BIG)
    q_block = jnp.repeat(q_block, BLK, axis=0)
    k_block = jnp.repeat(jnp.eye(NB, dtype=jnp.float32), BLK, axis=0)
    numbers = jnp.arange(-1, 2, dtype=jnp.int32)
    same = seg_row[:, None] == numbers[None, :]
    q_seg = jnp.where(same, 0.0, -BIG)
    k_seg = same.astype(jnp.float32)
    rest = SEQ_LEN, 128 - NB - 3
    ones = jnp.ones((SEQ_LEN, 3), jnp.float32)
    q_feat = jnp.concatenate([q_block, q_seg, jnp.zeros(rest, jnp.float32)], axis=1)
    k_feat = jnp.concatenate([k_block, k_seg, ones, jnp.zeros((SEQ_LEN, 128 - NB - 6), jnp.float32)], axis=1)
    return q_feat.astype(jnp.bfloat16), k_feat.astype(jnp.bfloat16)

TQ=256
def fwd_kernel(q_ref,k_ref,v_ref,qf_ref,kf_ref,o_ref,aux_ref,qc,kc,vm):
    lane = lax.broadcasted_iota(jnp.int32,(SEQ_LEN,128),1)
    kc[:,:128]=k_ref[...]
    kc[:,128:]=kf_ref[...]
    q=q_ref[...]*jnp.bfloat16(0.125)
    v=v_ref[...]
    zero=jnp.zeros_like(q)
    for h in range(2):
        sel = (lane<64) if h==0 else (lane>=64)
        qc[h,:,:128]=jnp.where(sel,q,zero)
        qc[h,:,128:]=qf_ref[...]
        vm[h]=jnp.where(sel,v,zero)
    for t in range(SEQ_LEN//TQ):
        rows=pl.ds(t*TQ,TQ)
        total=None
        for h in range(2):
            s=dot_nt(qc[h,rows,:],kc[...])
            m=jnp.max(s,axis=1,keepdims=True)
            p=jnp.exp2((s-m)*LOG2E)
            l=jnp.sum(p,axis=1,keepdims=True)
            o=dot_nn(p.astype(jnp.bfloat16),vm[h])*(1.0/l)
            total=o if total is None else total+o
            lse=-(m+jnp.log(l))
            hi=lse.astype(jnp.bfloat16).astype(jnp.float32)
            r=lse-hi
            mid=r.astype(jnp.bfloat16).astype(jnp.float32)
            lo=r-mid
            ln=lax.broadcasted_iota(jnp.int32,(TQ,128),1)
            a=jnp.where(ln==19,hi,jnp.where(ln==20,mid,jnp.where(ln==21,lo,qf_ref[rows,:].astype(jnp.float32))))
            aux_ref[h,rows,:]=a.astype(jnp.bfloat16)
        o_ref[rows,:]=total.astype(jnp.bfloat16)

def attention_forward(q,k,v,qf,kf):
    pair=pl.BlockSpec((SEQ_LEN,128),lambda i:(0,i))
    whole=pl.BlockSpec((SEQ_LEN,128),lambda i:(0,0))
    return pl.pallas_call(fwd_kernel,grid=(H//2,),
        in_specs=[pair,pair,pair,whole,whole],
        out_specs=[pair,pl.BlockSpec((2,SEQ_LEN,128),lambda i:(i,0,0))],
        out_shape=[jax.ShapeDtypeStruct((SEQ_LEN,D),jnp.bfloat16),jax.ShapeDtypeStruct((H,SEQ_LEN,128),jnp.bfloat16)],
        scratch_shapes=[pltpu.VMEM((2,SEQ_LEN,256),jnp.bfloat16),pltpu.VMEM((SEQ_LEN,256),jnp.bfloat16),pltpu.VMEM((2,SEQ_LEN,128),jnp.bfloat16)],
        compiler_params=pltpu.CompilerParams(vmem_limit_bytes=48<<20),
        cost_estimate=pl.CostEstimate(flops=30_000_000_000,bytes_accessed=10_000_000,transcendentals=12_582_912),
        name="attention_forward")(q,k,v,qf,kf)

TK=256
def bwd_kernel(q_ref,k_ref,v_ref,do_ref,o_ref,aux_ref,kf_ref,dq_ref,dk_ref,dv_ref,qc,dc,kc,vc,km,dqa):
    lane = lax.broadcasted_iota(jnp.int32,(SEQ_LEN,128),1)
    kc[:,:128]=k_ref[...]
    kc[:,128:]=kf_ref[...]
    vc[:,:128]=v_ref[...]
    vc[:,128:]=kf_ref[...]
    q=q_ref[...]*jnp.bfloat16(0.125)
    k=k_ref[...]*jnp.bfloat16(0.125)
    do=do_ref[...]
    prod=do.astype(jnp.float32)*o_ref[...].astype(jnp.float32)
    zero=jnp.zeros_like(q)
    for h in range(2):
        sel = (lane<64) if h==0 else (lane>=64)
        qc[h,:,:128]=jnp.where(sel,q,zero)
        qc[h,:,128:]=aux_ref[h]
        km[h]=jnp.where(sel,k,zero)
        dc[h,:,:128]=jnp.where(sel,do,zero)
        delta=-jnp.sum(jnp.where(sel,prod,0.0),axis=1,keepdims=True)
        hi=delta.astype(jnp.bfloat16).astype(jnp.float32)
        lo=delta-hi
        dc[h,:,128:]=jnp.where(lane==19,hi,jnp.where(lane==20,lo,0.0)).astype(jnp.bfloat16)
    for t in range(SEQ_LEN//TK):
        rows=pl.ds(t*TK,TK)
        dv=None;dk=None;dq=None
        for h in range(2):
            s=dot_nt(kc[rows,:],qc[h])
            p=jnp.exp2(s*LOG2E)
            dp=dot_nt(vc[rows,:],dc[h])
            ds=(p*dp).astype(jnp.bfloat16)
            pb=p.astype(jnp.bfloat16)
            dvh=dot_nn(pb,dc[h,:,:128])
            dkh=dot_nn(ds,qc[h,:,:128])
            dqh=dot_tn(ds,km[h,rows,:])
            dv=dvh if dv is None else dv+dvh
            dk=dkh if dk is None else dk+dkh
            dq=dqh if dq is None else dq+dqh
        dk_ref[rows,:]=dk.astype(jnp.bfloat16)
        dv_ref[rows,:]=dv.astype(jnp.bfloat16)
        if t==0: dqa[...]=dq
        else: dqa[...]+=dq
    dq_ref[...]=dqa[...].astype(jnp.bfloat16)

def attention_backward(q,k,v,do,o,aux,kf):
    pair=pl.BlockSpec((SEQ_LEN,128),lambda i:(0,i))
    whole=pl.BlockSpec((SEQ_LEN,128),lambda i:(0,0))
    sd=jax.ShapeDtypeStruct((SEQ_LEN,D),jnp.bfloat16)
    B=jnp.bfloat16
    return pl.pallas_call(bwd_kernel,grid=(H//2,),
        in_specs=[pair]*5+[pl.BlockSpec((2,SEQ_LEN,128),lambda i:(i,0,0)),whole],
        out_specs=[pair]*3,out_shape=[sd]*3,
        scratch_shapes=[pltpu.VMEM((2,SEQ_LEN,256),B),pltpu.VMEM((2,SEQ_LEN,256),B),pltpu.VMEM((SEQ_LEN,256),B),pltpu.VMEM((SEQ_LEN,256),B),pltpu.VMEM((2,SEQ_LEN,128),B),pltpu.VMEM((SEQ_LEN,128),jnp.float32)],
        compiler_params=pltpu.CompilerParams(vmem_limit_bytes=48<<20),
        cost_estimate=pl.CostEstimate(flops=42_000_000_000,bytes_accessed=15_000_000,transcendentals=12_582_912),
        name="attention_backward")(q,k,v,do,o,aux,kf)


def line_gather(piece):
    count = lax.axis_size("fsdp")
    place = lax.axis_index("fsdp")
    held = [piece]
    for step in range(1, count):
        pairs = [(i, (i + step) % count) for i in range(count)]
        held.append(lax.ppermute(piece, "fsdp", pairs))
    turned = jnp.stack([held[(count - 1 - s) % count] for s in range(2 * count - 1)])
    return lax.dynamic_slice_in_dim(turned, count - 1 - place, count, 0)


def line_scatter(parts):
    count = lax.axis_size("fsdp")
    place = lax.axis_index("fsdp")
    total = lax.dynamic_index_in_dim(parts, place, 0, False).astype(jnp.float32)
    for step in range(1, count):
        pairs = [(i, (i + step) % count) for i in range(count)]
        sent = lax.dynamic_index_in_dim(parts, (place + step) % count, 0, False)
        total = total + lax.ppermute(sent, "fsdp", pairs).astype(jnp.float32)
    return total


def rep_bit(bit):
    return (lax.axis_index("rep") // (1 << bit)) % 2


def swap(values, bit):
    pairs = [(i, i ^ (1 << bit)) for i in range(lax.axis_size("rep"))]
    return lax.ppermute(values, "rep", pairs)


def ordered(bit, mine, other, join):
    return jnp.where(rep_bit(bit) == 0, join(mine, other), join(other, mine))


def join_at(axis):
    return lambda a, b: jnp.stack([a, b], axis)


def join_cols(a, b):
    return jnp.concatenate([a, b], -1)


def merge(values, bit, join):
    return ordered(bit, values, swap(values, bit), join)


def gather_square(shards):
    kinds, rows, cols = shards.shape
    rep = lax.axis_index("rep") % 8
    half = cols // 2
    piece = lax.dynamic_slice(
        shards, (0, rep // 2 * (rows // 4), rep % 2 * half), (kinds, rows // 4, half)
    )
    lined = jnp.moveaxis(line_gather(piece), 0, 1)
    left = merge(lined[..., : half // 2 // 128 * 128], 1, join_at(2))
    left = merge(left, 2, join_at(2))
    right = merge(lined[..., half // 2 // 128 * 128 :], 2, join_at(2))
    right = merge(right, 1, join_at(3))
    both = jnp.concatenate([left, right], -1)
    both = merge(both, 0, join_cols)
    return both.reshape(kinds, -1, cols)


def gather_mlp(w_up, w_down):
    rep = lax.axis_index("rep") % 8
    cols = w_up.shape[1] // 8
    rows = w_down.shape[0] // 8
    up = line_gather(lax.dynamic_slice_in_dim(w_up, rep * cols, cols, 1))
    up = up.reshape(-1, cols)
    down = line_gather(
        lax.dynamic_slice_in_dim(w_down, (rep % 2 * 4 + rep // 2) * rows, rows, 0)
    )
    up = merge(up, 1, join_cols)
    down = merge(down, 2, join_at(1))
    up = merge(up, 2, join_cols)
    down = merge(down, 1, join_at(2)).reshape(-1, w_down.shape[1])
    return up, swap(up, 0), down, swap(down, 0)


def add_low(a, b):
    return (a.astype(jnp.float32) + b.astype(jnp.float32)).astype(jnp.bfloat16)


def fold(values, bit, take):
    mine = rep_bit(bit)
    return add_low(take(values, mine), swap(take(values, 1 - mine), bit))


def take_at(axis):
    return lambda values, i: lax.dynamic_index_in_dim(values, i, axis, False)


def take_cols(values, i):
    half = values.shape[-1] // 2
    return lax.dynamic_slice_in_dim(values, i * half, half, values.ndim - 1)


def take_inner(values, i):
    part = values.shape[-1] // 4
    return jnp.concatenate(
        [lax.dynamic_slice_in_dim(values, (2 * j + i) * part, part, 1) for j in range(2)], 1
    )


def beyond(values):
    bit = 3
    while (1 << bit) < lax.axis_size("rep"):
        values = add_low(values, swap(values, bit))
        bit += 1
    return values


def reduce_square(grads):
    kinds, rows, cols = grads.shape
    count = lax.axis_size("fsdp")
    part = fold(grads, 0, take_cols).reshape(kinds, count, 2, 2, -1, cols // 2)
    cut = cols // 4 // 128 * 128
    left = fold(part[..., :cut], 1, take_at(3))
    left = fold(left, 2, take_at(2))
    right = fold(part[..., cut:], 2, take_at(2))
    right = fold(right, 1, take_at(2))
    both = jnp.moveaxis(jnp.concatenate([left, right], -1), 1, 0)
    both = beyond(line_scatter(both).astype(jnp.bfloat16))
    left = merge(merge(both[..., :cut], 1, join_at(1)), 2, join_at(1))
    right = merge(merge(both[..., cut:], 2, join_at(1)), 1, join_at(2))
    both = merge(jnp.concatenate([left, right], -1), 0, join_cols)
    return both.reshape(kinds, -1, cols).astype(jnp.float32)


def reduce_up(grad):
    count = lax.axis_size("fsdp")
    part = fold(grad, 1, take_inner)
    part = fold(part, 2, take_cols)
    part = line_scatter(part.reshape(count, -1, part.shape[1]))
    part = beyond(part.astype(jnp.bfloat16))
    part = merge(part, 1, join_at(0))
    part = merge(part, 2, join_at(0))
    other = swap(part, 0)

    def join(a, b):
        return jnp.concatenate(
            [v[y, x] for y in range(2) for x in range(2) for v in (a, b)], 1
        ).astype(jnp.float32)

    return ordered(0, part, other, join)


def reduce_down(grad):
    count = lax.axis_size("fsdp")
    part = grad.reshape(count, 2, 2, -1, grad.shape[1])
    part = fold(part, 2, take_at(1))
    part = fold(part, 1, take_at(1))
    part = beyond(line_scatter(part).astype(jnp.bfloat16))
    part = merge(part, 1, join_at(0))
    part = merge(part, 2, join_at(0))
    part = merge(part, 0, join_at(0))
    return part.reshape(-1, grad.shape[1]).astype(jnp.float32)


def reduce_all(values):
    bit = 0
    while (1 << bit) < lax.axis_size("rep"):
        values = values + swap(values, bit)
        bit += 1
    count = lax.axis_size("fsdp")
    total = values
    for step in range(1, count):
        pairs = [(i, (i + step) % count) for i in range(count)]
        total = total + lax.ppermute(values, "fsdp", pairs)
    return total


def per_device(
    tokens,
    segments,
    random_blocks,
    out_grad,
    w_query,
    w_key,
    w_value,
    w_out,
    w_up,
    w_down,
    vectors,
    up_bias,
):
    count = lax.axis_size("fsdp")
    place = lax.axis_index("fsdp")
    small = line_gather(jnp.concatenate([vectors, up_bias.reshape(4, -1)], 0))
    full_vectors = jnp.moveaxis(small[:, :8], 0, 1).reshape(8, -1)
    bias_halves = small[:, 8:].reshape(count, 2, -1).astype(jnp.float32)
    core = rep_bit(0)
    bias_mine = lax.dynamic_index_in_dim(bias_halves, core, 1, False).reshape(-1)
    bias_other = lax.dynamic_index_in_dim(bias_halves, 1 - core, 1, False).reshape(-1)
    first = gather_square(jnp.stack([w_query, w_key, w_value]))
    full_query, full_key, full_value = first[0], first[1], first[2]
    (full_out,) = gather_square(w_out[None])
    up_mine, up_other, down_mine, down_other = gather_mlp(w_up, w_down)

    vec_float = full_vectors.astype(jnp.float32)
    inputs = tokens.astype(jnp.float32)
    q_low = (jnp.dot(tokens, full_query, preferred_element_type=jnp.float32) + vec_float[0]).astype(
        jnp.bfloat16
    )
    k_low = jnp.dot(tokens, full_key, preferred_element_type=jnp.float32).astype(jnp.bfloat16)
    v_low = (jnp.dot(tokens, full_value, preferred_element_type=jnp.float32) + vec_float[1]).astype(
        jnp.bfloat16
    )
    q_feat, k_feat = mask_features(segments, random_blocks[0])
    mixed_low, aux = attention_forward(q_low, k_low, v_low, q_feat, k_feat)
    attn_out = jnp.dot(mixed_low, full_out, preferred_element_type=jnp.float32) + vec_float[2]
    first_sum = inputs + attn_out
    normed_one, pull_one = jax.vjp(normalize, first_sum, vec_float[3], vec_float[4])
    normed_low = normed_one.astype(jnp.bfloat16)

    def widen(weight, bias):
        up_proj = jnp.dot(normed_low, weight, preferred_element_type=jnp.float32) + bias
        activated, pull = jax.vjp(gelu_exact, up_proj)
        return activated.astype(jnp.bfloat16), pull

    act_mine, pull_mine = widen(up_mine, bias_mine)
    act_other, pull_other = widen(up_other, bias_other)
    mlp_out = (
        jnp.dot(act_mine, down_mine, preferred_element_type=jnp.float32)
        + jnp.dot(act_other, down_other, preferred_element_type=jnp.float32)
        + vec_float[5]
    )
    second_sum = normed_one + mlp_out
    layer_out, pull_two = jax.vjp(normalize, second_sum, vec_float[6], vec_float[7])
    valid = (segments >= 0).astype(jnp.float32)[:, None]
    squares = jnp.stack(
        [
            jnp.sum(valid * first_sum * first_sum),
            jnp.sum(valid * attn_out * attn_out),
            jnp.sum(valid * mlp_out * mlp_out),
            jnp.sum(valid),
        ]
    )
    d_second, d_gain_two, d_shift_two = pull_two(out_grad.astype(jnp.float32))
    d_mlp = d_second.astype(jnp.bfloat16)

    down_sent = swap(dot_tn(act_other, d_mlp).astype(jnp.bfloat16), 0)
    d_up_other = pull_other(dot_nt(d_mlp, down_other))[0].astype(jnp.bfloat16)
    up_sent = swap(dot_tn(normed_low, d_up_other).astype(jnp.bfloat16), 0)
    d_up_mine = pull_mine(dot_nt(d_mlp, down_mine))[0].astype(jnp.bfloat16)
    grad_down = reduce_down(
        (dot_tn(act_mine, d_mlp) + down_sent.astype(jnp.float32)).astype(jnp.bfloat16)
    )
    grad_up = reduce_up(
        (dot_tn(normed_low, d_up_mine) + up_sent.astype(jnp.float32)).astype(jnp.bfloat16)
    )
    d_normed = d_second + dot_nt(d_up_mine, up_mine) + dot_nt(d_up_other, up_other)
    d_first, d_gain_one, d_shift_one = pull_one(d_normed)
    d_attn = d_first.astype(jnp.bfloat16)
    d_mixed = dot_nt(d_attn, full_out).astype(jnp.bfloat16)
    (grad_out,) = reduce_square(dot_tn(mixed_low, d_attn).astype(jnp.bfloat16)[None])
    dq_low, dk_low, dv_low = attention_backward(
        q_low, k_low, v_low, d_mixed, mixed_low, aux, k_feat
    )
    grad_first = reduce_square(
        jnp.stack([dot_tn(tokens, d).astype(jnp.bfloat16) for d in (dq_low, dk_low, dv_low)])
    )
    tokens_grad = (
        d_first + dot_nt(dq_low, full_query) + dot_nt(dk_low, full_key) + dot_nt(dv_low, full_value)
    )
    bias_mine = col_sums(d_up_mine).reshape(count, -1)
    bias_other = col_sums(d_up_other).reshape(count, -1)
    grad_bias = ordered(0, bias_mine, bias_other, join_cols)
    grad_vectors = jnp.stack(
        [
            col_sums(dq_low),
            col_sums(dv_low),
            col_sums(d_attn),
            d_gain_one,
            d_shift_one,
            col_sums(d_mlp),
            d_gain_two,
            d_shift_two,
            jnp.zeros((D,), jnp.float32).at[:4].set(squares),
        ]
    )
    sums = reduce_all(jnp.concatenate([grad_vectors, grad_bias.reshape(-1, D)], 0))
    width = vectors.shape[1]
    rms_values = jnp.sqrt(sums[8, :3] / (sums[8, 3] * D))
    bias_sums = sums[9:].reshape(count, -1)
    return (
        layer_out.astype(jnp.bfloat16),
        tokens_grad.astype(jnp.bfloat16),
        grad_first[0],
        grad_first[1],
        grad_first[2],
        grad_out,
        grad_up,
        grad_down,
        lax.dynamic_slice_in_dim(sums[:8], place * width, width, 1),
        lax.dynamic_index_in_dim(bias_sums, place, 0, False),
        rms_values,
    )


def solution(mesh):
    in_specs = (
        P(("rep", "fsdp"), None),
        P(("rep", "fsdp")),
        P(("rep", "fsdp"), None, None),
        P(("rep", "fsdp"), None),
        P("fsdp", None),
        P("fsdp", None),
        P("fsdp", None),
        P("fsdp", None),
        P("fsdp", None),
        P("fsdp", None),
        P(None, "fsdp"),
        P("fsdp"),
    )
    out_specs = (
        P(("rep", "fsdp"), None),
        P(("rep", "fsdp"), None),
        P("fsdp", None),
        P("fsdp", None),
        P("fsdp", None),
        P("fsdp", None),
        P("fsdp", None),
        P("fsdp", None),
        P(None, "fsdp"),
        P("fsdp"),
        P(),
    )
    return jax.shard_map(
        per_device, mesh=mesh, in_specs=in_specs, out_specs=out_specs, check_vma=False
    )
```

```python
import functools

import jax
import jax.numpy as jnp
from jax import lax
from jax.experimental import pallas as pl
from jax.experimental.pallas import tpu as pltpu
from jax.sharding import PartitionSpec as P

D = 768
H = 12
DH = 64
BLK = 64
SEQ_LEN = 1024
NB = 16


masked_score = -1e30
layer_eps = 1e-05


def normalize(values, gain, shift):
    centered = values - jnp.mean(values, axis=-1, keepdims=True)
    variance = jnp.mean(centered * centered, axis=-1, keepdims=True)
    return centered * lax.rsqrt(variance + layer_eps) * gain + shift


def gelu_exact(values):
    return jax.nn.gelu(values, approximate=False)


def dot_tn(left, right):
    return lax.dot_general(
        left, right, (((0,), (0,)), ((), ())), preferred_element_type=jnp.float32
    )


def dot_nt(left, right):
    return lax.dot_general(
        left, right, (((1,), (1,)), ((), ())), preferred_element_type=jnp.float32
    )


def col_sums(values):
    return jnp.sum(values.astype(jnp.float32), axis=0)


LOG2E=1.4426950408889634
BIG=1e30

def dot_nn(a,b): return lax.dot_general(a,b,(((1,),(0,)),((),())),preferred_element_type=jnp.float32)

def mask_features(seg_row, random_row):
    blocks = jnp.arange(NB, dtype=jnp.int32)
    near = jnp.abs(blocks[:, None] - blocks[None, :]) <= 1
    first = (blocks[:, None] < 2) | (blocks[None, :] < 2)
    picked = jnp.any(random_row[:, :, None] == blocks[None, None, :], axis=1)
    seen = first | near | picked
    q_block = jnp.where(seen, 0.0, -BIG)
    q_block = jnp.repeat(q_block, BLK, axis=0)
    k_block = jnp.repeat(jnp.eye(NB, dtype=jnp.float32), BLK, axis=0)
    numbers = jnp.arange(-1, 2, dtype=jnp.int32)
    same = seg_row[:, None] == numbers[None, :]
    q_seg = jnp.where(same, 0.0, -BIG)
    k_seg = same.astype(jnp.float32)
    rest = SEQ_LEN, 128 - NB - 3
    ones = jnp.ones((SEQ_LEN, 3), jnp.float32)
    q_feat = jnp.concatenate([q_block, q_seg, jnp.zeros(rest, jnp.float32)], axis=1)
    k_feat = jnp.concatenate([k_block, k_seg, ones, jnp.zeros((SEQ_LEN, 128 - NB - 6), jnp.float32)], axis=1)
    return q_feat.astype(jnp.bfloat16), k_feat.astype(jnp.bfloat16)

MESH = pl.DeviceIdType.MESH


def bit_of(index, bit):
    return lax.rem(lax.div(index, 1 << bit), 2)


def flipped(index, bit):
    return index + (1 - 2 * bit_of(index, bit)) * (1 << bit)


def greet(extra_bits=()):
    rep = lax.axis_index("rep")
    place = lax.axis_index("fsdp")
    count = lax.axis_size("fsdp")
    barrier = pltpu.get_barrier_semaphore()
    bits = (0, 1, 2) + tuple(extra_bits)
    for bit in bits:
        pl.semaphore_signal(
            barrier, inc=1, device_id={"rep": flipped(rep, bit)}, device_id_type=MESH
        )
    for step in range(1, count):
        pl.semaphore_signal(
            barrier,
            inc=1,
            device_id={"fsdp": lax.rem(place + step, count)},
            device_id_type=MESH,
        )
    pl.semaphore_wait(barrier, len(bits) + count - 1)


def region(kind, rows, cols, order, level):
    rep = lax.axis_index("rep")
    core = bit_of(rep, 0)
    first, second = bit_of(rep, order[0]), bit_of(rep, order[1])
    index = (second * 2 + first, second * 2, 0)[level]
    units = (1, 2, 4)[level]
    if kind == "square":
        unit = rows // 4
        return (
            pl.ds(pl.multiple_of(index * unit, unit), units * unit),
            pl.ds(pl.multiple_of(core * (cols // 2), cols // 2), cols // 2),
        )
    if kind == "wide":
        unit = cols // 8
        return (
            pl.ds(0, rows),
            pl.ds(pl.multiple_of((core * 4 + index) * unit, unit), units * unit),
        )
    unit = rows // 8
    return (
        pl.ds(pl.multiple_of((core * 4 + index) * unit, unit), units * unit),
        pl.ds(0, cols),
    )


AHEAD = 99
SPAN = 3


class Gather:
    def __init__(self, kinds, shards, fulls, send, recv, local):
        self.kinds, self.shards, self.fulls = kinds, shards, fulls
        self.send, self.recv, self.local = send, recv, local
        self.count = lax.axis_size("fsdp")
        self.rep, self.place = lax.axis_index("rep"), lax.axis_index("fsdp")
        self.greeted = ()
        self.blocks = []
        for step in range(1, self.count):
            for a in range(len(kinds)):
                order = (1, 2) if (a + step) % 2 == 0 else (2, 1)
                self.blocks.append((a, step, order))

    def copy(self, k, stage):
        a, step, order = self.blocks[k]
        kind, shard, full = self.kinds[a], self.shards[a], self.fulls[a]
        rows, cols = shard.shape
        if stage == 0:
            if kind == "whole":
                src, dst = shard, full.at[self.place]
            else:
                r, c = region(kind, rows, cols, order, 0)
                src, dst = shard.at[r, c], full.at[self.place, r, c]
            device = {"fsdp": lax.rem(self.place + step, self.count)}
        else:
            r, c = region(kind, rows, cols, order, stage - 1)
            origin = lax.rem(self.place + self.count - step, self.count)
            src = dst = full.at[origin, r, c]
            device = {"rep": flipped(self.rep, (order + (0,))[stage - 1])}
        return pltpu.make_async_remote_copy(
            src_ref=src,
            dst_ref=dst,
            send_sem=self.send.at[k, stage],
            recv_sem=self.recv.at[k, stage],
            device_id=device,
            device_id_type=MESH,
        )

    def stages(self, k):
        return 1 if self.kinds[self.blocks[k][0]] == "whole" else 4

    def own(self, a):
        return pltpu.make_async_copy(
            self.shards[a], self.fulls[a].at[self.place], self.local.at[a]
        )

    def begin(self):
        for k in range(min(AHEAD, len(self.blocks))):
            self.copy(k, 0).start()
        for a in range(len(self.kinds)):
            self.own(a).start()

    def ticks(self):
        return len(self.blocks) + 3 * SPAN

    def tick(self, t):
        for stage in range(1, 5):
            k = t - (stage - 1) * SPAN
            if 0 <= k < len(self.blocks) and stage <= self.stages(k):
                self.copy(k, stage - 1).wait_recv()
                if stage == 1 and k + AHEAD < len(self.blocks):
                    self.copy(k + AHEAD, 0).start()
                if stage < self.stages(k):
                    self.copy(k, stage).start()

    def finish(self):
        for k in range(len(self.blocks)):
            for stage in range(self.stages(k)):
                self.copy(k, stage).wait_send()
        for a in range(len(self.kinds)):
            self.own(a).wait()


def gather_kernel(kinds, *refs):
    n = len(kinds)
    job = Gather(kinds, refs[:n], refs[n : 2 * n], *refs[2 * n :])
    greet()
    job.begin()
    for t in range(job.ticks()):
        job.tick(t)
    job.finish()


def gather_sems(kinds, count):
    blocks = len(kinds) * (count - 1)
    return [
        pltpu.SemaphoreType.DMA((blocks, 4)),
        pltpu.SemaphoreType.DMA((blocks, 4)),
        pltpu.SemaphoreType.DMA((len(kinds),)),
    ]


def gather(kinds, shards, collective_id, name):
    count = lax.axis_size("fsdp")
    return pl.pallas_call(
        functools.partial(gather_kernel, kinds),
        in_specs=[pl.BlockSpec(memory_space=pltpu.VMEM)] * len(kinds),
        out_specs=[pl.BlockSpec(memory_space=pl.ANY)] * len(kinds),
        out_shape=[jax.ShapeDtypeStruct((count, *s.shape), s.dtype) for s in shards],
        scratch_shapes=gather_sems(kinds, count),
        compiler_params=pltpu.CompilerParams(
            collective_id=collective_id, has_side_effects=True, vmem_limit_bytes=24 << 20
        ),
        name=name,
    )(*shards)


LAG = 3


def half_shape(kind, rows, cols):
    return (rows // 2, cols) if kind == "tall" else (rows, cols // 2)


def part_shape(kind, rows, cols, level):
    r, c = half_shape(kind, rows, cols)
    cut = (4, 2, 1)[level]
    return (r, c // cut) if kind == "wide" else (r // cut, c)


def part(kind, rows, cols, first, second, level):
    index = (second * 2 + first, second * 2, 0)[level]
    units = (1, 2, 4)[level]
    r, c = half_shape(kind, rows, cols)
    if kind == "wide":
        unit = c // 4
        return pl.ds(0, r), pl.ds(pl.multiple_of(index * unit, unit), units * unit)
    unit = r // 4
    return pl.ds(pl.multiple_of(index * unit, unit), units * unit), pl.ds(0, c)


def half(kind, rows, cols, core):
    r, c = half_shape(kind, rows, cols)
    if kind == "tall":
        return pl.ds(pl.multiple_of(core * r, r), r), pl.ds(0, c)
    return pl.ds(0, r), pl.ds(pl.multiple_of(core * c, c), c)


def add_into(target, where, values):
    rows, cols = where
    chunk = 16
    total, base = rows.size, rows.start

    @pl.loop(0, total // chunk)
    def _(i):
        at = pl.ds(pl.multiple_of(base + i * chunk, chunk), chunk)
        more = values[pl.ds(pl.multiple_of(i * chunk, chunk), chunk), :]
        kept = target[at, cols]
        target[at, cols] = (kept.astype(jnp.float32) + more.astype(jnp.float32)).astype(
            target.dtype
        )


class Reduce:
    def __init__(self, kinds, grads, results, scratch, extra):
        self.kinds, self.grads, self.results, self.extra = kinds, grads, results, extra
        self.greeted = extra
        n = len(kinds)
        self.acc, self.got0, self.got1, self.got2, self.got3 = (
            scratch[i * n : (i + 1) * n] for i in range(5)
        )
        self.outs, rest = scratch[5 * n : 6 * n], scratch[6 * n :]
        if extra:
            self.gotx, rest = rest[:n], rest[n:]
        self.load, self.send, self.recv, self.gsend, self.grecv, self.store = rest[:6]
        self.count = lax.axis_size("fsdp")
        self.rep, self.place = lax.axis_index("rep"), lax.axis_index("fsdp")
        self.blocks = [
            (a, step) for step in list(range(1, self.count)) + [0] for a in range(n)
        ]

    def order(self, a):
        return (1, 2) if a % 2 == 0 else (2, 1)

    def bits(self, a):
        order = self.order(a)
        return bit_of(self.rep, order[0]), bit_of(self.rep, order[1])

    def shape(self, a):
        return self.grads[a].shape[1:]

    def mine(self, k):
        a, step = self.blocks[k]
        where = lax.rem(self.place + step, self.count)
        r, c = half(self.kinds[a], *self.shape(a), bit_of(self.rep, 0))
        return pltpu.make_async_copy(
            self.grads[a].at[where, r, c], self.acc[a].at[step], self.load.at[k]
        )

    def copy(self, k, stage):
        a, step = self.blocks[k]
        kind, shape = self.kinds[a], self.shape(a)
        first, second = self.bits(a)
        order = self.order(a)
        if stage == 0:
            where = lax.rem(self.place + step, self.count)
            r, c = half(kind, *shape, 1 - bit_of(self.rep, 0))
            src, dst = self.grads[a].at[where, r, c], self.got0[a].at[step]
            device = {"rep": flipped(self.rep, 0)}
        elif stage == 1:
            r, c = part(kind, *shape, first, 1 - second, 1)
            src, dst = self.acc[a].at[step, r, c], self.got1[a].at[step]
            device = {"rep": flipped(self.rep, order[1])}
        elif stage == 2:
            r, c = part(kind, *shape, 1 - first, second, 0)
            src, dst = self.acc[a].at[step, r, c], self.got2[a].at[step]
            device = {"rep": flipped(self.rep, order[0])}
        else:
            r, c = part(kind, *shape, first, second, 0)
            src, dst = self.acc[a].at[step, r, c], self.got3[a].at[step - 1]
            device = {"fsdp": lax.rem(self.place + step, self.count)}
        return pltpu.make_async_remote_copy(
            src_ref=src,
            dst_ref=dst,
            send_sem=self.send.at[k, stage],
            recv_sem=self.recv.at[k, stage],
            device_id=device,
            device_id_type=MESH,
        )

    def whole(self, a, level):
        kind, (rows, cols) = self.kinds[a], self.shape(a)
        return region(kind, rows, cols, self.order(a), level)

    def back(self, a, level):
        r, c = self.whole(a, level)
        ref = self.outs[a].at[r, c]
        bit = (self.order(a) + (0,))[level]
        return pltpu.make_async_remote_copy(
            src_ref=ref,
            dst_ref=ref,
            send_sem=self.gsend.at[a, level],
            recv_sem=self.grecv.at[a, level],
            device_id={"rep": flipped(self.rep, bit)},
            device_id_type=MESH,
        )

    def more(self, a, i):
        r, c = self.whole(a, 0)
        return pltpu.make_async_remote_copy(
            src_ref=self.outs[a].at[r, c],
            dst_ref=self.gotx[a].at[i],
            send_sem=self.gsend.at[a, 3 + i],
            recv_sem=self.grecv.at[a, 3 + i],
            device_id={"rep": flipped(self.rep, self.extra[i])},
            device_id_type=MESH,
        )

    def begin(self):
        for k in range(len(self.blocks)):
            self.copy(k, 0).start()
            self.mine(k).start()

    def absorb(self, k, stage):
        a, step = self.blocks[k]
        kind, shape = self.kinds[a], self.shape(a)
        first, second = self.bits(a)
        got = (self.got0, self.got1, self.got2)[stage][a].at[step]
        where = part(kind, *shape, first, second, 2 - stage)
        if stage == 0:
            self.mine(k).wait()
        self.copy(k, stage).wait_recv()
        add_into(self.acc[a].at[step], where, got)
        if stage < 2 or step:
            self.copy(k, stage + 1).start()

    def total(self, a):
        kind, shape = self.kinds[a], self.shape(a)
        first, second = self.bits(a)
        for step in range(1, self.count):
            self.copy(self.blocks.index((a, step)), 3).wait_recv()
        rows, cols = part(kind, *shape, first, second, 0)
        to_rows, to_cols = self.whole(a, 0)
        chunk = 16

        @pl.loop(0, rows.size // chunk)
        def _(i):
            at = pl.ds(pl.multiple_of(rows.start + i * chunk, chunk), chunk)
            total = self.acc[a][0, at, cols].astype(jnp.float32)
            near = pl.ds(pl.multiple_of(i * chunk, chunk), chunk)
            for step in range(self.count - 1):
                total = total + self.got3[a][step, near, :].astype(jnp.float32)
            to = pl.ds(pl.multiple_of(to_rows.start + i * chunk, chunk), chunk)
            self.outs[a][to, to_cols] = total.astype(jnp.bfloat16)

        for i in range(len(self.extra)):
            copy = self.more(a, i)
            copy.start()
            copy.wait()
            add_into(self.outs[a], self.whole(a, 0), self.gotx[a].at[i])
        self.back(a, 0).start()

    def put(self, a):
        return pltpu.make_async_copy(self.outs[a], self.results[a], self.store.at[a])

    def ticks(self):
        return len(self.blocks) + 6 * LAG

    def tick(self, t):
        blocks = len(self.blocks)
        for stage in range(3):
            k = t - stage * LAG
            if 0 <= k < blocks:
                self.absorb(k, stage)
        for a in range(len(self.kinds)):
            late = t - self.blocks.index((a, 0)) - 3 * LAG
            if late == 0:
                self.total(a)
            elif late in (LAG, 2 * LAG, 3 * LAG):
                level = late // LAG
                self.back(a, level - 1).wait_recv()
                if level < 3:
                    self.back(a, level).start()
                else:
                    self.put(a).start()

    def finish(self):
        for k, (a, step) in enumerate(self.blocks):
            for stage in range(4 if step else 3):
                self.copy(k, stage).wait_send()
        for a in range(len(self.kinds)):
            for level in range(3):
                self.back(a, level).wait_send()
            self.put(a).wait()


class Sums:
    def __init__(self, source, result, held, got, send, recv, extra):
        self.source, self.result, self.held, self.got = source, result, held, got
        self.send, self.recv = send, recv
        self.bits = (0, 1, 2) + tuple(extra)
        self.count = lax.axis_size("fsdp")
        self.rep, self.place = lax.axis_index("rep"), lax.axis_index("fsdp")

    def copy(self, i):
        level = min(i, len(self.bits))
        src = self.source if level == 0 else self.held.at[level - 1]
        if i < len(self.bits):
            device = {"rep": flipped(self.rep, self.bits[i])}
        else:
            step = i - len(self.bits) + 1
            device = {"fsdp": lax.rem(self.place + step, self.count)}
        return pltpu.make_async_remote_copy(
            src_ref=src,
            dst_ref=self.got.at[i],
            send_sem=self.send.at[i],
            recv_sem=self.recv.at[i],
            device_id=device,
            device_id_type=MESH,
        )

    def begin(self):
        self.copy(0).start()

    def ticks(self):
        return len(self.bits) + 1

    def tick(self, t):
        bits = len(self.bits)
        if t < bits:
            self.copy(t).wait_recv()
            before = self.source[...] if t == 0 else self.held[t - 1]
            self.held[t] = before + self.got[t]
            for i in range(t + 1, t + 2 if t + 1 < bits else bits + self.count - 1):
                self.copy(i).start()
        elif t == bits:
            total = self.held[bits - 1]
            for i in range(bits, bits + self.count - 1):
                self.copy(i).wait_recv()
                total = total + self.got[i]
            self.result[...] = total

    def finish(self):
        for i in range(len(self.bits) + self.count - 1):
            self.copy(i).wait_send()


def reduce_scratch(kinds, shapes, count, extra):
    B = jnp.bfloat16
    sizes = [(k, *s) for k, s in zip(kinds, shapes)]
    made = [pltpu.VMEM((count, *half_shape(*s)), B) for s in sizes]
    made += [pltpu.VMEM((count, *half_shape(*s)), B) for s in sizes]
    made += [pltpu.VMEM((count, *part_shape(*s, 1)), B) for s in sizes]
    made += [pltpu.VMEM((count, *part_shape(*s, 0)), B) for s in sizes]
    made += [pltpu.VMEM((count - 1, *part_shape(*s, 0)), B) for s in sizes]
    made += [pltpu.VMEM(s, B) for s in shapes]
    if extra:
        made += [pltpu.VMEM((len(extra), *part_shape(*s, 0)), B) for s in sizes]
    n = len(kinds)
    dma = pltpu.SemaphoreType.DMA
    made += [dma((n * count,)), dma((n * count, 4)), dma((n * count, 4))]
    made += [dma((n, 3 + len(extra))), dma((n, 3 + len(extra))), dma((n,))]
    return made


def sums_scratch(shape, count, extra):
    bits = 3 + len(extra)
    dma = pltpu.SemaphoreType.DMA
    return [
        pltpu.VMEM((bits, *shape), jnp.float32),
        pltpu.VMEM((bits + count - 1, *shape), jnp.float32),
        dma((bits + count - 1,)),
        dma((bits + count - 1,)),
    ]


def extra_bits():
    found, bit = [], 3
    while (1 << bit) < lax.axis_size("rep"):
        found.append(bit)
        bit += 1
    return tuple(found)


def reduce_kernel(kinds, extra, *refs):
    n = len(kinds)
    grads, small, outs, total = refs[:n], refs[n], refs[n + 1 : 2 * n + 1], refs[2 * n + 1]
    scratch = refs[2 * n + 2 :]
    job = Reduce(kinds, grads, outs, scratch[:-4], extra)
    sums = Sums(small, total, *scratch[-4:], extra)
    greet(extra)
    job.begin()
    sums.begin()
    for t in range(max(job.ticks(), sums.ticks())):
        job.tick(t)
        sums.tick(t)
    job.finish()
    sums.finish()


def reduce_last(kinds, grads, small, collective_id, name):
    count = lax.axis_size("fsdp")
    extra = extra_bits()
    shapes = [g.shape[1:] for g in grads]
    vmem = pl.BlockSpec(memory_space=pltpu.VMEM)
    return pl.pallas_call(
        functools.partial(reduce_kernel, kinds, extra),
        in_specs=[pl.BlockSpec(memory_space=pl.ANY)] * len(kinds) + [vmem],
        out_specs=[pl.BlockSpec(memory_space=pl.ANY)] * len(kinds) + [vmem],
        out_shape=[jax.ShapeDtypeStruct(s, jnp.bfloat16) for s in shapes]
        + [jax.ShapeDtypeStruct(small.shape, jnp.float32)],
        scratch_shapes=reduce_scratch(kinds, shapes, count, extra)
        + sums_scratch(small.shape, count, extra),
        compiler_params=pltpu.CompilerParams(
            collective_id=collective_id, has_side_effects=True, vmem_limit_bytes=48 << 20
        ),
        name=name,
    )(*grads, small)


TQ=256
POINTS = 12


def tick_at(points, job, half):
    for point, ticks in points.items():
        if point % 2 == half:

            @pl.when(pl.program_id(0) == point // 2)
            def _(ticks=ticks):
                if ticks.start == 0:
                    greet(job.greeted)
                    job.begin()
                for t in ticks[1:] if ticks.start == 0 else ticks:
                    job.tick(t - 1)


def finish_at(points, job):
    done = max(t.stop for t in points.values())

    @pl.when(pl.program_id(0) == POINTS // 2 - 1)
    def _():
        for t in range(done, job.ticks() + 1):
            job.tick(t - 1)
        job.finish()


GATHER_POINTS = {0: range(0, 1), 4: range(1, 4), 6: range(4, 7), 8: range(7, 10), 9: range(10, 13), 10: range(13, 16)}
REDUCE_POINTS = {0: range(0, 1), 2: range(1, 4), 3: range(4, 7), 5: range(7, 10), 6: range(10, 13), 8: range(13, 16), 10: range(16, 19)}
REST = ("square", "wide", "tall")


def fwd_kernel(q_ref,k_ref,v_ref,qf_ref,kf_ref,s0,s1,s2,o_ref,aux_ref,f0,f1,f2,qc,kc,vm,*sems):
    job = Gather(REST, (s0, s1, s2), (f0, f1, f2), *sems)
    tick_at(GATHER_POINTS, job, 0)
    lane = lax.broadcasted_iota(jnp.int32,(SEQ_LEN,128),1)
    kc[:,:128]=k_ref[...]
    kc[:,128:]=kf_ref[...]
    q=q_ref[...]*jnp.bfloat16(0.125)
    v=v_ref[...]
    zero=jnp.zeros_like(q)
    for h in range(2):
        sel = (lane<64) if h==0 else (lane>=64)
        qc[h,:,:128]=jnp.where(sel,q,zero)
        qc[h,:,128:]=qf_ref[...]
        vm[h]=jnp.where(sel,v,zero)
    for t in range(SEQ_LEN//TQ):
        if t==2: tick_at(GATHER_POINTS, job, 1)
        rows=pl.ds(t*TQ,TQ)
        total=None
        for h in range(2):
            s=dot_nt(qc[h,rows,:],kc[...])
            m=jnp.max(s,axis=1,keepdims=True)
            p=jnp.exp2((s-m)*LOG2E)
            l=jnp.sum(p,axis=1,keepdims=True)
            o=dot_nn(p.astype(jnp.bfloat16),vm[h])*(1.0/l)
            total=o if total is None else total+o
            lse=-(m+jnp.log(l))
            hi=lse.astype(jnp.bfloat16).astype(jnp.float32)
            r=lse-hi
            mid=r.astype(jnp.bfloat16).astype(jnp.float32)
            lo=r-mid
            ln=lax.broadcasted_iota(jnp.int32,(TQ,128),1)
            a=jnp.where(ln==19,hi,jnp.where(ln==20,mid,jnp.where(ln==21,lo,qf_ref[rows,:].astype(jnp.float32))))
            aux_ref[h,rows,:]=a.astype(jnp.bfloat16)
        o_ref[rows,:]=total.astype(jnp.bfloat16)
    finish_at(GATHER_POINTS, job)

def attention_forward(q,k,v,qf,kf,shards):
    count=lax.axis_size("fsdp")
    vmem=[pl.BlockSpec(memory_space=pltpu.VMEM)]*3
    hbm=[pl.BlockSpec(memory_space=pl.ANY)]*3
    pair=pl.BlockSpec((SEQ_LEN,128),lambda i:(0,i))
    whole=pl.BlockSpec((SEQ_LEN,128),lambda i:(0,0))
    return pl.pallas_call(fwd_kernel,grid=(H//2,),
        in_specs=[pair,pair,pair,whole,whole]+vmem,
        out_specs=[pair,pl.BlockSpec((2,SEQ_LEN,128),lambda i:(i,0,0))]+hbm,
        out_shape=[jax.ShapeDtypeStruct((SEQ_LEN,D),jnp.bfloat16),jax.ShapeDtypeStruct((H,SEQ_LEN,128),jnp.bfloat16)]+[jax.ShapeDtypeStruct((count,*s.shape),s.dtype) for s in shards],
        scratch_shapes=[pltpu.VMEM((2,SEQ_LEN,256),jnp.bfloat16),pltpu.VMEM((SEQ_LEN,256),jnp.bfloat16),pltpu.VMEM((2,SEQ_LEN,128),jnp.bfloat16)]+gather_sems(REST,count),
        compiler_params=pltpu.CompilerParams(vmem_limit_bytes=48<<20,collective_id=1,has_side_effects=True),
        cost_estimate=pl.CostEstimate(flops=30_000_000_000,bytes_accessed=10_000_000,transcendentals=12_582_912),
        name="attention_forward")(q,k,v,qf,kf,*shards)

TK=256
def bwd_kernel(extra,q_ref,k_ref,v_ref,do_ref,o_ref,aux_ref,kf_ref,g0,g1,g2,dq_ref,dk_ref,dv_ref,r0,r1,r2,qc,dc,kc,vc,km,dqa,*scratch):
    job = Reduce(REST, (g0, g1, g2), (r0, r1, r2), scratch, extra)
    tick_at(REDUCE_POINTS, job, 0)
    lane = lax.broadcasted_iota(jnp.int32,(SEQ_LEN,128),1)
    kc[:,:128]=k_ref[...]
    kc[:,128:]=kf_ref[...]
    vc[:,:128]=v_ref[...]
    vc[:,128:]=kf_ref[...]
    q=q_ref[...]*jnp.bfloat16(0.125)
    k=k_ref[...]*jnp.bfloat16(0.125)
    do=do_ref[...]
    prod=do.astype(jnp.float32)*o_ref[...].astype(jnp.float32)
    zero=jnp.zeros_like(q)
    for h in range(2):
        sel = (lane<64) if h==0 else (lane>=64)
        qc[h,:,:128]=jnp.where(sel,q,zero)
        qc[h,:,128:]=aux_ref[h]
        km[h]=jnp.where(sel,k,zero)
        dc[h,:,:128]=jnp.where(sel,do,zero)
        delta=-jnp.sum(jnp.where(sel,prod,0.0),axis=1,keepdims=True)
        hi=delta.astype(jnp.bfloat16).astype(jnp.float32)
        lo=delta-hi
        dc[h,:,128:]=jnp.where(lane==19,hi,jnp.where(lane==20,lo,0.0)).astype(jnp.bfloat16)
    for t in range(SEQ_LEN//TK):
        if t==2: tick_at(REDUCE_POINTS, job, 1)
        rows=pl.ds(t*TK,TK)
        dv=None;dk=None;dq=None
        for h in range(2):
            s=dot_nt(kc[rows,:],qc[h])
            p=jnp.exp2(s*LOG2E)
            dp=dot_nt(vc[rows,:],dc[h])
            ds=(p*dp).astype(jnp.bfloat16)
            pb=p.astype(jnp.bfloat16)
            dvh=dot_nn(pb,dc[h,:,:128])
            dkh=dot_nn(ds,qc[h,:,:128])
            dqh=dot_tn(ds,km[h,rows,:])
            dv=dvh if dv is None else dv+dvh
            dk=dkh if dk is None else dk+dkh
            dq=dqh if dq is None else dq+dqh
        dk_ref[rows,:]=dk.astype(jnp.bfloat16)
        dv_ref[rows,:]=dv.astype(jnp.bfloat16)
        if t==0: dqa[...]=dq
        else: dqa[...]+=dq
    dq_ref[...]=dqa[...].astype(jnp.bfloat16)
    finish_at(REDUCE_POINTS, job)

def attention_backward(q,k,v,do,o,aux,kf,grads):
    count=lax.axis_size("fsdp")
    extra=extra_bits()
    shapes=[g.shape[1:] for g in grads]
    hbm=[pl.BlockSpec(memory_space=pl.ANY)]*3
    pair=pl.BlockSpec((SEQ_LEN,128),lambda i:(0,i))
    whole=pl.BlockSpec((SEQ_LEN,128),lambda i:(0,0))
    sd=jax.ShapeDtypeStruct((SEQ_LEN,D),jnp.bfloat16)
    B=jnp.bfloat16
    return pl.pallas_call(functools.partial(bwd_kernel,extra),grid=(H//2,),
        in_specs=[pair]*5+[pl.BlockSpec((2,SEQ_LEN,128),lambda i:(i,0,0)),whole]+hbm,
        out_specs=[pair]*3+hbm,out_shape=[sd]*3+[jax.ShapeDtypeStruct(s,B) for s in shapes],
        scratch_shapes=[pltpu.VMEM((2,SEQ_LEN,256),B),pltpu.VMEM((2,SEQ_LEN,256),B),pltpu.VMEM((SEQ_LEN,256),B),pltpu.VMEM((SEQ_LEN,256),B),pltpu.VMEM((2,SEQ_LEN,128),B),pltpu.VMEM((SEQ_LEN,128),jnp.float32)]+reduce_scratch(REST,shapes,count,extra),
        compiler_params=pltpu.CompilerParams(vmem_limit_bytes=56<<20,collective_id=2,has_side_effects=True),
        cost_estimate=pl.CostEstimate(flops=42_000_000_000,bytes_accessed=15_000_000,transcendentals=12_582_912),
        name="attention_backward")(q,k,v,do,o,aux,kf,*grads)


def per_device(
    tokens,
    segments,
    random_blocks,
    out_grad,
    w_query,
    w_key,
    w_value,
    w_out,
    w_up,
    w_down,
    vectors,
    up_bias,
):
    count = lax.axis_size("fsdp")
    place = lax.axis_index("fsdp")
    width = vectors.shape[1]
    small = jnp.zeros((16, 256), jnp.bfloat16)
    small = small.at[:8, :width].set(vectors).at[8:12, :width].set(up_bias.reshape(4, -1))
    full_query, full_key, full_value, small = gather(
        ("square", "square", "square", "whole"), (w_query, w_key, w_value, small), 0, "gather_first"
    )
    full_query, full_key, full_value = (
        w.reshape(D, D) for w in (full_query, full_key, full_value)
    )
    full_vectors = jnp.moveaxis(small[:, :8, :width], 0, 1).reshape(8, -1)
    full_bias = small[:, 8:12, :width].reshape(-1).astype(jnp.float32)

    vec_float = full_vectors.astype(jnp.float32)
    inputs = tokens.astype(jnp.float32)
    q_low = (jnp.dot(tokens, full_query, preferred_element_type=jnp.float32) + vec_float[0]).astype(
        jnp.bfloat16
    )
    k_low = jnp.dot(tokens, full_key, preferred_element_type=jnp.float32).astype(jnp.bfloat16)
    v_low = (jnp.dot(tokens, full_value, preferred_element_type=jnp.float32) + vec_float[1]).astype(
        jnp.bfloat16
    )
    q_feat, k_feat = mask_features(segments, random_blocks[0])
    mixed_low, aux, full_out, full_up, full_down = attention_forward(
        q_low, k_low, v_low, q_feat, k_feat, (w_out, w_up, w_down)
    )
    full_out, full_up, full_down = (
        w.reshape(-1, w.shape[-1]) for w in (full_out, full_up, full_down)
    )
    attn_out = jnp.dot(mixed_low, full_out, preferred_element_type=jnp.float32) + vec_float[2]
    first_sum = inputs + attn_out
    normed_one, pull_one = jax.vjp(normalize, first_sum, vec_float[3], vec_float[4])
    normed_low = normed_one.astype(jnp.bfloat16)

    up_proj = jnp.dot(normed_low, full_up, preferred_element_type=jnp.float32) + full_bias
    activated, pull_gelu = jax.vjp(gelu_exact, up_proj)
    activated_low = activated.astype(jnp.bfloat16)
    mlp_out = jnp.dot(activated_low, full_down, preferred_element_type=jnp.float32) + vec_float[5]
    second_sum = normed_one + mlp_out
    layer_out, pull_two = jax.vjp(normalize, second_sum, vec_float[6], vec_float[7])
    valid = (segments >= 0).astype(jnp.float32)[:, None]
    squares = jnp.stack(
        [
            jnp.sum(valid * first_sum * first_sum),
            jnp.sum(valid * attn_out * attn_out),
            jnp.sum(valid * mlp_out * mlp_out),
            jnp.sum(valid),
        ]
    )
    d_second, d_gain_two, d_shift_two = pull_two(out_grad.astype(jnp.float32))
    d_mlp = d_second.astype(jnp.bfloat16)

    d_up = pull_gelu(dot_nt(d_mlp, full_down))[0].astype(jnp.bfloat16)
    d_normed = d_second + dot_nt(d_up, full_up)
    d_first, d_gain_one, d_shift_one = pull_one(d_normed)
    d_attn = d_first.astype(jnp.bfloat16)
    d_mixed = dot_nt(d_attn, full_out).astype(jnp.bfloat16)
    rest = [
        g.astype(jnp.bfloat16).reshape(count, -1, g.shape[1])
        for g in (
            dot_tn(mixed_low, d_attn),
            dot_tn(normed_low, d_up),
            dot_tn(activated_low, d_mlp),
        )
    ]
    dq_low, dk_low, dv_low, *rest = attention_backward(
        q_low, k_low, v_low, d_mixed, mixed_low, aux, k_feat, rest
    )
    first = [
        dot_tn(tokens, d).astype(jnp.bfloat16).reshape(count, -1, D)
        for d in (dq_low, dk_low, dv_low)
    ]
    tokens_grad = (
        d_first + dot_nt(dq_low, full_query) + dot_nt(dk_low, full_key) + dot_nt(dv_low, full_value)
    )
    grad_vectors = jnp.stack(
        [
            col_sums(dq_low),
            col_sums(dv_low),
            col_sums(d_attn),
            d_gain_one,
            d_shift_one,
            col_sums(d_mlp),
            d_gain_two,
            d_shift_two,
            jnp.zeros((D,), jnp.float32).at[:4].set(squares),
        ]
    )
    small = jnp.concatenate(
        [grad_vectors, col_sums(d_up).reshape(-1, D), jnp.zeros((3, D), jnp.float32)], 0
    )
    *first, sums = reduce_last(("square", "square", "square"), first, small, 3, "reduce_first")
    grads = [g.astype(jnp.float32) for g in (*first, *rest)]
    rms_values = jnp.sqrt(sums[8, :3] / (sums[8, 3] * D))
    bias_sums = sums[9:13].reshape(count, -1)
    return (
        layer_out.astype(jnp.bfloat16),
        tokens_grad.astype(jnp.bfloat16),
        *grads,
        lax.dynamic_slice_in_dim(sums[:8], place * width, width, 1),
        lax.dynamic_index_in_dim(bias_sums, place, 0, False),
        rms_values,
    )


def solution(mesh):
    in_specs = (
        P(("rep", "fsdp"), None),
        P(("rep", "fsdp")),
        P(("rep", "fsdp"), None, None),
        P(("rep", "fsdp"), None),
        P("fsdp", None),
        P("fsdp", None),
        P("fsdp", None),
        P("fsdp", None),
        P("fsdp", None),
        P("fsdp", None),
        P(None, "fsdp"),
        P("fsdp"),
    )
    out_specs = (
        P(("rep", "fsdp"), None),
        P(("rep", "fsdp"), None),
        P("fsdp", None),
        P("fsdp", None),
        P("fsdp", None),
        P("fsdp", None),
        P("fsdp", None),
        P("fsdp", None),
        P(None, "fsdp"),
        P("fsdp"),
        P(),
    )
    return jax.shard_map(
        per_device, mesh=mesh, in_specs=in_specs, out_specs=out_specs, check_vma=False
    )
```

```python
import functools

import jax
import jax.numpy as jnp
from jax import lax
from jax.experimental import pallas as pl
from jax.experimental.pallas import tpu as pltpu
from jax.sharding import PartitionSpec as P

D = 768
H = 12
DH = 64
BLK = 64
SEQ_LEN = 1024
NB = 16


masked_score = -1e30
layer_eps = 1e-05


def normalize(values, gain, shift):
    centered = values - jnp.mean(values, axis=-1, keepdims=True)
    variance = jnp.mean(centered * centered, axis=-1, keepdims=True)
    return centered * lax.rsqrt(variance + layer_eps) * gain + shift


def gelu_exact(values):
    return jax.nn.gelu(values, approximate=False)


def dot_tn(left, right):
    return lax.dot_general(
        left, right, (((0,), (0,)), ((), ())), preferred_element_type=jnp.float32
    )


def dot_nt(left, right):
    return lax.dot_general(
        left, right, (((1,), (1,)), ((), ())), preferred_element_type=jnp.float32
    )


def col_sums(values):
    return jnp.sum(values.astype(jnp.float32), axis=0)


LOG2E=1.4426950408889634
BIG=1e30

def dot_nn(a,b): return lax.dot_general(a,b,(((1,),(0,)),((),())),preferred_element_type=jnp.float32)

def mask_features(seg_row, random_row):
    blocks = jnp.arange(NB, dtype=jnp.int32)
    near = jnp.abs(blocks[:, None] - blocks[None, :]) <= 1
    first = (blocks[:, None] < 2) | (blocks[None, :] < 2)
    picked = jnp.any(random_row[:, :, None] == blocks[None, None, :], axis=1)
    seen = first | near | picked
    q_block = jnp.where(seen, 0.0, -BIG)
    q_block = jnp.repeat(q_block, BLK, axis=0)
    k_block = jnp.repeat(jnp.eye(NB, dtype=jnp.float32), BLK, axis=0)
    numbers = jnp.arange(-1, 2, dtype=jnp.int32)
    same = seg_row[:, None] == numbers[None, :]
    q_seg = jnp.where(same, 0.0, -BIG)
    k_seg = same.astype(jnp.float32)
    rest = SEQ_LEN, 128 - NB - 3
    ones = jnp.ones((SEQ_LEN, 3), jnp.float32)
    q_feat = jnp.concatenate([q_block, q_seg, jnp.zeros(rest, jnp.float32)], axis=1)
    k_feat = jnp.concatenate([k_block, k_seg, ones, jnp.zeros((SEQ_LEN, 128 - NB - 6), jnp.float32)], axis=1)
    return q_feat.astype(jnp.bfloat16), k_feat.astype(jnp.bfloat16)

MESH = pl.DeviceIdType.MESH


def bit_of(index, bit):
    return lax.rem(lax.div(index, 1 << bit), 2)


def flipped(index, bit):
    return index + (1 - 2 * bit_of(index, bit)) * (1 << bit)


def greet(extra_bits=()):
    rep = lax.axis_index("rep")
    place = lax.axis_index("fsdp")
    count = lax.axis_size("fsdp")
    barrier = pltpu.get_barrier_semaphore()
    bits = (0, 1, 2) + tuple(extra_bits)
    for bit in bits:
        pl.semaphore_signal(
            barrier, inc=1, device_id={"rep": flipped(rep, bit)}, device_id_type=MESH
        )
    for step in range(1, count):
        pl.semaphore_signal(
            barrier,
            inc=1,
            device_id={"fsdp": lax.rem(place + step, count)},
            device_id_type=MESH,
        )
    pl.semaphore_wait(barrier, len(bits) + count - 1)


def region(kind, rows, cols, order, level):
    rep = lax.axis_index("rep")
    core = bit_of(rep, 0)
    first, second = bit_of(rep, order[0]), bit_of(rep, order[1])
    index = (second * 2 + first, second * 2, 0)[level]
    units = (1, 2, 4)[level]
    if kind == "square":
        unit = rows // 4
        return (
            pl.ds(pl.multiple_of(index * unit, unit), units * unit),
            pl.ds(pl.multiple_of(core * (cols // 2), cols // 2), cols // 2),
        )
    if kind == "wide":
        unit = cols // 8
        return (
            pl.ds(0, rows),
            pl.ds(pl.multiple_of((core * 4 + index) * unit, unit), units * unit),
        )
    unit = rows // 8
    return (
        pl.ds(pl.multiple_of((core * 4 + index) * unit, unit), units * unit),
        pl.ds(0, cols),
    )


SPAN = 3


class Gather:
    def __init__(self, kinds, shards, fulls, sems, low, high):
        self.kinds, self.shards, self.fulls, self.low, self.high = kinds, shards, fulls, low, high
        self.send, self.recv, self.local = sems
        self.count = lax.axis_size("fsdp")
        self.rep, self.place = lax.axis_index("rep"), lax.axis_index("fsdp")
        self.blocks = []
        for step in range(1, self.count):
            for a in range(len(kinds)):
                order = (1, 2) if (a + step) % 2 == 0 else (2, 1)
                self.blocks.append((a, step, order))

    def copy(self, k, stage):
        a, step, order = self.blocks[k]
        kind, full = self.kinds[a], self.fulls[a]
        rows, cols = full.shape[1:]
        if stage == 0:
            if kind == "whole":
                src, dst = self.shards[a], full.at[self.place]
            else:
                r, c = region(kind, rows, cols, order, 0)
                src, dst = self.shards[a].at[r, c], full.at[self.place, r, c]
            device = {"fsdp": lax.rem(self.place + step, self.count)}
        else:
            r, c = region(kind, rows, cols, order, stage - 1)
            origin = lax.rem(self.place + self.count - step, self.count)
            src = dst = full.at[origin, r, c]
            device = {"rep": flipped(self.rep, (order + (0,))[stage - 1])}
        return pltpu.make_async_remote_copy(
            src_ref=src,
            dst_ref=dst,
            send_sem=self.send.at[k, stage],
            recv_sem=self.recv.at[k, stage],
            device_id=device,
            device_id_type=MESH,
        )

    def end(self, k):
        return 1 if self.kinds[self.blocks[k][0]] == "whole" else self.high

    def own(self, a):
        return pltpu.make_async_copy(
            self.shards[a], self.fulls[a].at[self.place], self.local.at[a]
        )

    def begin(self):
        for k in range(len(self.blocks)):
            self.copy(k, self.low).start()
        if self.low == 0:
            for a in range(len(self.kinds)):
                self.own(a).start()

    def ticks(self):
        return len(self.blocks) + (self.high - self.low - 1) * SPAN

    def tick(self, t):
        for stage in range(self.low, self.high):
            k = t - (stage - self.low) * SPAN
            if 0 <= k < len(self.blocks) and stage < self.end(k):
                self.copy(k, stage).wait_recv()
                if stage + 1 < self.end(k):
                    self.copy(k, stage + 1).start()

    def finish(self):
        for k in range(len(self.blocks)):
            for stage in range(self.low, self.end(k)):
                self.copy(k, stage).wait_send()
        if self.low == 0:
            for a in range(len(self.kinds)):
                self.own(a).wait()


def gather_sems(kinds, count):
    blocks = len(kinds) * (count - 1)
    return [
        pltpu.SemaphoreType.DMA((blocks, 4)),
        pltpu.SemaphoreType.DMA((blocks, 4)),
        pltpu.SemaphoreType.DMA((len(kinds),)),
    ]


def whole_like(shards):
    return [jax.ShapeDtypeStruct((lax.axis_size("fsdp"), *s.shape), s.dtype) for s in shards]


def run_all(jobs, delays, extra=()):
    greet(extra)
    for t in range(max(job.ticks() + delay for job, delay in zip(jobs, delays))):
        for job, delay in zip(jobs, delays):
            if t == delay:
                job.begin()
            if 0 <= t - delay < job.ticks():
                job.tick(t - delay)
    for job in jobs:
        job.finish()


FIRST = ("square", "square", "square", "whole")
REST = ("square", "wide")


def gather_kernel(*refs):
    n, m = len(FIRST), len(REST)
    shards, fulls, sems = refs[: n + m], refs[n + m : 2 * (n + m)], refs[2 * (n + m) :]
    run_all(
        [
            Gather(FIRST, shards[:n], fulls[:n], sems[:3], 0, 4),
            Gather(REST, shards[n:], fulls[n:], sems[3:], 0, 1),
        ],
        (0, 14),
    )


def gather_first(shards):
    count = lax.axis_size("fsdp")
    return pl.pallas_call(
        gather_kernel,
        in_specs=[pl.BlockSpec(memory_space=pltpu.VMEM)] * len(shards),
        out_specs=[pl.BlockSpec(memory_space=pl.ANY)] * len(shards),
        out_shape=whole_like(shards),
        scratch_shapes=gather_sems(FIRST, count) + gather_sems(REST, count),
        compiler_params=pltpu.CompilerParams(
            collective_id=0, has_side_effects=True, vmem_limit_bytes=24 << 20
        ),
        name="gather_first",
    )(*shards)


LAG = 3


def half_shape(kind, rows, cols):
    return (rows // 2, cols) if kind == "tall" else (rows, cols // 2)


def part_shape(kind, rows, cols, level):
    r, c = half_shape(kind, rows, cols)
    cut = (4, 2, 1)[level]
    return (r, c // cut) if kind == "wide" else (r // cut, c)


def part(kind, rows, cols, first, second, level):
    index = (second * 2 + first, second * 2, 0)[level]
    units = (1, 2, 4)[level]
    r, c = half_shape(kind, rows, cols)
    if kind == "wide":
        unit = c // 4
        return pl.ds(0, r), pl.ds(pl.multiple_of(index * unit, unit), units * unit)
    unit = r // 4
    return pl.ds(pl.multiple_of(index * unit, unit), units * unit), pl.ds(0, c)


def half(kind, rows, cols, core):
    r, c = half_shape(kind, rows, cols)
    if kind == "tall":
        return pl.ds(pl.multiple_of(core * r, r), r), pl.ds(0, c)
    return pl.ds(0, r), pl.ds(pl.multiple_of(core * c, c), c)


def add_into(target, where, values):
    rows, cols = where
    chunk = 16
    total, base = rows.size, rows.start

    @pl.loop(0, total // chunk)
    def _(i):
        at = pl.ds(pl.multiple_of(base + i * chunk, chunk), chunk)
        more = values[pl.ds(pl.multiple_of(i * chunk, chunk), chunk), :]
        kept = target[at, cols]
        target[at, cols] = (kept.astype(jnp.float32) + more.astype(jnp.float32)).astype(
            target.dtype
        )


class Reduce:
    def __init__(self, kinds, grads, results, scratch, extra, cuts):
        self.kinds, self.grads, self.results, self.extra = kinds, grads, results, extra
        self.cuts = cuts
        n = len(kinds)
        self.acc, self.got0, self.got1, self.got2, self.got3 = (
            scratch[i * n : (i + 1) * n] for i in range(5)
        )
        self.outs, rest = scratch[5 * n : 6 * n], scratch[6 * n :]
        if extra:
            self.gotx, rest = rest[:n], rest[n:]
        self.load, self.send, self.recv, self.gsend, self.grecv, self.store = rest[:6]
        self.count = lax.axis_size("fsdp")
        self.rep, self.place = lax.axis_index("rep"), lax.axis_index("fsdp")
        self.blocks = [
            (a, step) for step in list(range(1, self.count)) + [0] for a in range(n)
        ]

    def order(self, a):
        return (1, 2) if a % 2 == 0 else (2, 1)

    def bits(self, a):
        order = self.order(a)
        return bit_of(self.rep, order[0]), bit_of(self.rep, order[1])

    def shape(self, a):
        return self.cuts[a][3:]

    def source(self, a, step, core):
        g, row, col, rows, cols = self.cuts[a]
        r, c = half(self.kinds[a], rows, cols, core)
        if row:
            r = pl.ds(pl.multiple_of(r.start + row, 16), r.size)
        if col:
            c = pl.ds(pl.multiple_of(c.start + col, 128), c.size)
        return self.grads[g].at[lax.rem(self.place + step, self.count), r, c]

    def mine(self, k):
        a, step = self.blocks[k]
        return pltpu.make_async_copy(
            self.source(a, step, bit_of(self.rep, 0)), self.acc[a].at[step], self.load.at[k]
        )

    def copy(self, k, stage):
        a, step = self.blocks[k]
        kind, shape = self.kinds[a], self.shape(a)
        first, second = self.bits(a)
        order = self.order(a)
        if stage == 0:
            src, dst = self.source(a, step, 1 - bit_of(self.rep, 0)), self.got0[a].at[step]
            device = {"rep": flipped(self.rep, 0)}
        elif stage == 1:
            r, c = part(kind, *shape, first, 1 - second, 1)
            src, dst = self.acc[a].at[step, r, c], self.got1[a].at[step]
            device = {"rep": flipped(self.rep, order[1])}
        elif stage == 2:
            r, c = part(kind, *shape, 1 - first, second, 0)
            src, dst = self.acc[a].at[step, r, c], self.got2[a].at[step]
            device = {"rep": flipped(self.rep, order[0])}
        else:
            r, c = part(kind, *shape, first, second, 0)
            src, dst = self.acc[a].at[step, r, c], self.got3[a].at[step - 1]
            device = {"fsdp": lax.rem(self.place + step, self.count)}
        return pltpu.make_async_remote_copy(
            src_ref=src,
            dst_ref=dst,
            send_sem=self.send.at[k, stage],
            recv_sem=self.recv.at[k, stage],
            device_id=device,
            device_id_type=MESH,
        )

    def whole(self, a, level):
        kind, (rows, cols) = self.kinds[a], self.shape(a)
        return region(kind, rows, cols, self.order(a), level)

    def back(self, a, level):
        r, c = self.whole(a, level)
        ref = self.outs[a].at[r, c]
        bit = (self.order(a) + (0,))[level]
        return pltpu.make_async_remote_copy(
            src_ref=ref,
            dst_ref=ref,
            send_sem=self.gsend.at[a, level],
            recv_sem=self.grecv.at[a, level],
            device_id={"rep": flipped(self.rep, bit)},
            device_id_type=MESH,
        )

    def more(self, a, i):
        r, c = self.whole(a, 0)
        return pltpu.make_async_remote_copy(
            src_ref=self.outs[a].at[r, c],
            dst_ref=self.gotx[a].at[i],
            send_sem=self.gsend.at[a, 3 + i],
            recv_sem=self.grecv.at[a, 3 + i],
            device_id={"rep": flipped(self.rep, self.extra[i])},
            device_id_type=MESH,
        )

    def begin(self):
        for k in range(len(self.blocks)):
            self.copy(k, 0).start()
            self.mine(k).start()

    def absorb(self, k, stage):
        a, step = self.blocks[k]
        kind, shape = self.kinds[a], self.shape(a)
        first, second = self.bits(a)
        got = (self.got0, self.got1, self.got2)[stage][a].at[step]
        where = part(kind, *shape, first, second, 2 - stage)
        if stage == 0:
            self.mine(k).wait()
        self.copy(k, stage).wait_recv()
        add_into(self.acc[a].at[step], where, got)
        if stage < 2 or step:
            self.copy(k, stage + 1).start()

    def total(self, a):
        kind, shape = self.kinds[a], self.shape(a)
        first, second = self.bits(a)
        for step in range(1, self.count):
            self.copy(self.blocks.index((a, step)), 3).wait_recv()
        rows, cols = part(kind, *shape, first, second, 0)
        to_rows, to_cols = self.whole(a, 0)
        chunk = 16

        @pl.loop(0, rows.size // chunk)
        def _(i):
            at = pl.ds(pl.multiple_of(rows.start + i * chunk, chunk), chunk)
            total = self.acc[a][0, at, cols].astype(jnp.float32)
            near = pl.ds(pl.multiple_of(i * chunk, chunk), chunk)
            for step in range(self.count - 1):
                total = total + self.got3[a][step, near, :].astype(jnp.float32)
            to = pl.ds(pl.multiple_of(to_rows.start + i * chunk, chunk), chunk)
            self.outs[a][to, to_cols] = total.astype(jnp.bfloat16)

        for i in range(len(self.extra)):
            copy = self.more(a, i)
            copy.start()
            copy.wait()
            add_into(self.outs[a], self.whole(a, 0), self.gotx[a].at[i])
        self.back(a, 0).start()

    def put(self, a):
        g, row, col, rows, cols = self.cuts[a]
        to = self.results[g].at[pl.ds(row, rows), pl.ds(col, cols)]
        return pltpu.make_async_copy(self.outs[a], to, self.store.at[a])

    def ticks(self):
        return len(self.blocks) + 6 * LAG

    def tick(self, t):
        blocks = len(self.blocks)
        for stage in range(3):
            k = t - stage * LAG
            if 0 <= k < blocks:
                self.absorb(k, stage)
        for a in range(len(self.kinds)):
            late = t - self.blocks.index((a, 0)) - 3 * LAG
            if late == 0:
                self.total(a)
            elif late in (LAG, 2 * LAG, 3 * LAG):
                level = late // LAG
                self.back(a, level - 1).wait_recv()
                if level < 3:
                    self.back(a, level).start()
                else:
                    self.put(a).start()

    def finish(self):
        for k, (a, step) in enumerate(self.blocks):
            for stage in range(4 if step else 3):
                self.copy(k, stage).wait_send()
        for a in range(len(self.kinds)):
            for level in range(3):
                self.back(a, level).wait_send()
            self.put(a).wait()


class Fold(Reduce):
    def __init__(self, kinds, grads, units, scratch, cuts):
        self.kinds, self.grads, self.units, self.cuts = kinds, grads, units, cuts
        n = len(kinds)
        self.acc, self.got0, self.got1, self.got2 = (scratch[i * n : (i + 1) * n] for i in range(4))
        self.load, self.send, self.recv, self.store = scratch[4 * n :]
        self.count = lax.axis_size("fsdp")
        self.rep, self.place = lax.axis_index("rep"), lax.axis_index("fsdp")
        self.blocks = [(a, step) for step in [*range(1, self.count), 0] for a in range(n)]

    def keep(self, k):
        a, step = self.blocks[k]
        r, c = part(self.kinds[a], *self.shape(a), *self.bits(a), 0)
        return pltpu.make_async_copy(
            self.acc[a].at[step, r, c], self.units[a].at[step], self.store.at[k]
        )

    def absorb(self, k, stage):
        a, step = self.blocks[k]
        got = (self.got0, self.got1, self.got2)[stage][a].at[step]
        if stage == 0:
            self.mine(k).wait()
        self.copy(k, stage).wait_recv()
        where = part(self.kinds[a], *self.shape(a), *self.bits(a), 2 - stage)
        add_into(self.acc[a].at[step], where, got)
        (self.copy(k, stage + 1) if stage < 2 else self.keep(k)).start()

    def ticks(self):
        return len(self.blocks) + 2 * LAG

    def tick(self, t):
        for stage in range(3):
            k = t - stage * LAG
            if 0 <= k < len(self.blocks):
                self.absorb(k, stage)

    def finish(self):
        for k in range(len(self.blocks)):
            for stage in range(3):
                self.copy(k, stage).wait_send()
            self.keep(k).wait()


class Spread(Reduce):
    def __init__(self, kinds, units, results, scratch, extra, cuts):
        self.kinds, self.units, self.results = kinds, units, results
        self.extra, self.cuts = extra, cuts
        n = len(kinds)
        self.own, self.got3, self.outs = (scratch[i * n : (i + 1) * n] for i in range(3))
        rest = scratch[3 * n :]
        if extra:
            self.gotx, rest = rest[:n], rest[n:]
        self.load, self.send, self.recv, self.gsend, self.grecv, self.store = rest
        self.count = lax.axis_size("fsdp")
        self.rep, self.place = lax.axis_index("rep"), lax.axis_index("fsdp")

    def line(self, a, step):
        return pltpu.make_async_remote_copy(
            src_ref=self.units[a].at[step],
            dst_ref=self.got3[a].at[step - 1],
            send_sem=self.send.at[a, step],
            recv_sem=self.recv.at[a, step],
            device_id={"fsdp": lax.rem(self.place + step, self.count)},
            device_id_type=MESH,
        )

    def near(self, a):
        return pltpu.make_async_copy(self.units[a].at[0], self.own[a], self.load.at[a])

    def begin(self):
        for a in range(len(self.kinds)):
            for step in range(1, self.count):
                self.line(a, step).start()
            self.near(a).start()

    def total(self, a):
        self.near(a).wait()
        for step in range(1, self.count):
            self.line(a, step).wait_recv()
        to_rows, to_cols = self.whole(a, 0)
        chunk = 16

        @pl.loop(0, to_rows.size // chunk)
        def _(i):
            near = pl.ds(pl.multiple_of(i * chunk, chunk), chunk)
            total = self.own[a][near, :].astype(jnp.float32)
            for step in range(self.count - 1):
                total = total + self.got3[a][step, near, :].astype(jnp.float32)
            to = pl.ds(pl.multiple_of(to_rows.start + i * chunk, chunk), chunk)
            self.outs[a][to, to_cols] = total.astype(jnp.bfloat16)

        for i in range(len(self.extra)):
            copy = self.more(a, i)
            copy.start()
            copy.wait()
            add_into(self.outs[a], self.whole(a, 0), self.gotx[a].at[i])
        self.back(a, 0).start()

    def ticks(self):
        return 4 * len(self.kinds)

    def tick(self, t):
        level, a = divmod(t, len(self.kinds))
        if level == 0:
            self.total(a)
            return
        self.back(a, level - 1).wait_recv()
        (self.back(a, level) if level < 3 else self.put(a)).start()

    def finish(self):
        for a in range(len(self.kinds)):
            for step in range(1, self.count):
                self.line(a, step).wait_send()
            for level in range(3):
                self.back(a, level).wait_send()
            self.put(a).wait()


def units_like(kinds, cuts):
    count = lax.axis_size("fsdp")
    return [
        jax.ShapeDtypeStruct((count, *part_shape(k, *c[3:], 0)), jnp.bfloat16)
        for k, c in zip(kinds, cuts)
    ]


def fold_scratch(kinds, cuts, count):
    B = jnp.bfloat16
    sizes = [(k, *c[3:]) for k, c in zip(kinds, cuts)]
    blocks = len(kinds) * count
    dma = pltpu.SemaphoreType.DMA
    return (
        [pltpu.VMEM((count, *half_shape(*s)), B) for s in sizes] * 2
        + [pltpu.VMEM((count, *part_shape(*s, 1)), B) for s in sizes]
        + [pltpu.VMEM((count, *part_shape(*s, 0)), B) for s in sizes]
        + [dma((blocks,)), dma((blocks, 3)), dma((blocks, 3)), dma((blocks,))]
    )


def spread_scratch(kinds, cuts, count, extra):
    B = jnp.bfloat16
    sizes = [(k, *c[3:]) for k, c in zip(kinds, cuts)]
    n = len(kinds)
    dma = pltpu.SemaphoreType.DMA
    made = [pltpu.VMEM(part_shape(*s, 0), B) for s in sizes]
    made += [pltpu.VMEM((count - 1, *part_shape(*s, 0)), B) for s in sizes]
    made += [pltpu.VMEM(s[1:], B) for s in sizes]
    if extra:
        made += [pltpu.VMEM((len(extra), *part_shape(*s, 0)), B) for s in sizes]
    backs = 3 + len(extra)
    return made + [dma((n,)), dma((n, count)), dma((n, count)), dma((n, backs)), dma((n, backs)), dma((n,))]


class Sums:
    def __init__(self, source, result, held, got, send, recv, extra):
        self.source, self.result, self.held, self.got = source, result, held, got
        self.send, self.recv = send, recv
        self.bits = (0, 1, 2) + tuple(extra)
        self.count = lax.axis_size("fsdp")
        self.rep, self.place = lax.axis_index("rep"), lax.axis_index("fsdp")

    def copy(self, i):
        level = min(i, len(self.bits))
        src = self.source if level == 0 else self.held.at[level - 1]
        if i < len(self.bits):
            device = {"rep": flipped(self.rep, self.bits[i])}
        else:
            step = i - len(self.bits) + 1
            device = {"fsdp": lax.rem(self.place + step, self.count)}
        return pltpu.make_async_remote_copy(
            src_ref=src,
            dst_ref=self.got.at[i],
            send_sem=self.send.at[i],
            recv_sem=self.recv.at[i],
            device_id=device,
            device_id_type=MESH,
        )

    def begin(self):
        self.copy(0).start()

    def ticks(self):
        return len(self.bits) + 1

    def tick(self, t):
        bits = len(self.bits)
        if t < bits:
            self.copy(t).wait_recv()
            before = self.source[...] if t == 0 else self.held[t - 1]
            self.held[t] = before + self.got[t]
            for i in range(t + 1, t + 2 if t + 1 < bits else bits + self.count - 1):
                self.copy(i).start()
        elif t == bits:
            total = self.held[bits - 1]
            for i in range(bits, bits + self.count - 1):
                self.copy(i).wait_recv()
                total = total + self.got[i]
            self.result[...] = total

    def finish(self):
        for i in range(len(self.bits) + self.count - 1):
            self.copy(i).wait_send()


def reduce_scratch(kinds, shapes, count, extra):
    B = jnp.bfloat16
    sizes = [(k, *s) for k, s in zip(kinds, shapes)]
    made = [pltpu.VMEM((count, *half_shape(*s)), B) for s in sizes]
    made += [pltpu.VMEM((count, *half_shape(*s)), B) for s in sizes]
    made += [pltpu.VMEM((count, *part_shape(*s, 1)), B) for s in sizes]
    made += [pltpu.VMEM((count, *part_shape(*s, 0)), B) for s in sizes]
    made += [pltpu.VMEM((count - 1, *part_shape(*s, 0)), B) for s in sizes]
    made += [pltpu.VMEM(s, B) for s in shapes]
    if extra:
        made += [pltpu.VMEM((len(extra), *part_shape(*s, 0)), B) for s in sizes]
    n = len(kinds)
    dma = pltpu.SemaphoreType.DMA
    made += [dma((n * count,)), dma((n * count, 4)), dma((n * count, 4))]
    made += [dma((n, 3 + len(extra))), dma((n, 3 + len(extra))), dma((n,))]
    return made


def sums_scratch(shape, count, extra):
    bits = 3 + len(extra)
    dma = pltpu.SemaphoreType.DMA
    return [
        pltpu.VMEM((bits, *shape), jnp.float32),
        pltpu.VMEM((bits + count - 1, *shape), jnp.float32),
        dma((bits + count - 1,)),
        dma((bits + count - 1,)),
    ]


def extra_bits():
    found, bit = [], 3
    while (1 << bit) < lax.axis_size("rep"):
        found.append(bit)
        bit += 1
    return tuple(found)


REST_BACK = ("square", "wide", "wide")
REST_CUTS = ((0, 0, 0, D // 4, D), (1, 0, 0, D // 8, 4 * D), (1, D // 8, 0, D // 8, 4 * D))
TALL = ("tall", "tall")
TALL_CUTS = ((0, 0, 0, D, D // 2), (0, 0, D // 2, D, D // 2))
LAST = ("square", "square", "square")


def reduce_kernel(extra, spread_size, *refs):
    n, m, p = len(LAST), len(REST_BACK), len(REST)
    grads, units, small = refs[:n], refs[n : n + m], refs[n + m]
    outs = refs[n + m + 1 : n + m + 1 + n + p]
    total, scratch = refs[n + m + 1 + n + p], refs[n + m + 2 + n + p :]
    cuts = [(i, 0, 0, *g.shape[1:]) for i, g in enumerate(grads)]
    run_all(
        [
            Reduce(LAST, grads, outs[:n], scratch[spread_size:-4], extra, cuts),
            Spread(REST_BACK, units, outs[n:], scratch[:spread_size], extra, REST_CUTS),
            Sums(small, total, *scratch[-4:], extra),
        ],
        (0, 0, 0),
        extra,
    )


def reduce_last(grads, units, shards, small):
    count = lax.axis_size("fsdp")
    extra = extra_bits()
    shapes = [g.shape[1:] for g in grads]
    vmem = pl.BlockSpec(memory_space=pltpu.VMEM)
    hbm = pl.BlockSpec(memory_space=pl.ANY)
    spread = spread_scratch(REST_BACK, REST_CUTS, count, extra)
    return pl.pallas_call(
        functools.partial(reduce_kernel, extra, len(spread)),
        in_specs=[hbm] * (len(grads) + len(units)) + [vmem],
        out_specs=[hbm] * (len(grads) + len(shards)) + [vmem],
        out_shape=[jax.ShapeDtypeStruct(s, jnp.bfloat16) for s in shapes + shards]
        + [jax.ShapeDtypeStruct(small.shape, jnp.float32)],
        scratch_shapes=spread
        + reduce_scratch(LAST, shapes, count, extra)
        + sums_scratch(small.shape, count, extra),
        compiler_params=pltpu.CompilerParams(
            collective_id=3, has_side_effects=True, vmem_limit_bytes=48 << 20
        ),
        name="reduce_last",
    )(*grads, *units, small)


TQ = 256
POINTS = 12


def host(jobs, paces, half, extra=()):
    for point in range(half, POINTS, 2):
        due = [
            (job, i)
            for job, (first, pace) in zip(jobs, paces)
            for i in range(job.ticks())
            if int(first + pace * i) == point
        ]
        if due or point == 0:

            @pl.when(pl.program_id(0) == point // 2)
            def _(due=due, point=point):
                if point == 0:
                    greet(extra)
                    for job in jobs:
                        job.begin()
                for job, i in due:
                    job.tick(i)


def close(jobs, paces):
    left = [
        (i, j)
        for j, (job, (first, pace)) in enumerate(zip(jobs, paces))
        for i in range(job.ticks())
        if int(first + pace * i) >= POINTS
    ]

    @pl.when(pl.program_id(0) == POINTS // 2 - 1)
    def _():
        for i, j in sorted(left):
            jobs[j].tick(i)
        for job in jobs:
            job.finish()


FORWARD_PACES = ((2, 0.75), (12, 1))
WIDEN_PACES = ((3, 0.9),)
NARROW_PACES = ((2.5, 0.65),)
BACKWARD_PACES = ((2, 0.5), (5, 0.75))


def fwd_kernel(q_ref,k_ref,v_ref,qf_ref,kf_ref,s2,i0,i1,o_ref,aux_ref,f0,f1,f2,qc,kc,vm,*sems):
    jobs = [
        Gather(REST, None, (f0, f1), sems[:3], 1, 4),
        Gather(("tall",), (s2,), (f2,), sems[3:], 0, 1),
    ]
    host(jobs, FORWARD_PACES, 0)
    lane = lax.broadcasted_iota(jnp.int32,(SEQ_LEN,128),1)
    kc[:,:128]=k_ref[...]
    kc[:,128:]=kf_ref[...]
    q=q_ref[...]*jnp.bfloat16(0.125)
    v=v_ref[...]
    zero=jnp.zeros_like(q)
    for h in range(2):
        sel = (lane<64) if h==0 else (lane>=64)
        qc[h,:,:128]=jnp.where(sel,q,zero)
        qc[h,:,128:]=qf_ref[...]
        vm[h]=jnp.where(sel,v,zero)
    for t in range(SEQ_LEN//TQ):
        if t==2: host(jobs, FORWARD_PACES, 1)
        rows=pl.ds(t*TQ,TQ)
        total=None
        for h in range(2):
            s=dot_nt(qc[h,rows,:],kc[...])
            m=jnp.max(s,axis=1,keepdims=True)
            p=jnp.exp2((s-m)*LOG2E)
            l=jnp.sum(p,axis=1,keepdims=True)
            o=dot_nn(p.astype(jnp.bfloat16),vm[h])*(1.0/l)
            total=o if total is None else total+o
            lse=-(m+jnp.log(l))
            hi=lse.astype(jnp.bfloat16).astype(jnp.float32)
            r=lse-hi
            mid=r.astype(jnp.bfloat16).astype(jnp.float32)
            lo=r-mid
            ln=lax.broadcasted_iota(jnp.int32,(TQ,128),1)
            a=jnp.where(ln==19,hi,jnp.where(ln==20,mid,jnp.where(ln==21,lo,qf_ref[rows,:].astype(jnp.float32))))
            aux_ref[h,rows,:]=a.astype(jnp.bfloat16)
        o_ref[rows,:]=total.astype(jnp.bfloat16)
    close(jobs, FORWARD_PACES)

def attention_forward(q,k,v,qf,kf,w_down,full_out,full_up):
    count=lax.axis_size("fsdp")
    pair=pl.BlockSpec((SEQ_LEN,128),lambda i:(0,i))
    whole=pl.BlockSpec((SEQ_LEN,128),lambda i:(0,0))
    hbm=pl.BlockSpec(memory_space=pl.ANY)
    B=jnp.bfloat16
    same=[jax.ShapeDtypeStruct(w.shape,w.dtype) for w in (full_out,full_up)]
    return pl.pallas_call(fwd_kernel,grid=(H//2,),
        in_specs=[pair,pair,pair,whole,whole,pl.BlockSpec(memory_space=pltpu.VMEM),hbm,hbm],
        out_specs=[pair,pl.BlockSpec((2,SEQ_LEN,128),lambda i:(i,0,0)),hbm,hbm,hbm],
        out_shape=[jax.ShapeDtypeStruct((SEQ_LEN,D),B),jax.ShapeDtypeStruct((H,SEQ_LEN,128),B)]+same+whole_like([w_down]),
        input_output_aliases={6:2,7:3},
        scratch_shapes=[pltpu.VMEM((2,SEQ_LEN,256),B),pltpu.VMEM((SEQ_LEN,256),B),pltpu.VMEM((2,SEQ_LEN,128),B)]+gather_sems(REST,count)+gather_sems(("tall",),count),
        compiler_params=pltpu.CompilerParams(vmem_limit_bytes=48<<20,collective_id=1,has_side_effects=True),
        cost_estimate=pl.CostEstimate(flops=30_000_000_000,bytes_accessed=10_000_000,transcendentals=12_582_912),
        name="attention_forward")(q,k,v,qf,kf,w_down,full_out,full_up)

TK=256
def bwd_kernel(extra,q_ref,k_ref,v_ref,do_ref,o_ref,aux_ref,kf_ref,g0,g1,v0,v1,dq_ref,dk_ref,dv_ref,u0,u1,u2,r0,qc,dc,kc,vc,km,dqa,*scratch):
    jobs = [
        Fold(REST_BACK, (g0, g1), (u0, u1, u2), scratch[:16], REST_CUTS),
        Spread(TALL, (v0, v1), (r0,), scratch[16:], extra, TALL_CUTS),
    ]
    host(jobs, BACKWARD_PACES, 0, extra)
    lane = lax.broadcasted_iota(jnp.int32,(SEQ_LEN,128),1)
    kc[:,:128]=k_ref[...]
    kc[:,128:]=kf_ref[...]
    vc[:,:128]=v_ref[...]
    vc[:,128:]=kf_ref[...]
    q=q_ref[...]*jnp.bfloat16(0.125)
    k=k_ref[...]*jnp.bfloat16(0.125)
    do=do_ref[...]
    prod=do.astype(jnp.float32)*o_ref[...].astype(jnp.float32)
    zero=jnp.zeros_like(q)
    for h in range(2):
        sel = (lane<64) if h==0 else (lane>=64)
        qc[h,:,:128]=jnp.where(sel,q,zero)
        qc[h,:,128:]=aux_ref[h]
        km[h]=jnp.where(sel,k,zero)
        dc[h,:,:128]=jnp.where(sel,do,zero)
        delta=-jnp.sum(jnp.where(sel,prod,0.0),axis=1,keepdims=True)
        hi=delta.astype(jnp.bfloat16).astype(jnp.float32)
        lo=delta-hi
        dc[h,:,128:]=jnp.where(lane==19,hi,jnp.where(lane==20,lo,0.0)).astype(jnp.bfloat16)
    for t in range(SEQ_LEN//TK):
        if t==2: host(jobs, BACKWARD_PACES, 1, extra)
        rows=pl.ds(t*TK,TK)
        dv=None;dk=None;dq=None
        for h in range(2):
            s=dot_nt(kc[rows,:],qc[h])
            p=jnp.exp2(s*LOG2E)
            dp=dot_nt(vc[rows,:],dc[h])
            ds=(p*dp).astype(jnp.bfloat16)
            pb=p.astype(jnp.bfloat16)
            dvh=dot_nn(pb,dc[h,:,:128])
            dkh=dot_nn(ds,qc[h,:,:128])
            dqh=dot_tn(ds,km[h,rows,:])
            dv=dvh if dv is None else dv+dvh
            dk=dkh if dk is None else dk+dkh
            dq=dqh if dq is None else dq+dqh
        dk_ref[rows,:]=dk.astype(jnp.bfloat16)
        dv_ref[rows,:]=dv.astype(jnp.bfloat16)
        if t==0: dqa[...]=dq
        else: dqa[...]+=dq
    dq_ref[...]=dqa[...].astype(jnp.bfloat16)
    close(jobs, BACKWARD_PACES)

def attention_backward(q,k,v,do,o,aux,kf,grads,units,shard):
    count=lax.axis_size("fsdp")
    extra=extra_bits()
    pair=pl.BlockSpec((SEQ_LEN,128),lambda i:(0,i))
    whole=pl.BlockSpec((SEQ_LEN,128),lambda i:(0,0))
    hbm=pl.BlockSpec(memory_space=pl.ANY)
    sd=jax.ShapeDtypeStruct((SEQ_LEN,D),jnp.bfloat16)
    B=jnp.bfloat16
    return pl.pallas_call(functools.partial(bwd_kernel,extra),grid=(H//2,),
        in_specs=[pair]*5+[pl.BlockSpec((2,SEQ_LEN,128),lambda i:(i,0,0)),whole]+[hbm]*4,
        out_specs=[pair]*3+[hbm]*4,
        out_shape=[sd]*3+units_like(REST_BACK,REST_CUTS)+[jax.ShapeDtypeStruct(shard,B)],
        scratch_shapes=[pltpu.VMEM((2,SEQ_LEN,256),B),pltpu.VMEM((2,SEQ_LEN,256),B),pltpu.VMEM((SEQ_LEN,256),B),pltpu.VMEM((SEQ_LEN,256),B),pltpu.VMEM((2,SEQ_LEN,128),B),pltpu.VMEM((SEQ_LEN,128),jnp.float32)]
            +fold_scratch(REST_BACK,REST_CUTS,count)+spread_scratch(TALL,TALL_CUTS,count,extra),
        compiler_params=pltpu.CompilerParams(vmem_limit_bytes=56<<20,collective_id=2,has_side_effects=True),
        cost_estimate=pl.CostEstimate(flops=42_000_000_000,bytes_accessed=15_000_000,transcendentals=12_582_912),
        name="attention_backward")(q,k,v,do,o,aux,kf,*grads,*units)


FF_BLOCK = 512


def normal_cdf(u, bell):
    t = 1.0 / (1.0 + 0.3535533905932738 * jnp.abs(u))
    fit = 0.17087277
    for c in (
        -0.82215223,
        1.48851587,
        -1.13520398,
        0.27886807,
        -0.18628806,
        0.09678418,
        0.37409196,
        1.00002368,
        -1.26551223,
    ):
        fit = fit * t + c
    tail = 0.5 * t * jnp.exp2(fit * LOG2E + bell)
    return jnp.where(u < 0.0, tail, 1.0 - tail)


def widen_kernel(x_ref, w_ref, b_ref, i0, act_ref, slope_ref, f0, *sems):
    jobs = [Gather(("tall",), None, (f0,), sems, 1, 4)]
    host(jobs, WIDEN_PACES, 0)
    for t in range(4):
        if t == 2:
            host(jobs, WIDEN_PACES, 1)
        rows = pl.ds(t * 256, 256)
        u = dot_nn(x_ref[rows, :], w_ref[...]) + b_ref[...]
        bell = u * u * (-0.5 * LOG2E)
        cdf = normal_cdf(u, bell)
        act_ref[rows, :] = (u * cdf).astype(jnp.bfloat16)
        slope_ref[rows, :] = (cdf + u * (0.3989422804014327 * jnp.exp2(bell))).astype(jnp.bfloat16)
    close(jobs, WIDEN_PACES)


def widen(x, w, bias, full_down):
    count = lax.axis_size("fsdp")
    rows, ff = x.shape[0], w.shape[1]
    block = pl.BlockSpec((rows, FF_BLOCK), lambda i: (0, i))
    out = jax.ShapeDtypeStruct((rows, ff), jnp.bfloat16)
    return pl.pallas_call(
        widen_kernel,
        grid=(ff // FF_BLOCK,),
        in_specs=[
            pl.BlockSpec((rows, D), lambda i: (0, 0)),
            pl.BlockSpec((D, FF_BLOCK), lambda i: (0, i)),
            pl.BlockSpec((1, FF_BLOCK), lambda i: (0, i)),
            pl.BlockSpec(memory_space=pl.ANY),
        ],
        input_output_aliases={3: 2},
        out_specs=[block, block, pl.BlockSpec(memory_space=pl.ANY)],
        out_shape=[out, out, jax.ShapeDtypeStruct(full_down.shape, full_down.dtype)],
        scratch_shapes=gather_sems(("tall",), count),
        compiler_params=pltpu.CompilerParams(
            vmem_limit_bytes=40 << 20, collective_id=4, has_side_effects=True
        ),
        name="widen",
    )(x, w, bias[None], full_down)


def narrow_back_kernel(
    dm_ref, x_ref, slope_ref, wd_ref, wu_ref, g0, dx_ref, gu_ref, sum_ref, u0, u1, acc, du, *scratch
):
    jobs = [Fold(TALL, (g0,), (u0, u1), scratch, TALL_CUTS)]
    host(jobs, NARROW_PACES, 0)
    sums = jnp.zeros((1, FF_BLOCK), jnp.float32)
    for t in range(4):
        if t == 2:
            host(jobs, NARROW_PACES, 1)
        rows = pl.ds(t * 256, 256)
        d = dot_nt(dm_ref[rows, :], wd_ref[...]) * slope_ref[rows, :].astype(jnp.float32)
        low = d.astype(jnp.bfloat16)
        du[rows, :] = low
        sums = sums + jnp.sum(low.astype(jnp.float32), axis=0, keepdims=True)
        more = dot_nt(low, wu_ref[...])

        @pl.when(pl.program_id(0) == 0)
        def _():
            acc[rows, :] = more

        @pl.when(pl.program_id(0) > 0)
        def _():
            acc[rows, :] += more

    gu_ref[...] = dot_tn(x_ref[...], du[...]).astype(jnp.bfloat16)
    sum_ref[...] = sums

    @pl.when(pl.program_id(0) == pl.num_programs(0) - 1)
    def _():
        dx_ref[...] = acc[...]

    close(jobs, NARROW_PACES)


def narrow_back(d_mlp, x, slope, w_down, w_up, grad):
    count = lax.axis_size("fsdp")
    rows, ff = slope.shape
    whole = pl.BlockSpec((rows, D), lambda i: (0, 0))
    cols = pl.BlockSpec((D, FF_BLOCK), lambda i: (0, i))
    hbm = pl.BlockSpec(memory_space=pl.ANY)
    return pl.pallas_call(
        narrow_back_kernel,
        grid=(ff // FF_BLOCK,),
        in_specs=[
            whole,
            whole,
            pl.BlockSpec((rows, FF_BLOCK), lambda i: (0, i)),
            pl.BlockSpec((FF_BLOCK, D), lambda i: (i, 0)),
            cols,
            hbm,
        ],
        out_specs=[whole, cols, pl.BlockSpec((1, FF_BLOCK), lambda i: (0, i)), hbm, hbm],
        out_shape=[
            jax.ShapeDtypeStruct((rows, D), jnp.float32),
            jax.ShapeDtypeStruct((D, ff), jnp.bfloat16),
            jax.ShapeDtypeStruct((1, ff), jnp.float32),
            *units_like(TALL, TALL_CUTS),
        ],
        scratch_shapes=[
            pltpu.VMEM((rows, D), jnp.float32),
            pltpu.VMEM((rows, FF_BLOCK), jnp.bfloat16),
        ]
        + fold_scratch(TALL, TALL_CUTS, count),
        compiler_params=pltpu.CompilerParams(
            vmem_limit_bytes=56 << 20, collective_id=5, has_side_effects=True
        ),
        name="narrow_back",
    )(d_mlp, x, slope, w_down, w_up, grad)


def per_device(
    tokens,
    segments,
    random_blocks,
    out_grad,
    w_query,
    w_key,
    w_value,
    w_out,
    w_up,
    w_down,
    vectors,
    up_bias,
):
    count = lax.axis_size("fsdp")
    place = lax.axis_index("fsdp")
    width = vectors.shape[1]
    small = jnp.zeros((16, 256), jnp.bfloat16)
    small = small.at[:8, :width].set(vectors).at[8:12, :width].set(up_bias.reshape(4, -1))
    full_query, full_key, full_value, small, full_out, full_up = gather_first(
        (w_query, w_key, w_value, small, w_out, w_up)
    )
    full_query, full_key, full_value = (
        w.reshape(D, D) for w in (full_query, full_key, full_value)
    )
    full_vectors = jnp.moveaxis(small[:, :8, :width], 0, 1).reshape(8, -1)
    full_bias = small[:, 8:12, :width].reshape(-1).astype(jnp.float32)

    vec_float = full_vectors.astype(jnp.float32)
    inputs = tokens.astype(jnp.float32)
    q_low = (jnp.dot(tokens, full_query, preferred_element_type=jnp.float32) + vec_float[0]).astype(
        jnp.bfloat16
    )
    k_low = jnp.dot(tokens, full_key, preferred_element_type=jnp.float32).astype(jnp.bfloat16)
    v_low = (jnp.dot(tokens, full_value, preferred_element_type=jnp.float32) + vec_float[1]).astype(
        jnp.bfloat16
    )
    q_feat, k_feat = mask_features(segments, random_blocks[0])
    mixed_low, aux, full_out, full_up, full_down = attention_forward(
        q_low, k_low, v_low, q_feat, k_feat, w_down, full_out, full_up
    )
    full_out, full_up = (w.reshape(-1, w.shape[-1]) for w in (full_out, full_up))
    attn_out = jnp.dot(mixed_low, full_out, preferred_element_type=jnp.float32) + vec_float[2]
    first_sum = inputs + attn_out
    normed_one, pull_one = jax.vjp(normalize, first_sum, vec_float[3], vec_float[4])
    normed_low = normed_one.astype(jnp.bfloat16)

    activated_low, slope, full_down = widen(normed_low, full_up, full_bias, full_down)
    full_down = full_down.reshape(-1, D)
    mlp_out = jnp.dot(activated_low, full_down, preferred_element_type=jnp.float32) + vec_float[5]
    second_sum = normed_one + mlp_out
    layer_out, pull_two = jax.vjp(normalize, second_sum, vec_float[6], vec_float[7])
    valid = (segments >= 0).astype(jnp.float32)[:, None]
    squares = jnp.stack(
        [
            jnp.sum(valid * first_sum * first_sum),
            jnp.sum(valid * attn_out * attn_out),
            jnp.sum(valid * mlp_out * mlp_out),
            jnp.sum(valid),
        ]
    )
    d_second, d_gain_two, d_shift_two = pull_two(out_grad.astype(jnp.float32))
    d_mlp = d_second.astype(jnp.bfloat16)

    grad_down = dot_tn(activated_low, d_mlp).astype(jnp.bfloat16).reshape(count, -1, D)
    d_wide, grad_up, bias_sums, *down_units = narrow_back(
        d_mlp, normed_low, slope, full_down, full_up, grad_down
    )
    d_normed = d_second + d_wide
    d_first, d_gain_one, d_shift_one = pull_one(d_normed)
    d_attn = d_first.astype(jnp.bfloat16)
    d_mixed = dot_nt(d_attn, full_out).astype(jnp.bfloat16)
    rest = [
        g.astype(jnp.bfloat16).reshape(count, -1, g.shape[1])
        for g in (dot_tn(mixed_low, d_attn), grad_up)
    ]
    dq_low, dk_low, dv_low, *units, grad_down = attention_backward(
        q_low, k_low, v_low, d_mixed, mixed_low, aux, k_feat, rest, down_units, w_down.shape
    )
    first = [
        dot_tn(tokens, d).astype(jnp.bfloat16).reshape(count, -1, D)
        for d in (dq_low, dk_low, dv_low)
    ]
    tokens_grad = (
        d_first + dot_nt(dq_low, full_query) + dot_nt(dk_low, full_key) + dot_nt(dv_low, full_value)
    )
    grad_vectors = jnp.stack(
        [
            col_sums(dq_low),
            col_sums(dv_low),
            col_sums(d_attn),
            d_gain_one,
            d_shift_one,
            col_sums(d_mlp),
            d_gain_two,
            d_shift_two,
            jnp.zeros((D,), jnp.float32).at[:4].set(squares),
        ]
    )
    small = jnp.concatenate(
        [grad_vectors, bias_sums.reshape(-1, D), jnp.zeros((3, D), jnp.float32)], 0
    )
    *grads, sums = reduce_last(first, units, [w_out.shape, w_up.shape], small)
    grads = [g.astype(jnp.float32) for g in (*grads, grad_down)]
    rms_values = jnp.sqrt(sums[8, :3] / (sums[8, 3] * D))
    bias_sums = sums[9:13].reshape(count, -1)
    return (
        layer_out.astype(jnp.bfloat16),
        tokens_grad.astype(jnp.bfloat16),
        *grads,
        lax.dynamic_slice_in_dim(sums[:8], place * width, width, 1),
        lax.dynamic_index_in_dim(bias_sums, place, 0, False),
        rms_values,
    )


def solution(mesh):
    in_specs = (
        P(("rep", "fsdp"), None),
        P(("rep", "fsdp")),
        P(("rep", "fsdp"), None, None),
        P(("rep", "fsdp"), None),
        P("fsdp", None),
        P("fsdp", None),
        P("fsdp", None),
        P("fsdp", None),
        P("fsdp", None),
        P("fsdp", None),
        P(None, "fsdp"),
        P("fsdp"),
    )
    out_specs = (
        P(("rep", "fsdp"), None),
        P(("rep", "fsdp"), None),
        P("fsdp", None),
        P("fsdp", None),
        P("fsdp", None),
        P("fsdp", None),
        P("fsdp", None),
        P("fsdp", None),
        P(None, "fsdp"),
        P("fsdp"),
        P(),
    )
    return jax.shard_map(
        per_device, mesh=mesh, in_specs=in_specs, out_specs=out_specs, check_vma=False
    )
```

```python
import functools

import jax
import jax.numpy as jnp
from jax import lax
from jax.experimental import pallas as pl
from jax.experimental.pallas import tpu as pltpu
from jax.sharding import PartitionSpec as P

D = 768
H = 12
DH = 64
BLK = 64
SEQ_LEN = 1024
NB = 16


masked_score = -1e30
layer_eps = 1e-05


def normalize(values, gain, shift):
    centered = values - jnp.mean(values, axis=-1, keepdims=True)
    variance = jnp.mean(centered * centered, axis=-1, keepdims=True)
    return centered * lax.rsqrt(variance + layer_eps) * gain + shift


def gelu_exact(values):
    return jax.nn.gelu(values, approximate=False)


def dot_tn(left, right):
    return lax.dot_general(
        left, right, (((0,), (0,)), ((), ())), preferred_element_type=jnp.float32
    )


def dot_nt(left, right):
    return lax.dot_general(
        left, right, (((1,), (1,)), ((), ())), preferred_element_type=jnp.float32
    )


def col_sums(values):
    return jnp.sum(values.astype(jnp.float32), axis=0)


LOG2E=1.4426950408889634
BIG=1e30

def dot_nn(a,b): return lax.dot_general(a,b,(((1,),(0,)),((),())),preferred_element_type=jnp.float32)

def mask_features(seg_row, random_row):
    blocks = jnp.arange(NB, dtype=jnp.int32)
    near = jnp.abs(blocks[:, None] - blocks[None, :]) <= 1
    first = (blocks[:, None] < 2) | (blocks[None, :] < 2)
    picked = jnp.any(random_row[:, :, None] == blocks[None, None, :], axis=1)
    seen = first | near | picked
    q_block = jnp.where(seen, 0.0, -BIG)
    q_block = jnp.repeat(q_block, BLK, axis=0)
    k_block = jnp.repeat(jnp.eye(NB, dtype=jnp.float32), BLK, axis=0)
    numbers = jnp.arange(-1, 2, dtype=jnp.int32)
    same = seg_row[:, None] == numbers[None, :]
    q_seg = jnp.where(same, 0.0, -BIG)
    k_seg = same.astype(jnp.float32)
    rest = SEQ_LEN, 128 - NB - 3
    ones = jnp.ones((SEQ_LEN, 3), jnp.float32)
    q_feat = jnp.concatenate([q_block, q_seg, jnp.zeros(rest, jnp.float32)], axis=1)
    k_feat = jnp.concatenate([k_block, k_seg, ones, jnp.zeros((SEQ_LEN, 128 - NB - 6), jnp.float32)], axis=1)
    return q_feat.astype(jnp.bfloat16), k_feat.astype(jnp.bfloat16)

MESH = pl.DeviceIdType.MESH


class Where:
    def __init__(self, extra=()):
        rep, place, count = lax.axis_index("rep"), lax.axis_index("fsdp"), lax.axis_size("fsdp")
        self.place, self.extra = place, tuple(extra)
        self.bits, self.flips = {}, {}
        for bit in (0, 1, 2) + self.extra:
            value = lax.rem(lax.div(rep, 1 << bit), 2)
            self.bits[bit] = value
            self.flips[bit] = rep + (1 - 2 * value) * (1 << bit)
        self.ahead = [lax.rem(place + step, count) for step in range(count)]
        self.behind = [lax.rem(place + count - step, count) for step in range(count)]

    def greet(self):
        barrier = pltpu.get_barrier_semaphore()
        for flip in self.flips.values():
            pl.semaphore_signal(barrier, inc=1, device_id={"rep": flip}, device_id_type=MESH)
        for there in self.ahead[1:]:
            pl.semaphore_signal(barrier, inc=1, device_id={"fsdp": there}, device_id_type=MESH)

    def meet(self):
        pl.semaphore_wait(
            pltpu.get_barrier_semaphore(), len(self.flips) + len(self.ahead) - 1
        )


def region(where, kind, rows, cols, order, level):
    core, first, second = (where.bits[bit] for bit in (0, *order))
    index = (second * 2 + first, second * 2, 0)[level]
    units = (1, 2, 4)[level]
    if kind == "square":
        unit = rows // 4
        return (
            pl.ds(pl.multiple_of(index * unit, unit), units * unit),
            pl.ds(pl.multiple_of(core * (cols // 2), cols // 2), cols // 2),
        )
    if kind == "wide":
        unit = cols // 8
        return (
            pl.ds(0, rows),
            pl.ds(pl.multiple_of((core * 4 + index) * unit, unit), units * unit),
        )
    unit = rows // 8
    return (
        pl.ds(pl.multiple_of((core * 4 + index) * unit, unit), units * unit),
        pl.ds(0, cols),
    )


SPAN = 3
AHEAD = 6


class Gather:
    def __init__(self, where, parts, shards, fulls, sems, low, highs):
        self.where = where
        self.parts, self.shards, self.fulls, self.low, self.highs = parts, shards, fulls, low, highs
        self.send, self.recv, self.local = sems
        self.count, self.place = lax.axis_size("fsdp"), where.place
        self.blocks = []
        for p in range(len(parts)):
            for step in range(1, self.count):
                _, array, row, col, _, _ = parts[p]
                turn = array + row // 48 + col // 256 + step
                self.blocks.append((p, step, (1, 2) if turn % 2 == 0 else (2, 1)))

    def copy(self, k, stage):
        p, step, order = self.blocks[k]
        kind, a, row, col, rows, cols = self.parts[p]
        full = self.fulls[a]
        if kind != "whole":
            r, c = region(self.where, kind, rows, cols, order, max(stage - 1, 0))
            if row:
                r = pl.ds(pl.multiple_of(r.start + row, 16), r.size)
            if col:
                c = pl.ds(pl.multiple_of(c.start + col, 128), c.size)
        if stage == 0:
            if kind == "whole":
                src, dst = self.shards[a], full.at[self.place]
            else:
                src, dst = self.shards[a].at[r, c], full.at[self.place, r, c]
            device = {"fsdp": self.where.ahead[step]}
        else:
            origin = self.where.behind[step]
            src = dst = full.at[origin, r, c]
            device = {"rep": self.where.flips[(order + (0,))[stage - 1]]}
        return pltpu.make_async_remote_copy(
            src_ref=src,
            dst_ref=dst,
            send_sem=self.send.at[k, stage],
            recv_sem=self.recv.at[k, stage],
            device_id=device,
            device_id_type=MESH,
        )

    def end(self, k):
        return self.highs[self.blocks[k][0]]

    def own(self, a):
        return pltpu.make_async_copy(
            self.shards[a], self.fulls[a].at[self.place], self.local.at[a]
        )

    def begin(self):
        for k in range(min(AHEAD, len(self.blocks)) if self.low == 0 else len(self.blocks)):
            self.copy(k, self.low).start()
        if self.low == 0:
            for a in range(len(self.shards)):
                self.own(a).start()

    def ticks(self):
        return len(self.blocks) + (max(self.highs) - self.low - 1) * SPAN

    def tick(self, t):
        for stage in range(self.low, max(self.highs)):
            k = t - (stage - self.low) * SPAN
            if 0 <= k < len(self.blocks) and stage < self.end(k):
                self.copy(k, stage).wait_recv()
                if stage == 0 and k + AHEAD < len(self.blocks):
                    self.copy(k + AHEAD, 0).start()
                if stage + 1 < self.end(k):
                    self.copy(k, stage + 1).start()

    def finish(self):
        for k in range(len(self.blocks)):
            for stage in range(self.low, self.end(k)):
                self.copy(k, stage).wait_send()
        if self.low == 0:
            for a in range(len(self.shards)):
                self.own(a).wait()


def gather_sems(parts, arrays, count):
    blocks = len(parts) * (count - 1)
    return [
        pltpu.SemaphoreType.DMA((blocks, 4)),
        pltpu.SemaphoreType.DMA((blocks, 4)),
        pltpu.SemaphoreType.DMA((arrays,)),
    ]


def whole_like(shards):
    return [jax.ShapeDtypeStruct((lax.axis_size("fsdp"), *s.shape), s.dtype) for s in shards]


def run_all(where, jobs, delays):
    where.greet()
    where.meet()
    for t in range(max(job.ticks() + delay for job, delay in zip(jobs, delays))):
        for job, delay in zip(jobs, delays):
            if t == delay:
                job.begin()
            if 0 <= t - delay < job.ticks():
                job.tick(t - delay)
    for job in jobs:
        job.finish()


FIRST = (
    *(("square", i, 0, 0, D // 4, D) for i in range(3)),
    ("whole", 3, 0, 0, 16, 256),
)
REST = (
    ("square", 0, 0, 0, D // 4, D),
    *(("wide", 1, 48 * i, 0, 48, 4 * D) for i in range(4)),
)
LATER = tuple(("tall", 2, 0, 256 * i, D, 256) for i in range(3))
DOWN = tuple(("tall", 0, *p[2:]) for p in LATER)


def gather_kernel(*refs):
    n = (len(refs) - 3) // 2
    where = Where()
    job = Gather(where, FIRST, refs[:n], refs[n : 2 * n], refs[2 * n :], 0, (4, 4, 4, 1))
    run_all(where, [job], (0,))


def gather_first(shards):
    count = lax.axis_size("fsdp")
    return pl.pallas_call(
        gather_kernel,
        in_specs=[pl.BlockSpec(memory_space=pltpu.VMEM)] * len(shards),
        out_specs=[pl.BlockSpec(memory_space=pl.ANY)] * len(shards),
        out_shape=whole_like(shards),
        scratch_shapes=gather_sems(FIRST, len(shards), count),
        compiler_params=pltpu.CompilerParams(
            collective_id=0, has_side_effects=True, vmem_limit_bytes=24 << 20
        ),
        name="gather_first",
    )(*shards)


LAG = 3


def half_shape(kind, rows, cols):
    return (rows // 2, cols) if kind == "tall" else (rows, cols // 2)


def part_shape(kind, rows, cols, level):
    r, c = half_shape(kind, rows, cols)
    cut = (4, 2, 1)[level]
    return (r, c // cut) if kind == "wide" else (r // cut, c)


def part(kind, rows, cols, first, second, level):
    index = (second * 2 + first, second * 2, 0)[level]
    units = (1, 2, 4)[level]
    r, c = half_shape(kind, rows, cols)
    if kind == "wide":
        unit = c // 4
        return pl.ds(0, r), pl.ds(pl.multiple_of(index * unit, unit), units * unit)
    unit = r // 4
    return pl.ds(pl.multiple_of(index * unit, unit), units * unit), pl.ds(0, c)


def half(kind, rows, cols, core):
    r, c = half_shape(kind, rows, cols)
    if kind == "tall":
        return pl.ds(pl.multiple_of(core * r, r), r), pl.ds(0, c)
    return pl.ds(0, r), pl.ds(pl.multiple_of(core * c, c), c)


def add_into(target, where, values):
    rows, cols = where
    chunk = 16
    total, base = rows.size, rows.start

    @pl.loop(0, total // chunk)
    def _(i):
        at = pl.ds(pl.multiple_of(base + i * chunk, chunk), chunk)
        more = values[pl.ds(pl.multiple_of(i * chunk, chunk), chunk), :]
        kept = target[at, cols]
        target[at, cols] = (kept.astype(jnp.float32) + more.astype(jnp.float32)).astype(
            target.dtype
        )


class Reduce:
    def __init__(self, where, kinds, grads, results, scratch, extra, cuts):
        self.where = where
        self.kinds, self.grads, self.results, self.extra = kinds, grads, results, extra
        self.cuts = cuts
        n = len(kinds)
        self.acc, self.got0, self.got1, self.got2, self.got3 = (
            scratch[i * n : (i + 1) * n] for i in range(5)
        )
        self.outs, rest = scratch[5 * n : 6 * n], scratch[6 * n :]
        if extra:
            self.gotx, rest = rest[:n], rest[n:]
        self.load, self.send, self.recv, self.gsend, self.grecv, self.store = rest[:6]
        self.count, self.place = lax.axis_size("fsdp"), where.place
        self.blocks = [
            (a, step) for step in list(range(1, self.count)) + [0] for a in range(n)
        ]

    def order(self, a):
        return (1, 2) if a % 2 == 0 else (2, 1)

    def bits(self, a):
        order = self.order(a)
        return self.where.bits[order[0]], self.where.bits[order[1]]

    def shape(self, a):
        return self.cuts[a][3:]

    def source(self, a, step, core):
        g, row, col, rows, cols = self.cuts[a]
        r, c = half(self.kinds[a], rows, cols, core)
        if row:
            r = pl.ds(pl.multiple_of(r.start + row, 16), r.size)
        if col:
            c = pl.ds(pl.multiple_of(c.start + col, 128), c.size)
        return self.grads[g].at[self.where.ahead[step], r, c]

    def mine(self, k):
        a, step = self.blocks[k]
        return pltpu.make_async_copy(
            self.source(a, step, self.where.bits[0]), self.acc[a].at[step], self.load.at[k]
        )

    def copy(self, k, stage):
        a, step = self.blocks[k]
        kind, shape = self.kinds[a], self.shape(a)
        first, second = self.bits(a)
        order = self.order(a)
        if stage == 0:
            src, dst = self.source(a, step, 1 - self.where.bits[0]), self.got0[a].at[step]
            device = {"rep": self.where.flips[0]}
        elif stage == 1:
            r, c = part(kind, *shape, first, 1 - second, 1)
            src, dst = self.acc[a].at[step, r, c], self.got1[a].at[step]
            device = {"rep": self.where.flips[order[1]]}
        elif stage == 2:
            r, c = part(kind, *shape, 1 - first, second, 0)
            src, dst = self.acc[a].at[step, r, c], self.got2[a].at[step]
            device = {"rep": self.where.flips[order[0]]}
        else:
            r, c = part(kind, *shape, first, second, 0)
            src, dst = self.acc[a].at[step, r, c], self.got3[a].at[step - 1]
            device = {"fsdp": self.where.ahead[step]}
        return pltpu.make_async_remote_copy(
            src_ref=src,
            dst_ref=dst,
            send_sem=self.send.at[k, stage],
            recv_sem=self.recv.at[k, stage],
            device_id=device,
            device_id_type=MESH,
        )

    def whole(self, a, level):
        kind, (rows, cols) = self.kinds[a], self.shape(a)
        return region(self.where, kind, rows, cols, self.order(a), level)

    def back(self, a, level):
        r, c = self.whole(a, level)
        ref = self.outs[a].at[r, c]
        bit = (self.order(a) + (0,))[level]
        return pltpu.make_async_remote_copy(
            src_ref=ref,
            dst_ref=ref,
            send_sem=self.gsend.at[a, level],
            recv_sem=self.grecv.at[a, level],
            device_id={"rep": self.where.flips[bit]},
            device_id_type=MESH,
        )

    def more(self, a, i):
        r, c = self.whole(a, 0)
        return pltpu.make_async_remote_copy(
            src_ref=self.outs[a].at[r, c],
            dst_ref=self.gotx[a].at[i],
            send_sem=self.gsend.at[a, 3 + i],
            recv_sem=self.grecv.at[a, 3 + i],
            device_id={"rep": self.where.flips[self.extra[i]]},
            device_id_type=MESH,
        )

    def begin(self):
        for k in range(len(self.blocks)):
            self.copy(k, 0).start()
            self.mine(k).start()

    def absorb(self, k, stage):
        a, step = self.blocks[k]
        kind, shape = self.kinds[a], self.shape(a)
        first, second = self.bits(a)
        got = (self.got0, self.got1, self.got2)[stage][a].at[step]
        where = part(kind, *shape, first, second, 2 - stage)
        if stage == 0:
            self.mine(k).wait()
        self.copy(k, stage).wait_recv()
        add_into(self.acc[a].at[step], where, got)
        if stage < 2 or step:
            self.copy(k, stage + 1).start()

    def total(self, a):
        kind, shape = self.kinds[a], self.shape(a)
        first, second = self.bits(a)
        for step in range(1, self.count):
            self.copy(self.blocks.index((a, step)), 3).wait_recv()
        rows, cols = part(kind, *shape, first, second, 0)
        to_rows, to_cols = self.whole(a, 0)
        chunk = 16

        @pl.loop(0, rows.size // chunk)
        def _(i):
            at = pl.ds(pl.multiple_of(rows.start + i * chunk, chunk), chunk)
            total = self.acc[a][0, at, cols].astype(jnp.float32)
            near = pl.ds(pl.multiple_of(i * chunk, chunk), chunk)
            for step in range(self.count - 1):
                total = total + self.got3[a][step, near, :].astype(jnp.float32)
            to = pl.ds(pl.multiple_of(to_rows.start + i * chunk, chunk), chunk)
            self.outs[a][to, to_cols] = total.astype(jnp.bfloat16)

        for i in range(len(self.extra)):
            copy = self.more(a, i)
            copy.start()
            copy.wait()
            add_into(self.outs[a], self.whole(a, 0), self.gotx[a].at[i])
        self.back(a, 0).start()

    def put(self, a):
        g, row, col, rows, cols = self.cuts[a]
        to = self.results[g].at[pl.ds(row, rows), pl.ds(col, cols)]
        return pltpu.make_async_copy(self.outs[a], to, self.store.at[a])

    def ticks(self):
        return len(self.blocks) + 6 * LAG

    def tick(self, t):
        blocks = len(self.blocks)
        for stage in range(3):
            k = t - stage * LAG
            if 0 <= k < blocks:
                self.absorb(k, stage)
        for a in range(len(self.kinds)):
            late = t - self.blocks.index((a, 0)) - 3 * LAG
            if late == 0:
                self.total(a)
            elif late in (LAG, 2 * LAG, 3 * LAG):
                level = late // LAG
                self.back(a, level - 1).wait_recv()
                if level < 3:
                    self.back(a, level).start()
                else:
                    self.put(a).start()

    def finish(self):
        for k, (a, step) in enumerate(self.blocks):
            for stage in range(4 if step else 3):
                self.copy(k, stage).wait_send()
        for a in range(len(self.kinds)):
            for level in range(3):
                self.back(a, level).wait_send()
            self.put(a).wait()


class Fold(Reduce):
    def __init__(self, where, kinds, grads, units, scratch, cuts):
        self.where = where
        self.kinds, self.grads, self.units, self.cuts = kinds, grads, units, cuts
        n = len(kinds)
        self.acc, self.got0, self.got1, self.got2, self.got3, self.kept = (
            scratch[i * n : (i + 1) * n] for i in range(6)
        )
        self.load, self.send, self.recv, self.store = scratch[6 * n :]
        self.count, self.place = lax.axis_size("fsdp"), where.place
        self.blocks = [(a, step) for step in [*range(1, self.count), 0] for a in range(n)]

    def keep(self, a):
        return pltpu.make_async_copy(self.kept[a], self.units[a], self.store.at[a])

    def total(self, a):
        for step in range(1, self.count):
            self.copy(self.blocks.index((a, step)), 3).wait_recv()
        rows, cols = part(self.kinds[a], *self.shape(a), *self.bits(a), 0)
        chunk = 16

        @pl.loop(0, rows.size // chunk)
        def _(i):
            at = pl.ds(pl.multiple_of(rows.start + i * chunk, chunk), chunk)
            total = self.acc[a][0, at, cols].astype(jnp.float32)
            near = pl.ds(pl.multiple_of(i * chunk, chunk), chunk)
            for step in range(self.count - 1):
                total = total + self.got3[a][step, near, :].astype(jnp.float32)
            self.kept[a][near, :] = total.astype(jnp.bfloat16)

        self.keep(a).start()

    def ticks(self):
        return len(self.blocks) + 3 * LAG

    def tick(self, t):
        for stage in range(3):
            k = t - stage * LAG
            if 0 <= k < len(self.blocks):
                self.absorb(k, stage)
        for a in range(len(self.kinds)):
            if t == self.blocks.index((a, 0)) + 3 * LAG:
                self.total(a)

    def finish(self):
        for k, (a, step) in enumerate(self.blocks):
            for stage in range(4 if step else 3):
                self.copy(k, stage).wait_send()
        for a in range(len(self.kinds)):
            self.keep(a).wait()


class Spread(Reduce):
    def __init__(self, where, kinds, units, results, scratch, extra, cuts):
        self.where = where
        self.kinds, self.units, self.results = kinds, units, results
        self.extra, self.cuts = extra, cuts
        n = len(kinds)
        self.outs, rest = scratch[:n], scratch[n:]
        if extra:
            self.gotx, rest = rest[:n], rest[n:]
        self.load, self.gsend, self.grecv, self.store = rest

    def near(self, a):
        r, c = self.whole(a, 0)
        return pltpu.make_async_copy(self.units[a], self.outs[a].at[r, c], self.load.at[a])

    def begin(self):
        for a in range(len(self.kinds)):
            self.near(a).start()

    def ticks(self):
        return 4 * len(self.kinds)

    def tick(self, t):
        level, a = divmod(t, len(self.kinds))
        if level:
            self.back(a, level - 1).wait_recv()
            (self.back(a, level) if level < 3 else self.put(a)).start()
            return
        self.near(a).wait()
        for i in range(len(self.extra)):
            copy = self.more(a, i)
            copy.start()
            copy.wait()
            add_into(self.outs[a], self.whole(a, 0), self.gotx[a].at[i])
        self.back(a, 0).start()

    def finish(self):
        for a in range(len(self.kinds)):
            for level in range(3):
                self.back(a, level).wait_send()
            self.put(a).wait()


def units_like(kinds, cuts):
    return [jax.ShapeDtypeStruct(part_shape(k, *c[3:], 0), jnp.bfloat16) for k, c in zip(kinds, cuts)]


def fold_scratch(kinds, cuts, count):
    B = jnp.bfloat16
    sizes = [(k, *c[3:]) for k, c in zip(kinds, cuts)]
    blocks = len(kinds) * count
    dma = pltpu.SemaphoreType.DMA
    return (
        [pltpu.VMEM((count, *half_shape(*s)), B) for s in sizes] * 2
        + [pltpu.VMEM((count, *part_shape(*s, 1)), B) for s in sizes]
        + [pltpu.VMEM((count, *part_shape(*s, 0)), B) for s in sizes]
        + [pltpu.VMEM((count - 1, *part_shape(*s, 0)), B) for s in sizes]
        + [pltpu.VMEM(part_shape(*s, 0), B) for s in sizes]
        + [dma((blocks,)), dma((blocks, 4)), dma((blocks, 4)), dma((len(kinds),))]
    )


def spread_scratch(kinds, cuts, count, extra):
    B = jnp.bfloat16
    sizes = [(k, *c[3:]) for k, c in zip(kinds, cuts)]
    n = len(kinds)
    dma = pltpu.SemaphoreType.DMA
    made = [pltpu.VMEM(s[1:], B) for s in sizes]
    if extra:
        made += [pltpu.VMEM((len(extra), *part_shape(*s, 0)), B) for s in sizes]
    backs = 3 + len(extra)
    return made + [dma((n,)), dma((n, backs)), dma((n, backs)), dma((n,))]


class Sums:
    def __init__(self, where, source, result, held, got, send, recv, extra):
        self.where = where
        self.source, self.result, self.held, self.got = source, result, held, got
        self.send, self.recv = send, recv
        self.bits = (0, 1, 2) + tuple(extra)
        self.count, self.place = lax.axis_size("fsdp"), where.place

    def copy(self, i):
        level = min(i, len(self.bits))
        src = self.source if level == 0 else self.held.at[level - 1]
        if i < len(self.bits):
            device = {"rep": self.where.flips[self.bits[i]]}
        else:
            step = i - len(self.bits) + 1
            device = {"fsdp": self.where.ahead[step]}
        return pltpu.make_async_remote_copy(
            src_ref=src,
            dst_ref=self.got.at[i],
            send_sem=self.send.at[i],
            recv_sem=self.recv.at[i],
            device_id=device,
            device_id_type=MESH,
        )

    def begin(self):
        self.copy(0).start()

    def ticks(self):
        return len(self.bits) + 1

    def tick(self, t):
        bits = len(self.bits)
        if t < bits:
            self.copy(t).wait_recv()
            before = self.source[...] if t == 0 else self.held[t - 1]
            self.held[t] = before + self.got[t]
            for i in range(t + 1, t + 2 if t + 1 < bits else bits + self.count - 1):
                self.copy(i).start()
        elif t == bits:
            total = self.held[bits - 1]
            for i in range(bits, bits + self.count - 1):
                self.copy(i).wait_recv()
                total = total + self.got[i]
            self.result[...] = total

    def finish(self):
        for i in range(len(self.bits) + self.count - 1):
            self.copy(i).wait_send()


def reduce_scratch(kinds, shapes, count, extra):
    B = jnp.bfloat16
    sizes = [(k, *s) for k, s in zip(kinds, shapes)]
    made = [pltpu.VMEM((count, *half_shape(*s)), B) for s in sizes]
    made += [pltpu.VMEM((count, *half_shape(*s)), B) for s in sizes]
    made += [pltpu.VMEM((count, *part_shape(*s, 1)), B) for s in sizes]
    made += [pltpu.VMEM((count, *part_shape(*s, 0)), B) for s in sizes]
    made += [pltpu.VMEM((count - 1, *part_shape(*s, 0)), B) for s in sizes]
    made += [pltpu.VMEM(s, B) for s in shapes]
    if extra:
        made += [pltpu.VMEM((len(extra), *part_shape(*s, 0)), B) for s in sizes]
    n = len(kinds)
    dma = pltpu.SemaphoreType.DMA
    made += [dma((n * count,)), dma((n * count, 4)), dma((n * count, 4))]
    made += [dma((n, 3 + len(extra))), dma((n, 3 + len(extra))), dma((n,))]
    return made


def sums_scratch(shape, count, extra):
    bits = 3 + len(extra)
    dma = pltpu.SemaphoreType.DMA
    return [
        pltpu.VMEM((bits, *shape), jnp.float32),
        pltpu.VMEM((bits + count - 1, *shape), jnp.float32),
        dma((bits + count - 1,)),
        dma((bits + count - 1,)),
    ]


def extra_bits():
    found, bit = [], 3
    while (1 << bit) < lax.axis_size("rep"):
        found.append(bit)
        bit += 1
    return tuple(found)


REST_BACK = ("square", "wide", "wide")
REST_CUTS = ((0, 0, 0, D // 4, D), (1, 0, 0, D // 8, 4 * D), (1, D // 8, 0, D // 8, 4 * D))
TALL = ("tall", "tall")
TALL_CUTS = ((0, 0, 0, D, D // 2), (0, 0, D // 2, D, D // 2))
LAST = ("square", "square", "square")


def reduce_kernel(extra, spread_size, *refs):
    n, m, p = len(LAST), len(REST_BACK), 2
    grads, units, small = refs[:n], refs[n : n + m], refs[n + m]
    outs = refs[n + m + 1 : n + m + 1 + n + p]
    total, scratch = refs[n + m + 1 + n + p], refs[n + m + 2 + n + p :]
    cuts = [(i, 0, 0, *g.shape[1:]) for i, g in enumerate(grads)]
    where = Where(extra)
    run_all(
        where,
        [
            Reduce(where, LAST, grads, outs[:n], scratch[spread_size:-4], extra, cuts),
            Spread(where, REST_BACK, units, outs[n:], scratch[:spread_size], extra, REST_CUTS),
            Sums(where, small, total, *scratch[-4:], extra),
        ],
        (0, 0, 0),
    )


def reduce_last(grads, units, shards, small):
    count = lax.axis_size("fsdp")
    extra = extra_bits()
    shapes = [g.shape[1:] for g in grads]
    vmem = pl.BlockSpec(memory_space=pltpu.VMEM)
    hbm = pl.BlockSpec(memory_space=pl.ANY)
    spread = spread_scratch(REST_BACK, REST_CUTS, count, extra)
    return pl.pallas_call(
        functools.partial(reduce_kernel, extra, len(spread)),
        in_specs=[hbm] * (len(grads) + len(units)) + [vmem],
        out_specs=[hbm] * (len(grads) + len(shards)) + [vmem],
        out_shape=[jax.ShapeDtypeStruct(s, jnp.bfloat16) for s in shapes + shards]
        + [jax.ShapeDtypeStruct(small.shape, jnp.float32)],
        scratch_shapes=spread
        + reduce_scratch(LAST, shapes, count, extra)
        + sums_scratch(small.shape, count, extra),
        compiler_params=pltpu.CompilerParams(
            collective_id=3, has_side_effects=True, vmem_limit_bytes=48 << 20
        ),
        name="reduce_last",
    )(*grads, *units, small)


TQ = 256
POINTS = 24


def host(where, jobs, paces, tile):
    for point in range(tile, POINTS, 4):
        due = [
            (job, i)
            for job, (first, pace) in zip(jobs, paces)
            for i in range(job.ticks())
            if int(first + pace * i) == point
        ]
        if due or point == 0:

            @pl.when(pl.program_id(0) == point // 4)
            def _(due=due, point=point):
                if point == 0:
                    where.greet()
                    where.meet()
                    for job in jobs:
                        job.begin()
                for job, i in due:
                    job.tick(i)


def close(jobs, paces):
    left = [
        (i, j)
        for j, (job, (first, pace)) in enumerate(zip(jobs, paces))
        for i in range(job.ticks())
        if int(first + pace * i) >= POINTS
    ]

    @pl.when(pl.program_id(0) == POINTS // 4 - 1)
    def _():
        for i, j in sorted(left):
            jobs[j].tick(i)
        for job in jobs:
            job.finish()


FORWARD_PACES = ((5, 0.85),)
WIDEN_PACES = ((8, 1.4),)
NARROW_PACES = ((4, 1.8),)
BACKWARD_PACES = ((4, 1.3), (2, 2.5))


def fwd_kernel(q_ref,k_ref,v_ref,qf_ref,kf_ref,s0,s1,s2,o_ref,aux_ref,f0,f1,f2,qc,kc,vm,*sems):
    highs = (4,) * len(REST) + (1,) * len(LATER)
    where = Where()
    jobs = [Gather(where, REST + LATER, (s0, s1, s2), (f0, f1, f2), sems, 0, highs)]
    lane = lax.broadcasted_iota(jnp.int32,(SEQ_LEN,128),1)
    kc[:,:128]=k_ref[...]
    kc[:,128:]=kf_ref[...]
    q=q_ref[...]*jnp.bfloat16(0.125)
    v=v_ref[...]
    zero=jnp.zeros_like(q)
    for h in range(2):
        sel = (lane<64) if h==0 else (lane>=64)
        qc[h,:,:128]=jnp.where(sel,q,zero)
        qc[h,:,128:]=qf_ref[...]
        vm[h]=jnp.where(sel,v,zero)
    for t in range(SEQ_LEN//TQ):
        host(where, jobs, FORWARD_PACES, t)
        rows=pl.ds(t*TQ,TQ)
        total=None
        for h in range(2):
            s=dot_nt(qc[h,rows,:],kc[...])
            m=jnp.max(s,axis=1,keepdims=True)
            p=jnp.exp2((s-m)*LOG2E)
            l=jnp.sum(p,axis=1,keepdims=True)
            o=dot_nn(p.astype(jnp.bfloat16),vm[h])*(1.0/l)
            total=o if total is None else total+o
            lse=-(m+jnp.log(l))
            hi=lse.astype(jnp.bfloat16).astype(jnp.float32)
            r=lse-hi
            mid=r.astype(jnp.bfloat16).astype(jnp.float32)
            lo=r-mid
            ln=lax.broadcasted_iota(jnp.int32,(TQ,128),1)
            a=jnp.where(ln==19,hi,jnp.where(ln==20,mid,jnp.where(ln==21,lo,qf_ref[rows,:].astype(jnp.float32))))
            aux_ref[h,rows,:]=a.astype(jnp.bfloat16)
        o_ref[rows,:]=total.astype(jnp.bfloat16)
    close(jobs, FORWARD_PACES)

def attention_forward(q,k,v,qf,kf,shards):
    count=lax.axis_size("fsdp")
    pair=pl.BlockSpec((SEQ_LEN,128),lambda i:(0,i))
    whole=pl.BlockSpec((SEQ_LEN,128),lambda i:(0,0))
    hbm=pl.BlockSpec(memory_space=pl.ANY)
    B=jnp.bfloat16
    return pl.pallas_call(fwd_kernel,grid=(H//2,),
        in_specs=[pair,pair,pair,whole,whole]+[pl.BlockSpec(memory_space=pltpu.VMEM)]*3,
        out_specs=[pair,pl.BlockSpec((2,SEQ_LEN,128),lambda i:(i,0,0)),hbm,hbm,hbm],
        out_shape=[jax.ShapeDtypeStruct((SEQ_LEN,D),B),jax.ShapeDtypeStruct((H,SEQ_LEN,128),B)]+whole_like(shards),
        scratch_shapes=[pltpu.VMEM((2,SEQ_LEN,256),B),pltpu.VMEM((SEQ_LEN,256),B),pltpu.VMEM((2,SEQ_LEN,128),B)]+gather_sems(REST+LATER,3,count),
        compiler_params=pltpu.CompilerParams(vmem_limit_bytes=48<<20,collective_id=1,has_side_effects=True),
        cost_estimate=pl.CostEstimate(flops=30_000_000_000,bytes_accessed=10_000_000,transcendentals=12_582_912),
        name="attention_forward")(q,k,v,qf,kf,*shards)

TK=256
def bwd_kernel(extra,q_ref,k_ref,v_ref,do_ref,o_ref,aux_ref,kf_ref,g0,g1,v0,v1,dq_ref,dk_ref,dv_ref,u0,u1,u2,r0,qc,dc,kc,vc,km,dqa,*scratch):
    where = Where(extra)
    jobs = [
        Fold(where, REST_BACK, (g0, g1), (u0, u1, u2), scratch[:22], REST_CUTS),
        Spread(where, TALL, (v0, v1), (r0,), scratch[22:], extra, TALL_CUTS),
    ]
    lane = lax.broadcasted_iota(jnp.int32,(SEQ_LEN,128),1)
    kc[:,:128]=k_ref[...]
    kc[:,128:]=kf_ref[...]
    vc[:,:128]=v_ref[...]
    vc[:,128:]=kf_ref[...]
    q=q_ref[...]*jnp.bfloat16(0.125)
    k=k_ref[...]*jnp.bfloat16(0.125)
    do=do_ref[...]
    prod=do.astype(jnp.float32)*o_ref[...].astype(jnp.float32)
    zero=jnp.zeros_like(q)
    for h in range(2):
        sel = (lane<64) if h==0 else (lane>=64)
        qc[h,:,:128]=jnp.where(sel,q,zero)
        qc[h,:,128:]=aux_ref[h]
        km[h]=jnp.where(sel,k,zero)
        dc[h,:,:128]=jnp.where(sel,do,zero)
        delta=-jnp.sum(jnp.where(sel,prod,0.0),axis=1,keepdims=True)
        hi=delta.astype(jnp.bfloat16).astype(jnp.float32)
        lo=delta-hi
        dc[h,:,128:]=jnp.where(lane==19,hi,jnp.where(lane==20,lo,0.0)).astype(jnp.bfloat16)
    for t in range(SEQ_LEN//TK):
        host(where, jobs, BACKWARD_PACES, t)
        rows=pl.ds(t*TK,TK)
        dv=None;dk=None;dq=None
        for h in range(2):
            s=dot_nt(kc[rows,:],qc[h])
            p=jnp.exp2(s*LOG2E)
            dp=dot_nt(vc[rows,:],dc[h])
            ds=(p*dp).astype(jnp.bfloat16)
            pb=p.astype(jnp.bfloat16)
            dvh=dot_nn(pb,dc[h,:,:128])
            dkh=dot_nn(ds,qc[h,:,:128])
            dqh=dot_tn(ds,km[h,rows,:])
            dv=dvh if dv is None else dv+dvh
            dk=dkh if dk is None else dk+dkh
            dq=dqh if dq is None else dq+dqh
        dk_ref[rows,:]=dk.astype(jnp.bfloat16)
        dv_ref[rows,:]=dv.astype(jnp.bfloat16)
        if t==0: dqa[...]=dq
        else: dqa[...]+=dq
    dq_ref[...]=dqa[...].astype(jnp.bfloat16)
    close(jobs, BACKWARD_PACES)

def attention_backward(q,k,v,do,o,aux,kf,grads,units,shard):
    count=lax.axis_size("fsdp")
    extra=extra_bits()
    pair=pl.BlockSpec((SEQ_LEN,128),lambda i:(0,i))
    whole=pl.BlockSpec((SEQ_LEN,128),lambda i:(0,0))
    hbm=pl.BlockSpec(memory_space=pl.ANY)
    sd=jax.ShapeDtypeStruct((SEQ_LEN,D),jnp.bfloat16)
    B=jnp.bfloat16
    return pl.pallas_call(functools.partial(bwd_kernel,extra),grid=(H//2,),
        in_specs=[pair]*5+[pl.BlockSpec((2,SEQ_LEN,128),lambda i:(i,0,0)),whole]+[hbm]*4,
        out_specs=[pair]*3+[hbm]*4,
        out_shape=[sd]*3+units_like(REST_BACK,REST_CUTS)+[jax.ShapeDtypeStruct(shard,B)],
        scratch_shapes=[pltpu.VMEM((2,SEQ_LEN,256),B),pltpu.VMEM((2,SEQ_LEN,256),B),pltpu.VMEM((SEQ_LEN,256),B),pltpu.VMEM((SEQ_LEN,256),B),pltpu.VMEM((2,SEQ_LEN,128),B),pltpu.VMEM((SEQ_LEN,128),jnp.float32)]
            +fold_scratch(REST_BACK,REST_CUTS,count)+spread_scratch(TALL,TALL_CUTS,count,extra),
        compiler_params=pltpu.CompilerParams(vmem_limit_bytes=56<<20,collective_id=2,has_side_effects=True),
        cost_estimate=pl.CostEstimate(flops=42_000_000_000,bytes_accessed=15_000_000,transcendentals=12_582_912),
        name="attention_backward")(q,k,v,do,o,aux,kf,*grads,*units)


FF_BLOCK = 512


def normal_cdf(u, bell):
    t = 1.0 / (1.0 + 0.3535533905932738 * jnp.abs(u))
    fit = 0.17087277
    for c in (
        -0.82215223,
        1.48851587,
        -1.13520398,
        0.27886807,
        -0.18628806,
        0.09678418,
        0.37409196,
        1.00002368,
        -1.26551223,
    ):
        fit = fit * t + c
    tail = 0.5 * t * jnp.exp2(fit * LOG2E + bell)
    return jnp.where(u < 0.0, tail, 1.0 - tail)


def widen_kernel(x_ref, w_ref, b_ref, i0, act_ref, slope_ref, f0, *sems):
    where = Where()
    jobs = [Gather(where, DOWN, None, (f0,), sems, 1, (4,) * len(DOWN))]
    for t in range(4):
        host(where, jobs, WIDEN_PACES, t)
        rows = pl.ds(t * 256, 256)
        u = dot_nn(x_ref[rows, :], w_ref[...]) + b_ref[...]
        bell = u * u * (-0.5 * LOG2E)
        cdf = normal_cdf(u, bell)
        act_ref[rows, :] = (u * cdf).astype(jnp.bfloat16)
        slope_ref[rows, :] = (cdf + u * (0.3989422804014327 * jnp.exp2(bell))).astype(jnp.bfloat16)
    close(jobs, WIDEN_PACES)


def widen(x, w, bias, full_down):
    count = lax.axis_size("fsdp")
    rows, ff = x.shape[0], w.shape[1]
    block = pl.BlockSpec((rows, FF_BLOCK), lambda i: (0, i))
    out = jax.ShapeDtypeStruct((rows, ff), jnp.bfloat16)
    return pl.pallas_call(
        widen_kernel,
        grid=(ff // FF_BLOCK,),
        in_specs=[
            pl.BlockSpec((rows, D), lambda i: (0, 0)),
            pl.BlockSpec((D, FF_BLOCK), lambda i: (0, i)),
            pl.BlockSpec((1, FF_BLOCK), lambda i: (0, i)),
            pl.BlockSpec(memory_space=pl.ANY),
        ],
        input_output_aliases={3: 2},
        out_specs=[block, block, pl.BlockSpec(memory_space=pl.ANY)],
        out_shape=[out, out, jax.ShapeDtypeStruct(full_down.shape, full_down.dtype)],
        scratch_shapes=gather_sems(DOWN, 1, count),
        compiler_params=pltpu.CompilerParams(
            vmem_limit_bytes=40 << 20, collective_id=4, has_side_effects=True
        ),
        name="widen",
    )(x, w, bias[None], full_down)


def narrow_back_kernel(
    dm_ref, x_ref, slope_ref, wd_ref, wu_ref, g0, dx_ref, gu_ref, sum_ref, u0, u1, acc, du, *scratch
):
    where = Where()
    jobs = [Fold(where, TALL, (g0,), (u0, u1), scratch, TALL_CUTS)]
    sums = jnp.zeros((1, FF_BLOCK), jnp.float32)
    for t in range(4):
        host(where, jobs, NARROW_PACES, t)
        rows = pl.ds(t * 256, 256)
        d = dot_nt(dm_ref[rows, :], wd_ref[...]) * slope_ref[rows, :].astype(jnp.float32)
        low = d.astype(jnp.bfloat16)
        du[rows, :] = low
        sums = sums + jnp.sum(low.astype(jnp.float32), axis=0, keepdims=True)
        more = dot_nt(low, wu_ref[...])

        @pl.when(pl.program_id(0) == 0)
        def _():
            acc[rows, :] = more

        @pl.when(pl.program_id(0) > 0)
        def _():
            acc[rows, :] += more

    gu_ref[...] = dot_tn(x_ref[...], du[...]).astype(jnp.bfloat16)
    sum_ref[...] = sums

    @pl.when(pl.program_id(0) == pl.num_programs(0) - 1)
    def _():
        dx_ref[...] = acc[...]

    close(jobs, NARROW_PACES)


def narrow_back(d_mlp, x, slope, w_down, w_up, grad):
    count = lax.axis_size("fsdp")
    rows, ff = slope.shape
    whole = pl.BlockSpec((rows, D), lambda i: (0, 0))
    cols = pl.BlockSpec((D, FF_BLOCK), lambda i: (0, i))
    hbm = pl.BlockSpec(memory_space=pl.ANY)
    return pl.pallas_call(
        narrow_back_kernel,
        grid=(ff // FF_BLOCK,),
        in_specs=[
            whole,
            whole,
            pl.BlockSpec((rows, FF_BLOCK), lambda i: (0, i)),
            pl.BlockSpec((FF_BLOCK, D), lambda i: (i, 0)),
            cols,
            hbm,
        ],
        out_specs=[whole, cols, pl.BlockSpec((1, FF_BLOCK), lambda i: (0, i)), hbm, hbm],
        out_shape=[
            jax.ShapeDtypeStruct((rows, D), jnp.float32),
            jax.ShapeDtypeStruct((D, ff), jnp.bfloat16),
            jax.ShapeDtypeStruct((1, ff), jnp.float32),
            *units_like(TALL, TALL_CUTS),
        ],
        scratch_shapes=[
            pltpu.VMEM((rows, D), jnp.float32),
            pltpu.VMEM((rows, FF_BLOCK), jnp.bfloat16),
        ]
        + fold_scratch(TALL, TALL_CUTS, count),
        compiler_params=pltpu.CompilerParams(
            vmem_limit_bytes=56 << 20, collective_id=5, has_side_effects=True
        ),
        name="narrow_back",
    )(d_mlp, x, slope, w_down, w_up, grad)


def per_device(
    tokens,
    segments,
    random_blocks,
    out_grad,
    w_query,
    w_key,
    w_value,
    w_out,
    w_up,
    w_down,
    vectors,
    up_bias,
):
    count = lax.axis_size("fsdp")
    place = lax.axis_index("fsdp")
    width = vectors.shape[1]
    small = jnp.zeros((16, 256), jnp.bfloat16)
    small = small.at[:8, :width].set(vectors).at[8:12, :width].set(up_bias.reshape(4, -1))
    full_query, full_key, full_value, small = gather_first((w_query, w_key, w_value, small))
    full_query, full_key, full_value = (
        w.reshape(D, D) for w in (full_query, full_key, full_value)
    )
    full_vectors = jnp.moveaxis(small[:, :8, :width], 0, 1).reshape(8, -1)
    full_bias = small[:, 8:12, :width].reshape(-1).astype(jnp.float32)

    vec_float = full_vectors.astype(jnp.float32)
    inputs = tokens.astype(jnp.float32)
    q_low = (jnp.dot(tokens, full_query, preferred_element_type=jnp.float32) + vec_float[0]).astype(
        jnp.bfloat16
    )
    k_low = jnp.dot(tokens, full_key, preferred_element_type=jnp.float32).astype(jnp.bfloat16)
    v_low = (jnp.dot(tokens, full_value, preferred_element_type=jnp.float32) + vec_float[1]).astype(
        jnp.bfloat16
    )
    q_feat, k_feat = mask_features(segments, random_blocks[0])
    mixed_low, aux, full_out, full_up, full_down = attention_forward(
        q_low, k_low, v_low, q_feat, k_feat, (w_out, w_up, w_down)
    )
    full_out, full_up = (w.reshape(-1, w.shape[-1]) for w in (full_out, full_up))
    attn_out = jnp.dot(mixed_low, full_out, preferred_element_type=jnp.float32) + vec_float[2]
    first_sum = inputs + attn_out
    normed_one, pull_one = jax.vjp(normalize, first_sum, vec_float[3], vec_float[4])
    normed_low = normed_one.astype(jnp.bfloat16)

    activated_low, slope, full_down = widen(normed_low, full_up, full_bias, full_down)
    full_down = full_down.reshape(-1, D)
    mlp_out = jnp.dot(activated_low, full_down, preferred_element_type=jnp.float32) + vec_float[5]
    second_sum = normed_one + mlp_out
    layer_out, pull_two = jax.vjp(normalize, second_sum, vec_float[6], vec_float[7])
    valid = (segments >= 0).astype(jnp.float32)[:, None]
    squares = jnp.stack(
        [
            jnp.sum(valid * first_sum * first_sum),
            jnp.sum(valid * attn_out * attn_out),
            jnp.sum(valid * mlp_out * mlp_out),
            jnp.sum(valid),
        ]
    )
    d_second, d_gain_two, d_shift_two = pull_two(out_grad.astype(jnp.float32))
    d_mlp = d_second.astype(jnp.bfloat16)

    grad_down = dot_tn(activated_low, d_mlp).astype(jnp.bfloat16).reshape(count, -1, D)
    d_wide, grad_up, bias_sums, *down_units = narrow_back(
        d_mlp, normed_low, slope, full_down, full_up, grad_down
    )
    d_normed = d_second + d_wide
    d_first, d_gain_one, d_shift_one = pull_one(d_normed)
    d_attn = d_first.astype(jnp.bfloat16)
    d_mixed = dot_nt(d_attn, full_out).astype(jnp.bfloat16)
    rest = [
        g.astype(jnp.bfloat16).reshape(count, -1, g.shape[1])
        for g in (dot_tn(mixed_low, d_attn), grad_up)
    ]
    dq_low, dk_low, dv_low, *units, grad_down = attention_backward(
        q_low, k_low, v_low, d_mixed, mixed_low, aux, k_feat, rest, down_units, w_down.shape
    )
    first = [
        dot_tn(tokens, d).astype(jnp.bfloat16).reshape(count, -1, D)
        for d in (dq_low, dk_low, dv_low)
    ]
    tokens_grad = (
        d_first + dot_nt(dq_low, full_query) + dot_nt(dk_low, full_key) + dot_nt(dv_low, full_value)
    )
    grad_vectors = jnp.stack(
        [
            col_sums(dq_low),
            col_sums(dv_low),
            col_sums(d_attn),
            d_gain_one,
            d_shift_one,
            col_sums(d_mlp),
            d_gain_two,
            d_shift_two,
            jnp.zeros((D,), jnp.float32).at[:4].set(squares),
        ]
    )
    small = jnp.concatenate(
        [grad_vectors, bias_sums.reshape(-1, D), jnp.zeros((3, D), jnp.float32)], 0
    )
    *grads, sums = reduce_last(first, units, [w_out.shape, w_up.shape], small)
    grads = [g.astype(jnp.float32) for g in (*grads, grad_down)]
    rms_values = jnp.sqrt(sums[8, :3] / (sums[8, 3] * D))
    bias_sums = sums[9:13].reshape(count, -1)
    return (
        layer_out.astype(jnp.bfloat16),
        tokens_grad.astype(jnp.bfloat16),
        *grads,
        lax.dynamic_slice_in_dim(sums[:8], place * width, width, 1),
        lax.dynamic_index_in_dim(bias_sums, place, 0, False),
        rms_values,
    )


def solution(mesh):
    in_specs = (
        P(("rep", "fsdp"), None),
        P(("rep", "fsdp")),
        P(("rep", "fsdp"), None, None),
        P(("rep", "fsdp"), None),
        P("fsdp", None),
        P("fsdp", None),
        P("fsdp", None),
        P("fsdp", None),
        P("fsdp", None),
        P("fsdp", None),
        P(None, "fsdp"),
        P("fsdp"),
    )
    out_specs = (
        P(("rep", "fsdp"), None),
        P(("rep", "fsdp"), None),
        P("fsdp", None),
        P("fsdp", None),
        P("fsdp", None),
        P("fsdp", None),
        P("fsdp", None),
        P("fsdp", None),
        P(None, "fsdp"),
        P("fsdp"),
        P(),
    )
    return jax.shard_map(
        per_device, mesh=mesh, in_specs=in_specs, out_specs=out_specs, check_vma=False
    )
```

```python
import functools

import jax
import jax.numpy as jnp
from jax import lax
from jax.experimental import pallas as pl
from jax.experimental.pallas import tpu as pltpu
from jax.sharding import PartitionSpec as P

D = 768
H = 12
DH = 64
BLK = 64
SEQ_LEN = 1024
NB = 16


masked_score = -1e30
layer_eps = 1e-05


def normalize(values, gain, shift):
    centered = values - jnp.mean(values, axis=-1, keepdims=True)
    variance = jnp.mean(centered * centered, axis=-1, keepdims=True)
    return centered * lax.rsqrt(variance + layer_eps) * gain + shift


def gelu_exact(values):
    return jax.nn.gelu(values, approximate=False)


def dot_tn(left, right):
    return lax.dot_general(
        left, right, (((0,), (0,)), ((), ())), preferred_element_type=jnp.float32
    )


def dot_nt(left, right):
    return lax.dot_general(
        left, right, (((1,), (1,)), ((), ())), preferred_element_type=jnp.float32
    )


def col_sums(values):
    return jnp.sum(values.astype(jnp.float32), axis=0)


LOG2E=1.4426950408889634
BIG=1e30

def dot_nn(a,b): return lax.dot_general(a,b,(((1,),(0,)),((),())),preferred_element_type=jnp.float32)

def mask_features(seg_row, random_row):
    blocks = jnp.arange(NB, dtype=jnp.int32)
    near = jnp.abs(blocks[:, None] - blocks[None, :]) <= 1
    first = (blocks[:, None] < 2) | (blocks[None, :] < 2)
    picked = jnp.any(random_row[:, :, None] == blocks[None, None, :], axis=1)
    seen = first | near | picked
    q_block = jnp.where(seen, 0.0, -BIG)
    q_block = jnp.repeat(q_block, BLK, axis=0)
    k_block = jnp.repeat(jnp.eye(NB, dtype=jnp.float32), BLK, axis=0)
    numbers = jnp.arange(-1, 2, dtype=jnp.int32)
    same = seg_row[:, None] == numbers[None, :]
    q_seg = jnp.where(same, 0.0, -BIG)
    k_seg = same.astype(jnp.float32)
    rest = SEQ_LEN, 128 - NB - 3
    ones = jnp.ones((SEQ_LEN, 3), jnp.float32)
    q_feat = jnp.concatenate([q_block, q_seg, jnp.zeros(rest, jnp.float32)], axis=1)
    k_feat = jnp.concatenate([k_block, k_seg, ones, jnp.zeros((SEQ_LEN, 128 - NB - 6), jnp.float32)], axis=1)
    return q_feat.astype(jnp.bfloat16), k_feat.astype(jnp.bfloat16)

MESH = pl.DeviceIdType.MESH


class Where:
    def __init__(self, extra=()):
        rep, place, count = lax.axis_index("rep"), lax.axis_index("fsdp"), lax.axis_size("fsdp")
        self.place, self.extra = place, tuple(extra)
        self.bits, self.flips = {}, {}
        for bit in (0, 1, 2) + self.extra:
            value = lax.rem(lax.div(rep, 1 << bit), 2)
            self.bits[bit] = value
            self.flips[bit] = rep + (1 - 2 * value) * (1 << bit)
        self.ahead = [lax.rem(place + step, count) for step in range(count)]
        self.behind = [lax.rem(place + count - step, count) for step in range(count)]

    def greet(self):
        barrier = pltpu.get_barrier_semaphore()
        for flip in self.flips.values():
            pl.semaphore_signal(barrier, inc=1, device_id={"rep": flip}, device_id_type=MESH)
        for there in self.ahead[1:]:
            pl.semaphore_signal(barrier, inc=1, device_id={"fsdp": there}, device_id_type=MESH)

    def meet(self):
        pl.semaphore_wait(
            pltpu.get_barrier_semaphore(), len(self.flips) + len(self.ahead) - 1
        )


def region(where, kind, rows, cols, order, level):
    core, first, second = (where.bits[bit] for bit in (0, *order))
    index = (second * 2 + first, second * 2, 0)[level]
    units = (1, 2, 4)[level]
    if kind == "square":
        unit = rows // 4
        return (
            pl.ds(pl.multiple_of(index * unit, unit), units * unit),
            pl.ds(pl.multiple_of(core * (cols // 2), cols // 2), cols // 2),
        )
    if kind == "wide":
        unit = cols // 8
        return (
            pl.ds(0, rows),
            pl.ds(pl.multiple_of((core * 4 + index) * unit, unit), units * unit),
        )
    unit = rows // 8
    return (
        pl.ds(pl.multiple_of((core * 4 + index) * unit, unit), units * unit),
        pl.ds(0, cols),
    )


SPAN = 3
AHEAD = 6


class Gather:
    def __init__(self, where, parts, shards, fulls, sems, low, highs):
        self.where = where
        self.parts, self.shards, self.fulls, self.low, self.highs = parts, shards, fulls, low, highs
        self.send, self.recv, self.local = sems
        self.count, self.place = lax.axis_size("fsdp"), where.place
        self.blocks = []
        for p in range(len(parts)):
            for step in range(1, self.count):
                _, array, row, col, _, _ = parts[p]
                turn = array + row // 48 + col // 256 + step
                self.blocks.append((p, step, (1, 2) if turn % 2 == 0 else (2, 1)))

    def copy(self, k, stage):
        p, step, order = self.blocks[k]
        kind, a, row, col, rows, cols = self.parts[p]
        full = self.fulls[a]
        if kind != "whole":
            r, c = region(self.where, kind, rows, cols, order, max(stage - 1, 0))
            if row:
                r = pl.ds(pl.multiple_of(r.start + row, 16), r.size)
            if col:
                c = pl.ds(pl.multiple_of(c.start + col, 128), c.size)
        if stage == 0:
            if kind == "whole":
                src, dst = self.shards[a], full.at[self.place]
            else:
                src, dst = self.shards[a].at[r, c], full.at[self.place, r, c]
            device = {"fsdp": self.where.ahead[step]}
        else:
            origin = self.where.behind[step]
            src = dst = full.at[origin, r, c]
            device = {"rep": self.where.flips[(order + (0,))[stage - 1]]}
        return pltpu.make_async_remote_copy(
            src_ref=src,
            dst_ref=dst,
            send_sem=self.send.at[k, stage],
            recv_sem=self.recv.at[k, stage],
            device_id=device,
            device_id_type=MESH,
        )

    def end(self, k):
        return self.highs[self.blocks[k][0]]

    def own(self, a):
        return pltpu.make_async_copy(
            self.shards[a], self.fulls[a].at[self.place], self.local.at[a]
        )

    def begin(self):
        for k in range(min(AHEAD, len(self.blocks)) if self.low == 0 else len(self.blocks)):
            self.copy(k, self.low).start()
        if self.low == 0:
            for a in range(len(self.shards)):
                self.own(a).start()

    def ticks(self):
        return len(self.blocks) + (max(self.highs) - self.low - 1) * SPAN

    def tick(self, t):
        for stage in range(self.low, max(self.highs)):
            k = t - (stage - self.low) * SPAN
            if 0 <= k < len(self.blocks) and stage < self.end(k):
                self.copy(k, stage).wait_recv()
                if stage == 0 and k + AHEAD < len(self.blocks):
                    self.copy(k + AHEAD, 0).start()
                if stage + 1 < self.end(k):
                    self.copy(k, stage + 1).start()

    def finish(self):
        for k in range(len(self.blocks)):
            for stage in range(self.low, self.end(k)):
                self.copy(k, stage).wait_send()
        if self.low == 0:
            for a in range(len(self.shards)):
                self.own(a).wait()


def gather_sems(parts, arrays, count):
    blocks = len(parts) * (count - 1)
    return [
        pltpu.SemaphoreType.DMA((blocks, 4)),
        pltpu.SemaphoreType.DMA((blocks, 4)),
        pltpu.SemaphoreType.DMA((arrays,)),
    ]


def whole_like(shards):
    return [jax.ShapeDtypeStruct((lax.axis_size("fsdp"), *s.shape), s.dtype) for s in shards]


def run_all(where, jobs, delays):
    where.greet()
    where.meet()
    for t in range(max(job.ticks() + delay for job, delay in zip(jobs, delays))):
        for job, delay in zip(jobs, delays):
            if t == delay:
                job.begin()
            if 0 <= t - delay < job.ticks():
                job.tick(t - delay)
    for job in jobs:
        job.finish()


FIRST = (
    *(("square", i, 0, 0, D // 4, D) for i in range(3)),
    ("whole", 3, 0, 0, 16, 256),
)
REST = (
    ("square", 0, 0, 0, D // 4, D),
    *(("wide", 1, 48 * i, 0, 48, 4 * D) for i in range(4)),
)
LATER = tuple(("tall", 2, 0, 256 * i, D, 256) for i in range(3))
DOWN = tuple(("tall", 0, *p[2:]) for p in LATER)


def gather_kernel(*refs):
    n = (len(refs) - 3) // 2
    where = Where()
    job = Gather(where, FIRST, refs[:n], refs[n : 2 * n], refs[2 * n :], 0, (4, 4, 4, 1))
    run_all(where, [job], (0,))


def gather_first(shards):
    count = lax.axis_size("fsdp")
    return pl.pallas_call(
        gather_kernel,
        in_specs=[pl.BlockSpec(memory_space=pl.ANY)] * len(shards),
        out_specs=[pl.BlockSpec(memory_space=pl.ANY)] * len(shards),
        out_shape=whole_like(shards),
        scratch_shapes=gather_sems(FIRST, len(shards), count),
        compiler_params=pltpu.CompilerParams(
            collective_id=0, has_side_effects=True, vmem_limit_bytes=60 << 20
        ),
        name="gather_first",
    )(*shards)


LAG = 3


def half_shape(kind, rows, cols):
    return (rows // 2, cols) if kind == "tall" else (rows, cols // 2)


def part_shape(kind, rows, cols, level):
    r, c = half_shape(kind, rows, cols)
    cut = (4, 2, 1)[level]
    return (r, c // cut) if kind == "wide" else (r // cut, c)


def part(kind, rows, cols, first, second, level):
    index = (second * 2 + first, second * 2, 0)[level]
    units = (1, 2, 4)[level]
    r, c = half_shape(kind, rows, cols)
    if kind == "wide":
        unit = c // 4
        return pl.ds(0, r), pl.ds(pl.multiple_of(index * unit, unit), units * unit)
    unit = r // 4
    return pl.ds(pl.multiple_of(index * unit, unit), units * unit), pl.ds(0, c)


def half(kind, rows, cols, core):
    r, c = half_shape(kind, rows, cols)
    if kind == "tall":
        return pl.ds(pl.multiple_of(core * r, r), r), pl.ds(0, c)
    return pl.ds(0, r), pl.ds(pl.multiple_of(core * c, c), c)


def add_into(target, where, values):
    rows, cols = where
    chunk = 16
    total, base = rows.size, rows.start

    @pl.loop(0, total // chunk)
    def _(i):
        at = pl.ds(pl.multiple_of(base + i * chunk, chunk), chunk)
        more = values[pl.ds(pl.multiple_of(i * chunk, chunk), chunk), :]
        kept = target[at, cols]
        target[at, cols] = (kept.astype(jnp.float32) + more.astype(jnp.float32)).astype(
            target.dtype
        )


class Reduce:
    def __init__(self, where, kinds, grads, results, scratch, extra, cuts):
        self.where = where
        self.kinds, self.grads, self.results, self.extra = kinds, grads, results, extra
        self.cuts = cuts
        n = len(kinds)
        self.acc, self.got0, self.got1, self.got2, self.got3 = (
            scratch[i * n : (i + 1) * n] for i in range(5)
        )
        self.outs, rest = scratch[5 * n : 6 * n], scratch[6 * n :]
        if extra:
            self.gotx, rest = rest[:n], rest[n:]
        self.load, self.send, self.recv, self.gsend, self.grecv, self.store = rest[:6]
        self.count, self.place = lax.axis_size("fsdp"), where.place
        self.blocks = [
            (a, step) for step in list(range(1, self.count)) + [0] for a in range(n)
        ]

    def order(self, a):
        return (1, 2) if a % 2 == 0 else (2, 1)

    def bits(self, a):
        order = self.order(a)
        return self.where.bits[order[0]], self.where.bits[order[1]]

    def shape(self, a):
        return self.cuts[a][3:]

    def source(self, a, step, core):
        g, row, col, rows, cols = self.cuts[a]
        r, c = half(self.kinds[a], rows, cols, core)
        if row:
            r = pl.ds(pl.multiple_of(r.start + row, 16), r.size)
        if col:
            c = pl.ds(pl.multiple_of(c.start + col, 128), c.size)
        return self.grads[g].at[self.where.ahead[step], r, c]

    def mine(self, k):
        a, step = self.blocks[k]
        return pltpu.make_async_copy(
            self.source(a, step, self.where.bits[0]), self.acc[a].at[step], self.load.at[k]
        )

    def copy(self, k, stage):
        a, step = self.blocks[k]
        kind, shape = self.kinds[a], self.shape(a)
        first, second = self.bits(a)
        order = self.order(a)
        if stage == 0:
            src, dst = self.source(a, step, 1 - self.where.bits[0]), self.got0[a].at[step]
            device = {"rep": self.where.flips[0]}
        elif stage == 1:
            r, c = part(kind, *shape, first, 1 - second, 1)
            src, dst = self.acc[a].at[step, r, c], self.got1[a].at[step]
            device = {"rep": self.where.flips[order[1]]}
        elif stage == 2:
            r, c = part(kind, *shape, 1 - first, second, 0)
            src, dst = self.acc[a].at[step, r, c], self.got2[a].at[step]
            device = {"rep": self.where.flips[order[0]]}
        else:
            r, c = part(kind, *shape, first, second, 0)
            src, dst = self.acc[a].at[step, r, c], self.got3[a].at[step - 1]
            device = {"fsdp": self.where.ahead[step]}
        return pltpu.make_async_remote_copy(
            src_ref=src,
            dst_ref=dst,
            send_sem=self.send.at[k, stage],
            recv_sem=self.recv.at[k, stage],
            device_id=device,
            device_id_type=MESH,
        )

    def whole(self, a, level):
        kind, (rows, cols) = self.kinds[a], self.shape(a)
        return region(self.where, kind, rows, cols, self.order(a), level)

    def back(self, a, level):
        r, c = self.whole(a, level)
        ref = self.outs[a].at[r, c]
        bit = (self.order(a) + (0,))[level]
        return pltpu.make_async_remote_copy(
            src_ref=ref,
            dst_ref=ref,
            send_sem=self.gsend.at[a, level],
            recv_sem=self.grecv.at[a, level],
            device_id={"rep": self.where.flips[bit]},
            device_id_type=MESH,
        )

    def more(self, a, i):
        r, c = self.whole(a, 0)
        return pltpu.make_async_remote_copy(
            src_ref=self.outs[a].at[r, c],
            dst_ref=self.gotx[a].at[i],
            send_sem=self.gsend.at[a, 3 + i],
            recv_sem=self.grecv.at[a, 3 + i],
            device_id={"rep": self.where.flips[self.extra[i]]},
            device_id_type=MESH,
        )

    def begin(self):
        for k in range(len(self.blocks)):
            self.copy(k, 0).start()
            self.mine(k).start()

    def absorb(self, k, stage):
        a, step = self.blocks[k]
        kind, shape = self.kinds[a], self.shape(a)
        first, second = self.bits(a)
        got = (self.got0, self.got1, self.got2)[stage][a].at[step]
        where = part(kind, *shape, first, second, 2 - stage)
        if stage == 0:
            self.mine(k).wait()
        self.copy(k, stage).wait_recv()
        add_into(self.acc[a].at[step], where, got)
        if stage < 2 or step:
            self.copy(k, stage + 1).start()

    def total(self, a):
        kind, shape = self.kinds[a], self.shape(a)
        first, second = self.bits(a)
        for step in range(1, self.count):
            self.copy(self.blocks.index((a, step)), 3).wait_recv()
        rows, cols = part(kind, *shape, first, second, 0)
        to_rows, to_cols = self.whole(a, 0)
        chunk = 16

        @pl.loop(0, rows.size // chunk)
        def _(i):
            at = pl.ds(pl.multiple_of(rows.start + i * chunk, chunk), chunk)
            total = self.acc[a][0, at, cols].astype(jnp.float32)
            near = pl.ds(pl.multiple_of(i * chunk, chunk), chunk)
            for step in range(self.count - 1):
                total = total + self.got3[a][step, near, :].astype(jnp.float32)
            to = pl.ds(pl.multiple_of(to_rows.start + i * chunk, chunk), chunk)
            self.outs[a][to, to_cols] = total.astype(jnp.bfloat16)

        for i in range(len(self.extra)):
            copy = self.more(a, i)
            copy.start()
            copy.wait()
            add_into(self.outs[a], self.whole(a, 0), self.gotx[a].at[i])
        self.back(a, 0).start()

    def put(self, a):
        g, row, col, rows, cols = self.cuts[a]
        to = self.results[g].at[pl.ds(row, rows), pl.ds(col, cols)]
        return pltpu.make_async_copy(self.outs[a], to, self.store.at[a])

    def ticks(self):
        return len(self.blocks) + 6 * LAG

    def tick(self, t):
        blocks = len(self.blocks)
        for stage in range(3):
            k = t - stage * LAG
            if 0 <= k < blocks:
                self.absorb(k, stage)
        for a in range(len(self.kinds)):
            late = t - self.blocks.index((a, 0)) - 3 * LAG
            if late == 0:
                self.total(a)
            elif late in (LAG, 2 * LAG, 3 * LAG):
                level = late // LAG
                self.back(a, level - 1).wait_recv()
                if level < 3:
                    self.back(a, level).start()
                else:
                    self.put(a).start()

    def finish(self):
        for k, (a, step) in enumerate(self.blocks):
            for stage in range(4 if step else 3):
                self.copy(k, stage).wait_send()
        for a in range(len(self.kinds)):
            for level in range(3):
                self.back(a, level).wait_send()
            self.put(a).wait()


class Fold(Reduce):
    def __init__(self, where, kinds, grads, units, scratch, cuts):
        self.where = where
        self.kinds, self.grads, self.units, self.cuts = kinds, grads, units, cuts
        n = len(kinds)
        self.acc, self.got0, self.got1, self.got2, self.got3, self.kept = (
            scratch[i * n : (i + 1) * n] for i in range(6)
        )
        self.load, self.send, self.recv, self.store = scratch[6 * n :]
        self.count, self.place = lax.axis_size("fsdp"), where.place
        self.blocks = [(a, step) for step in [*range(1, self.count), 0] for a in range(n)]

    def keep(self, a):
        return pltpu.make_async_copy(self.kept[a], self.units[a], self.store.at[a])

    def total(self, a):
        for step in range(1, self.count):
            self.copy(self.blocks.index((a, step)), 3).wait_recv()
        rows, cols = part(self.kinds[a], *self.shape(a), *self.bits(a), 0)
        chunk = 16

        @pl.loop(0, rows.size // chunk)
        def _(i):
            at = pl.ds(pl.multiple_of(rows.start + i * chunk, chunk), chunk)
            total = self.acc[a][0, at, cols].astype(jnp.float32)
            near = pl.ds(pl.multiple_of(i * chunk, chunk), chunk)
            for step in range(self.count - 1):
                total = total + self.got3[a][step, near, :].astype(jnp.float32)
            self.kept[a][near, :] = total.astype(jnp.bfloat16)

        self.keep(a).start()

    def ticks(self):
        return len(self.blocks) + 3 * LAG

    def tick(self, t):
        for stage in range(3):
            k = t - stage * LAG
            if 0 <= k < len(self.blocks):
                self.absorb(k, stage)
        for a in range(len(self.kinds)):
            if t == self.blocks.index((a, 0)) + 3 * LAG:
                self.total(a)

    def finish(self):
        for k, (a, step) in enumerate(self.blocks):
            for stage in range(4 if step else 3):
                self.copy(k, stage).wait_send()
        for a in range(len(self.kinds)):
            self.keep(a).wait()


class Spread(Reduce):
    def __init__(self, where, kinds, units, results, scratch, extra, cuts):
        self.where = where
        self.kinds, self.units, self.results = kinds, units, results
        self.extra, self.cuts = extra, cuts
        n = len(kinds)
        self.outs, rest = scratch[:n], scratch[n:]
        if extra:
            self.gotx, rest = rest[:n], rest[n:]
        self.load, self.gsend, self.grecv, self.store = rest

    def near(self, a):
        r, c = self.whole(a, 0)
        return pltpu.make_async_copy(self.units[a], self.outs[a].at[r, c], self.load.at[a])

    def begin(self):
        for a in range(len(self.kinds)):
            self.near(a).start()

    def ticks(self):
        return 4 * len(self.kinds)

    def tick(self, t):
        level, a = divmod(t, len(self.kinds))
        if level:
            self.back(a, level - 1).wait_recv()
            (self.back(a, level) if level < 3 else self.put(a)).start()
            return
        self.near(a).wait()
        for i in range(len(self.extra)):
            copy = self.more(a, i)
            copy.start()
            copy.wait()
            add_into(self.outs[a], self.whole(a, 0), self.gotx[a].at[i])
        self.back(a, 0).start()

    def finish(self):
        for a in range(len(self.kinds)):
            for level in range(3):
                self.back(a, level).wait_send()
            self.put(a).wait()


def units_like(kinds, cuts):
    return [jax.ShapeDtypeStruct(part_shape(k, *c[3:], 0), jnp.bfloat16) for k, c in zip(kinds, cuts)]


def fold_scratch(kinds, cuts, count):
    B = jnp.bfloat16
    sizes = [(k, *c[3:]) for k, c in zip(kinds, cuts)]
    blocks = len(kinds) * count
    dma = pltpu.SemaphoreType.DMA
    return (
        [pltpu.VMEM((count, *half_shape(*s)), B) for s in sizes] * 2
        + [pltpu.VMEM((count, *part_shape(*s, 1)), B) for s in sizes]
        + [pltpu.VMEM((count, *part_shape(*s, 0)), B) for s in sizes]
        + [pltpu.VMEM((count - 1, *part_shape(*s, 0)), B) for s in sizes]
        + [pltpu.VMEM(part_shape(*s, 0), B) for s in sizes]
        + [dma((blocks,)), dma((blocks, 4)), dma((blocks, 4)), dma((len(kinds),))]
    )


def spread_scratch(kinds, cuts, count, extra):
    B = jnp.bfloat16
    sizes = [(k, *c[3:]) for k, c in zip(kinds, cuts)]
    n = len(kinds)
    dma = pltpu.SemaphoreType.DMA
    made = [pltpu.VMEM(s[1:], B) for s in sizes]
    if extra:
        made += [pltpu.VMEM((len(extra), *part_shape(*s, 0)), B) for s in sizes]
    backs = 3 + len(extra)
    return made + [dma((n,)), dma((n, backs)), dma((n, backs)), dma((n,))]


class Sums:
    def __init__(self, where, source, result, held, got, send, recv, extra):
        self.where = where
        self.source, self.result, self.held, self.got = source, result, held, got
        self.send, self.recv = send, recv
        self.bits = (0, 1, 2) + tuple(extra)
        self.count, self.place = lax.axis_size("fsdp"), where.place

    def copy(self, i):
        level = min(i, len(self.bits))
        src = self.source if level == 0 else self.held.at[level - 1]
        if i < len(self.bits):
            device = {"rep": self.where.flips[self.bits[i]]}
        else:
            step = i - len(self.bits) + 1
            device = {"fsdp": self.where.ahead[step]}
        return pltpu.make_async_remote_copy(
            src_ref=src,
            dst_ref=self.got.at[i],
            send_sem=self.send.at[i],
            recv_sem=self.recv.at[i],
            device_id=device,
            device_id_type=MESH,
        )

    def begin(self):
        self.copy(0).start()

    def ticks(self):
        return len(self.bits) + 1

    def tick(self, t):
        bits = len(self.bits)
        if t < bits:
            self.copy(t).wait_recv()
            before = self.source[...] if t == 0 else self.held[t - 1]
            self.held[t] = before + self.got[t]
            for i in range(t + 1, t + 2 if t + 1 < bits else bits + self.count - 1):
                self.copy(i).start()
        elif t == bits:
            total = self.held[bits - 1]
            for i in range(bits, bits + self.count - 1):
                self.copy(i).wait_recv()
                total = total + self.got[i]
            self.result[...] = total

    def finish(self):
        for i in range(len(self.bits) + self.count - 1):
            self.copy(i).wait_send()


def reduce_scratch(kinds, shapes, count, extra):
    B = jnp.bfloat16
    sizes = [(k, *s) for k, s in zip(kinds, shapes)]
    made = [pltpu.VMEM((count, *half_shape(*s)), B) for s in sizes]
    made += [pltpu.VMEM((count, *half_shape(*s)), B) for s in sizes]
    made += [pltpu.VMEM((count, *part_shape(*s, 1)), B) for s in sizes]
    made += [pltpu.VMEM((count, *part_shape(*s, 0)), B) for s in sizes]
    made += [pltpu.VMEM((count - 1, *part_shape(*s, 0)), B) for s in sizes]
    made += [pltpu.VMEM(s, B) for s in shapes]
    if extra:
        made += [pltpu.VMEM((len(extra), *part_shape(*s, 0)), B) for s in sizes]
    n = len(kinds)
    dma = pltpu.SemaphoreType.DMA
    made += [dma((n * count,)), dma((n * count, 4)), dma((n * count, 4))]
    made += [dma((n, 3 + len(extra))), dma((n, 3 + len(extra))), dma((n,))]
    return made


def sums_scratch(shape, count, extra):
    bits = 3 + len(extra)
    dma = pltpu.SemaphoreType.DMA
    return [
        pltpu.VMEM((bits, *shape), jnp.float32),
        pltpu.VMEM((bits + count - 1, *shape), jnp.float32),
        dma((bits + count - 1,)),
        dma((bits + count - 1,)),
    ]


def extra_bits():
    found, bit = [], 3
    while (1 << bit) < lax.axis_size("rep"):
        found.append(bit)
        bit += 1
    return tuple(found)


REST_BACK = ("square", "wide", "wide")
REST_CUTS = ((0, 0, 0, D // 4, D), (1, 0, 0, D // 8, 4 * D), (1, D // 8, 0, D // 8, 4 * D))
TALL = ("tall", "tall")
TALL_CUTS = ((0, 0, 0, D, D // 2), (0, 0, D // 2, D, D // 2))
LAST = ("square", "square", "square")


def reduce_kernel(extra, spread_size, *refs):
    n, m, p = len(LAST), len(REST_BACK), 2
    grads, units, small = refs[:n], refs[n : n + m], refs[n + m]
    outs = refs[n + m + 1 : n + m + 1 + n + p]
    total, scratch = refs[n + m + 1 + n + p], refs[n + m + 2 + n + p :]
    cuts = [(i, 0, 0, *g.shape[1:]) for i, g in enumerate(grads)]
    where = Where(extra)
    run_all(
        where,
        [
            Reduce(where, LAST, grads, outs[:n], scratch[spread_size:-4], extra, cuts),
            Spread(where, REST_BACK, units, outs[n:], scratch[:spread_size], extra, REST_CUTS),
            Sums(where, small, total, *scratch[-4:], extra),
        ],
        (0, 0, 0),
    )


def reduce_last(grads, units, shards, small):
    count = lax.axis_size("fsdp")
    extra = extra_bits()
    shapes = [g.shape[1:] for g in grads]
    vmem = pl.BlockSpec(memory_space=pltpu.VMEM)
    hbm = pl.BlockSpec(memory_space=pl.ANY)
    spread = spread_scratch(REST_BACK, REST_CUTS, count, extra)
    return pl.pallas_call(
        functools.partial(reduce_kernel, extra, len(spread)),
        in_specs=[hbm] * (len(grads) + len(units)) + [vmem],
        out_specs=[hbm] * (len(grads) + len(shards)) + [vmem],
        out_shape=[jax.ShapeDtypeStruct(s, jnp.bfloat16) for s in shapes + shards]
        + [jax.ShapeDtypeStruct(small.shape, jnp.float32)],
        scratch_shapes=spread
        + reduce_scratch(LAST, shapes, count, extra)
        + sums_scratch(small.shape, count, extra),
        compiler_params=pltpu.CompilerParams(
            collective_id=3, has_side_effects=True, vmem_limit_bytes=48 << 20
        ),
        name="reduce_last",
    )(*grads, *units, small)


TQ = 256
POINTS = 24


def host(where, jobs, paces, tile):
    for point in range(tile, POINTS, 4):
        due = [
            (job, i)
            for job, (first, pace) in zip(jobs, paces)
            for i in range(job.ticks())
            if int(first + pace * i) == point
        ]
        if due or point == 0:

            @pl.when(pl.program_id(0) == point // 4)
            def _(due=due, point=point):
                if point == 0:
                    where.greet()
                    where.meet()
                    for job in jobs:
                        job.begin()
                for job, i in due:
                    job.tick(i)


def close(jobs, paces):
    left = [
        (i, j)
        for j, (job, (first, pace)) in enumerate(zip(jobs, paces))
        for i in range(job.ticks())
        if int(first + pace * i) >= POINTS
    ]

    @pl.when(pl.program_id(0) == POINTS // 4 - 1)
    def _():
        for i, j in sorted(left):
            jobs[j].tick(i)
        for job in jobs:
            job.finish()


FORWARD_PACES = ((5, 0.85),)
WIDEN_PACES = ((8, 1.4),)
NARROW_PACES = ((4, 1.8),)
BACKWARD_PACES = ((4, 1.3), (2, 2.5))


def fwd_kernel(q_ref,k_ref,v_ref,qf_ref,kf_ref,s0,s1,s2,o_ref,aux_ref,f0,f1,f2,qc,kc,vm,*sems):
    highs = (4,) * len(REST) + (1,) * len(LATER)
    where = Where()
    jobs = [Gather(where, REST + LATER, (s0, s1, s2), (f0, f1, f2), sems, 0, highs)]
    lane = lax.broadcasted_iota(jnp.int32,(SEQ_LEN,128),1)
    kc[:,:128]=k_ref[...]
    kc[:,128:]=kf_ref[...]
    q=q_ref[...]*jnp.bfloat16(0.125)
    v=v_ref[...]
    zero=jnp.zeros_like(q)
    for h in range(2):
        sel = (lane<64) if h==0 else (lane>=64)
        qc[h,:,:128]=jnp.where(sel,q,zero)
        qc[h,:,128:]=qf_ref[...]
        vm[h]=jnp.where(sel,v,zero)
    for t in range(SEQ_LEN//TQ):
        host(where, jobs, FORWARD_PACES, t)
        rows=pl.ds(t*TQ,TQ)
        total=None
        for h in range(2):
            s=dot_nt(qc[h,rows,:],kc[...])
            m=jnp.max(s,axis=1,keepdims=True)
            p=jnp.exp2((s-m)*LOG2E)
            l=jnp.sum(p,axis=1,keepdims=True)
            o=dot_nn(p.astype(jnp.bfloat16),vm[h])*(1.0/l)
            total=o if total is None else total+o
            lse=-(m+jnp.log(l))
            hi=lse.astype(jnp.bfloat16).astype(jnp.float32)
            r=lse-hi
            mid=r.astype(jnp.bfloat16).astype(jnp.float32)
            lo=r-mid
            ln=lax.broadcasted_iota(jnp.int32,(TQ,128),1)
            a=jnp.where(ln==19,hi,jnp.where(ln==20,mid,jnp.where(ln==21,lo,qf_ref[rows,:].astype(jnp.float32))))
            aux_ref[h,rows,:]=a.astype(jnp.bfloat16)
        o_ref[rows,:]=total.astype(jnp.bfloat16)
    close(jobs, FORWARD_PACES)

def attention_forward(q,k,v,qf,kf,shards):
    count=lax.axis_size("fsdp")
    pair=pl.BlockSpec((SEQ_LEN,128),lambda i:(0,i))
    whole=pl.BlockSpec((SEQ_LEN,128),lambda i:(0,0))
    hbm=pl.BlockSpec(memory_space=pl.ANY)
    B=jnp.bfloat16
    return pl.pallas_call(fwd_kernel,grid=(H//2,),
        in_specs=[pair,pair,pair,whole,whole]+[pl.BlockSpec(memory_space=pltpu.VMEM)]*3,
        out_specs=[pair,pl.BlockSpec((2,SEQ_LEN,128),lambda i:(i,0,0)),hbm,hbm,hbm],
        out_shape=[jax.ShapeDtypeStruct((SEQ_LEN,D),B),jax.ShapeDtypeStruct((H,SEQ_LEN,128),B)]+whole_like(shards),
        scratch_shapes=[pltpu.VMEM((2,SEQ_LEN,256),B),pltpu.VMEM((SEQ_LEN,256),B),pltpu.VMEM((2,SEQ_LEN,128),B)]+gather_sems(REST+LATER,3,count),
        compiler_params=pltpu.CompilerParams(vmem_limit_bytes=48<<20,collective_id=1,has_side_effects=True),
        cost_estimate=pl.CostEstimate(flops=30_000_000_000,bytes_accessed=10_000_000,transcendentals=12_582_912),
        name="attention_forward")(q,k,v,qf,kf,*shards)

TK=256
def bwd_kernel(extra,q_ref,k_ref,v_ref,do_ref,o_ref,aux_ref,kf_ref,g0,g1,v0,v1,dq_ref,dk_ref,dv_ref,u0,u1,u2,r0,qc,dc,kc,vc,km,dqa,*scratch):
    where = Where(extra)
    jobs = [
        Fold(where, REST_BACK, (g0, g1), (u0, u1, u2), scratch[:22], REST_CUTS),
        Spread(where, TALL, (v0, v1), (r0,), scratch[22:], extra, TALL_CUTS),
    ]
    lane = lax.broadcasted_iota(jnp.int32,(SEQ_LEN,128),1)
    kc[:,:128]=k_ref[...]
    kc[:,128:]=kf_ref[...]
    vc[:,:128]=v_ref[...]
    vc[:,128:]=kf_ref[...]
    q=q_ref[...]*jnp.bfloat16(0.125)
    k=k_ref[...]*jnp.bfloat16(0.125)
    do=do_ref[...]
    prod=do.astype(jnp.float32)*o_ref[...].astype(jnp.float32)
    zero=jnp.zeros_like(q)
    for h in range(2):
        sel = (lane<64) if h==0 else (lane>=64)
        qc[h,:,:128]=jnp.where(sel,q,zero)
        qc[h,:,128:]=aux_ref[h]
        km[h]=jnp.where(sel,k,zero)
        dc[h,:,:128]=jnp.where(sel,do,zero)
        delta=-jnp.sum(jnp.where(sel,prod,0.0),axis=1,keepdims=True)
        hi=delta.astype(jnp.bfloat16).astype(jnp.float32)
        lo=delta-hi
        dc[h,:,128:]=jnp.where(lane==19,hi,jnp.where(lane==20,lo,0.0)).astype(jnp.bfloat16)
    for t in range(SEQ_LEN//TK):
        host(where, jobs, BACKWARD_PACES, t)
        rows=pl.ds(t*TK,TK)
        dv=None;dk=None;dq=None
        for h in range(2):
            s=dot_nt(kc[rows,:],qc[h])
            p=jnp.exp2(s*LOG2E)
            dp=dot_nt(vc[rows,:],dc[h])
            ds=(p*dp).astype(jnp.bfloat16)
            pb=p.astype(jnp.bfloat16)
            dvh=dot_nn(pb,dc[h,:,:128])
            dkh=dot_nn(ds,qc[h,:,:128])
            dqh=dot_tn(ds,km[h,rows,:])
            dv=dvh if dv is None else dv+dvh
            dk=dkh if dk is None else dk+dkh
            dq=dqh if dq is None else dq+dqh
        dk_ref[rows,:]=dk.astype(jnp.bfloat16)
        dv_ref[rows,:]=dv.astype(jnp.bfloat16)
        if t==0: dqa[...]=dq
        else: dqa[...]+=dq
    dq_ref[...]=dqa[...].astype(jnp.bfloat16)
    close(jobs, BACKWARD_PACES)

def attention_backward(q,k,v,do,o,aux,kf,grads,units,shard):
    count=lax.axis_size("fsdp")
    extra=extra_bits()
    pair=pl.BlockSpec((SEQ_LEN,128),lambda i:(0,i))
    whole=pl.BlockSpec((SEQ_LEN,128),lambda i:(0,0))
    hbm=pl.BlockSpec(memory_space=pl.ANY)
    sd=jax.ShapeDtypeStruct((SEQ_LEN,D),jnp.bfloat16)
    B=jnp.bfloat16
    return pl.pallas_call(functools.partial(bwd_kernel,extra),grid=(H//2,),
        in_specs=[pair]*5+[pl.BlockSpec((2,SEQ_LEN,128),lambda i:(i,0,0)),whole]+[hbm]*4,
        out_specs=[pair]*3+[hbm]*4,
        out_shape=[sd]*3+units_like(REST_BACK,REST_CUTS)+[jax.ShapeDtypeStruct(shard,B)],
        scratch_shapes=[pltpu.VMEM((2,SEQ_LEN,256),B),pltpu.VMEM((2,SEQ_LEN,256),B),pltpu.VMEM((SEQ_LEN,256),B),pltpu.VMEM((SEQ_LEN,256),B),pltpu.VMEM((2,SEQ_LEN,128),B),pltpu.VMEM((SEQ_LEN,128),jnp.float32)]
            +fold_scratch(REST_BACK,REST_CUTS,count)+spread_scratch(TALL,TALL_CUTS,count,extra),
        compiler_params=pltpu.CompilerParams(vmem_limit_bytes=56<<20,collective_id=2,has_side_effects=True),
        cost_estimate=pl.CostEstimate(flops=42_000_000_000,bytes_accessed=15_000_000,transcendentals=12_582_912),
        name="attention_backward")(q,k,v,do,o,aux,kf,*grads,*units)


FF_BLOCK = 512


def normal_cdf(u, bell):
    t = 1.0 / (1.0 + 0.3535533905932738 * jnp.abs(u))
    fit = 0.17087277
    for c in (
        -0.82215223,
        1.48851587,
        -1.13520398,
        0.27886807,
        -0.18628806,
        0.09678418,
        0.37409196,
        1.00002368,
        -1.26551223,
    ):
        fit = fit * t + c
    tail = 0.5 * t * jnp.exp2(fit * LOG2E + bell)
    return jnp.where(u < 0.0, tail, 1.0 - tail)


def widen_kernel(x_ref, w_ref, b_ref, i0, act_ref, slope_ref, f0, *sems):
    where = Where()
    jobs = [Gather(where, DOWN, None, (f0,), sems, 1, (4,) * len(DOWN))]
    for t in range(4):
        host(where, jobs, WIDEN_PACES, t)
        rows = pl.ds(t * 256, 256)
        u = dot_nn(x_ref[rows, :], w_ref[...]) + b_ref[...]
        bell = u * u * (-0.5 * LOG2E)
        cdf = normal_cdf(u, bell)
        act_ref[rows, :] = (u * cdf).astype(jnp.bfloat16)
        slope_ref[rows, :] = (cdf + u * (0.3989422804014327 * jnp.exp2(bell))).astype(jnp.bfloat16)
    close(jobs, WIDEN_PACES)


def widen(x, w, bias, full_down):
    count = lax.axis_size("fsdp")
    rows, ff = x.shape[0], w.shape[1]
    block = pl.BlockSpec((rows, FF_BLOCK), lambda i: (0, i))
    out = jax.ShapeDtypeStruct((rows, ff), jnp.bfloat16)
    return pl.pallas_call(
        widen_kernel,
        grid=(ff // FF_BLOCK,),
        in_specs=[
            pl.BlockSpec((rows, D), lambda i: (0, 0)),
            pl.BlockSpec((D, FF_BLOCK), lambda i: (0, i)),
            pl.BlockSpec((1, FF_BLOCK), lambda i: (0, i)),
            pl.BlockSpec(memory_space=pl.ANY),
        ],
        input_output_aliases={3: 2},
        out_specs=[block, block, pl.BlockSpec(memory_space=pl.ANY)],
        out_shape=[out, out, jax.ShapeDtypeStruct(full_down.shape, full_down.dtype)],
        scratch_shapes=gather_sems(DOWN, 1, count),
        compiler_params=pltpu.CompilerParams(
            vmem_limit_bytes=40 << 20, collective_id=4, has_side_effects=True
        ),
        name="widen",
    )(x, w, bias[None], full_down)


def narrow_back_kernel(
    dm_ref, x_ref, slope_ref, wd_ref, wu_ref, g0, dx_ref, gu_ref, sum_ref, u0, u1, acc, du, *scratch
):
    where = Where()
    jobs = [Fold(where, TALL, (g0,), (u0, u1), scratch, TALL_CUTS)]
    sums = jnp.zeros((1, FF_BLOCK), jnp.float32)
    for t in range(4):
        host(where, jobs, NARROW_PACES, t)
        rows = pl.ds(t * 256, 256)
        d = dot_nt(dm_ref[rows, :], wd_ref[...]) * slope_ref[rows, :].astype(jnp.float32)
        low = d.astype(jnp.bfloat16)
        du[rows, :] = low
        sums = sums + jnp.sum(low.astype(jnp.float32), axis=0, keepdims=True)
        more = dot_nt(low, wu_ref[...])

        @pl.when(pl.program_id(0) == 0)
        def _():
            acc[rows, :] = more

        @pl.when(pl.program_id(0) > 0)
        def _():
            acc[rows, :] += more

    gu_ref[...] = dot_tn(x_ref[...], du[...]).astype(jnp.bfloat16)
    sum_ref[...] = sums

    @pl.when(pl.program_id(0) == pl.num_programs(0) - 1)
    def _():
        dx_ref[...] = acc[...]

    close(jobs, NARROW_PACES)


def narrow_back(d_mlp, x, slope, w_down, w_up, grad):
    count = lax.axis_size("fsdp")
    rows, ff = slope.shape
    whole = pl.BlockSpec((rows, D), lambda i: (0, 0))
    cols = pl.BlockSpec((D, FF_BLOCK), lambda i: (0, i))
    hbm = pl.BlockSpec(memory_space=pl.ANY)
    return pl.pallas_call(
        narrow_back_kernel,
        grid=(ff // FF_BLOCK,),
        in_specs=[
            whole,
            whole,
            pl.BlockSpec((rows, FF_BLOCK), lambda i: (0, i)),
            pl.BlockSpec((FF_BLOCK, D), lambda i: (i, 0)),
            cols,
            hbm,
        ],
        out_specs=[whole, cols, pl.BlockSpec((1, FF_BLOCK), lambda i: (0, i)), hbm, hbm],
        out_shape=[
            jax.ShapeDtypeStruct((rows, D), jnp.float32),
            jax.ShapeDtypeStruct((D, ff), jnp.bfloat16),
            jax.ShapeDtypeStruct((1, ff), jnp.float32),
            *units_like(TALL, TALL_CUTS),
        ],
        scratch_shapes=[
            pltpu.VMEM((rows, D), jnp.float32),
            pltpu.VMEM((rows, FF_BLOCK), jnp.bfloat16),
        ]
        + fold_scratch(TALL, TALL_CUTS, count),
        compiler_params=pltpu.CompilerParams(
            vmem_limit_bytes=56 << 20, collective_id=5, has_side_effects=True
        ),
        name="narrow_back",
    )(d_mlp, x, slope, w_down, w_up, grad)


def per_device(
    tokens,
    segments,
    random_blocks,
    out_grad,
    w_query,
    w_key,
    w_value,
    w_out,
    w_up,
    w_down,
    vectors,
    up_bias,
):
    count = lax.axis_size("fsdp")
    place = lax.axis_index("fsdp")
    width = vectors.shape[1]
    small = jnp.zeros((16, 256), jnp.bfloat16)
    small = small.at[:8, :width].set(vectors).at[8:12, :width].set(up_bias.reshape(4, -1))
    full_query, full_key, full_value, small = gather_first((w_query, w_key, w_value, small))
    full_query, full_key, full_value = (
        w.reshape(D, D) for w in (full_query, full_key, full_value)
    )
    full_vectors = jnp.moveaxis(small[:, :8, :width], 0, 1).reshape(8, -1)
    full_bias = small[:, 8:12, :width].reshape(-1).astype(jnp.float32)

    vec_float = full_vectors.astype(jnp.float32)
    inputs = tokens.astype(jnp.float32)
    q_low = (jnp.dot(tokens, full_query, preferred_element_type=jnp.float32) + vec_float[0]).astype(
        jnp.bfloat16
    )
    k_low = jnp.dot(tokens, full_key, preferred_element_type=jnp.float32).astype(jnp.bfloat16)
    v_low = (jnp.dot(tokens, full_value, preferred_element_type=jnp.float32) + vec_float[1]).astype(
        jnp.bfloat16
    )
    q_feat, k_feat = mask_features(segments, random_blocks[0])
    mixed_low, aux, full_out, full_up, full_down = attention_forward(
        q_low, k_low, v_low, q_feat, k_feat, (w_out, w_up, w_down)
    )
    full_out, full_up = (w.reshape(-1, w.shape[-1]) for w in (full_out, full_up))
    attn_out = jnp.dot(mixed_low, full_out, preferred_element_type=jnp.float32) + vec_float[2]
    first_sum = inputs + attn_out
    normed_one, pull_one = jax.vjp(normalize, first_sum, vec_float[3], vec_float[4])
    normed_low = normed_one.astype(jnp.bfloat16)

    activated_low, slope, full_down = widen(normed_low, full_up, full_bias, full_down)
    full_down = full_down.reshape(-1, D)
    mlp_out = jnp.dot(activated_low, full_down, preferred_element_type=jnp.float32) + vec_float[5]
    second_sum = normed_one + mlp_out
    layer_out, pull_two = jax.vjp(normalize, second_sum, vec_float[6], vec_float[7])
    valid = (segments >= 0).astype(jnp.float32)[:, None]
    squares = jnp.stack(
        [
            jnp.sum(valid * first_sum * first_sum),
            jnp.sum(valid * attn_out * attn_out),
            jnp.sum(valid * mlp_out * mlp_out),
            jnp.sum(valid),
        ]
    )
    d_second, d_gain_two, d_shift_two = pull_two(out_grad.astype(jnp.float32))
    d_mlp = d_second.astype(jnp.bfloat16)

    grad_down = dot_tn(activated_low, d_mlp).astype(jnp.bfloat16).reshape(count, -1, D)
    d_wide, grad_up, bias_sums, *down_units = narrow_back(
        d_mlp, normed_low, slope, full_down, full_up, grad_down
    )
    d_normed = d_second + d_wide
    d_first, d_gain_one, d_shift_one = pull_one(d_normed)
    d_attn = d_first.astype(jnp.bfloat16)
    d_mixed = dot_nt(d_attn, full_out).astype(jnp.bfloat16)
    rest = [
        g.astype(jnp.bfloat16).reshape(count, -1, g.shape[1])
        for g in (dot_tn(mixed_low, d_attn), grad_up)
    ]
    dq_low, dk_low, dv_low, *units, grad_down = attention_backward(
        q_low, k_low, v_low, d_mixed, mixed_low, aux, k_feat, rest, down_units, w_down.shape
    )
    first = [
        dot_tn(tokens, d).astype(jnp.bfloat16).reshape(count, -1, D)
        for d in (dq_low, dk_low, dv_low)
    ]
    tokens_grad = (
        d_first + dot_nt(dq_low, full_query) + dot_nt(dk_low, full_key) + dot_nt(dv_low, full_value)
    )
    grad_vectors = jnp.stack(
        [
            col_sums(dq_low),
            col_sums(dv_low),
            col_sums(d_attn),
            d_gain_one,
            d_shift_one,
            col_sums(d_mlp),
            d_gain_two,
            d_shift_two,
            jnp.zeros((D,), jnp.float32).at[:4].set(squares),
        ]
    )
    small = jnp.concatenate(
        [grad_vectors, bias_sums.reshape(-1, D), jnp.zeros((3, D), jnp.float32)], 0
    )
    *grads, sums = reduce_last(first, units, [w_out.shape, w_up.shape], small)
    grads = [g.astype(jnp.float32) for g in (*grads, grad_down)]
    rms_values = jnp.sqrt(sums[8, :3] / (sums[8, 3] * D))
    bias_sums = sums[9:13].reshape(count, -1)
    return (
        layer_out.astype(jnp.bfloat16),
        tokens_grad.astype(jnp.bfloat16),
        *grads,
        lax.dynamic_slice_in_dim(sums[:8], place * width, width, 1),
        lax.dynamic_index_in_dim(bias_sums, place, 0, False),
        rms_values,
    )


def solution(mesh):
    in_specs = (
        P(("rep", "fsdp"), None),
        P(("rep", "fsdp")),
        P(("rep", "fsdp"), None, None),
        P(("rep", "fsdp"), None),
        P("fsdp", None),
        P("fsdp", None),
        P("fsdp", None),
        P("fsdp", None),
        P("fsdp", None),
        P("fsdp", None),
        P(None, "fsdp"),
        P("fsdp"),
    )
    out_specs = (
        P(("rep", "fsdp"), None),
        P(("rep", "fsdp"), None),
        P("fsdp", None),
        P("fsdp", None),
        P("fsdp", None),
        P("fsdp", None),
        P("fsdp", None),
        P("fsdp", None),
        P(None, "fsdp"),
        P("fsdp"),
        P(),
    )
    return jax.shard_map(
        per_device, mesh=mesh, in_specs=in_specs, out_specs=out_specs, check_vma=False
    )
```
